512 devices in a mesh: blk: 32 (over y_lo, z), gy: 4 (over x), rep: 4 (over y_hi, core).
Axes of the slice: x: 4, y: 4 (y_hi: 2, y_lo: 2; y = y_hi * 2 + y_lo), z: 16, core: 2. Of those that a mesh axis runs over, the one named last changes fastest.
Arguments:
- grain_id: int32 [128, 32, 512], P('blk', 'gy', 'rep'), may hold values from 0 to 255
- init_masks: int32 [2, 128, 32, 512], P(None, 'blk', 'gy', 'rep'), may hold values from 0 to 1, as said below
- target_masks: int32 [2, 128, 32, 512], P(None, 'blk', 'gy', 'rep'), may hold values from 0 to 1, as said below
- emb_table: bfloat16 [256, 8], replicated, may hold values from -6 to 6
- w_in: float32 [64, 10], P('rep'), may hold values from -2 to 2
- b_in: float32 [64], P('rep'), may hold values from -3 to 3
- w_mid: float32 [64, 64], P('rep'), may hold values from -0.75 to 0.75
- b_mid: float32 [64], P('rep'), may hold values from -3 to 3
- w_out: float32 [6, 64], P(None, 'rep'), may hold values from -0.75 to 0.75
- b_out: float32 [6], replicated, may hold values from -4 to 4
Outputs:
- final_state: float32 [2, 128, 32, 512], P(None, 'blk', 'gy', 'rep')
- loss: float32 [], replicated
- grad_w_in: float32 [64, 10], P('rep')
- grad_b_in: float32 [64], P('rep')
- grad_w_mid: float32 [64, 64], P('rep')
- grad_b_mid: float32 [64], P('rep')
- grad_w_out: float32 [6, 64], P(None, 'rep')
- grad_b_out: float32 [6], replicated
- start_sensitivity: float32 [2, 128, 32, 512], P(None, 'blk', 'gy', 'rep')
The draws below stay inside these ranges and needn't reach their ends.
Inputs may be any that keep to these rules, and one draw needn't show every extreme that they name: `init_masks`: 0 or 1 in every cell. `target_masks`: 0 or 1 in every cell.
All inputs are finite; a program needn't handle non-finite values.
Results may differ from the reference program's by a relative error of at most 0.0054.
The reference program's roundings to bfloat16 on the way count: a program that leaves them out, or rounds other values in their place, can miss the bound.
Values may be sent and summed in bfloat16 or wider, within the bound.
A program may use at most 64 MiB of HBM per device.

```python
import jax
import jax.numpy as jnp
from jax import lax

UNITS = 64
EMBED = 8
TABLE = 256
STEPS = 4
CZ = 4
NX = 512
NY = 32
NZ = 128


def mask_pair(key):
    pore_mask = (jax.random.randint(jax.random.fold_in(key, 11), (NZ, NY, NX), 0, 3) == 0).astype(jnp.int32)
    vacancy_mask = (jax.random.randint(jax.random.fold_in(key, 12), (NZ, NY, NX), 0, 8) == 0).astype(jnp.int32)
    start_mask = jnp.stack([pore_mask, vacancy_mask])
    flip_mask = (jax.random.randint(jax.random.fold_in(key, 13), (2, NZ, NY, NX), 0, 6) == 0).astype(jnp.int32)
    finish_mask = jnp.abs(start_mask - flip_mask)
    return (start_mask, finish_mask)


def draw_init_masks(key, part):
    return mask_pair(key)[0]


def draw_target_masks(key, part):
    return mask_pair(key)[1]


def place_ends(drawn, rng, least, largest):
    longest = drawn.shape.index(max(drawn.shape))
    spots = []
    for shift in (0, 1):
        where = [jax.random.randint(jax.random.fold_in(rng, axis), (), 0, length) for axis, length in enumerate(drawn.shape)]
        where[longest] = (where[longest] + shift) % drawn.shape[longest]
        spots.append(tuple(where))
    return drawn.at[spots[0]].set(least).at[spots[1]].set(largest)


def level_of(rng, dims, shards, least, high):
    level = 1.0
    for position, parts in shards:
        heights = jax.random.uniform(jax.random.fold_in(jax.random.fold_in(rng, 6), position), (parts,), jnp.float32, least / len(shards), high / len(shards))
        level = level * jnp.repeat(jnp.exp(heights), dims[position] // parts).reshape((-1,) + (1,) * (len(dims) - 1 - position))
    return level


def gaussian(key, shape, deviation, reach, split=(), kind=jnp.bfloat16):
    values = deviation * jax.random.normal(key, shape, jnp.float32)
    if split:
        values = values * level_of(key, shape, split, -0.22, 0.18)
    return jnp.clip(values, -reach, reach).astype(kind)


def setup_inputs(seed: int = 0) -> dict:
    keys = jax.random.split(jax.random.key(seed), 11)
    grain_id = place_ends(jax.random.randint(keys[0], (NZ, NY, NX), 0, TABLE), jax.random.fold_in(keys[0], 1), 0, TABLE - 1).astype(jnp.int32)
    init_masks = draw_init_masks(jax.random.fold_in(keys[10], 71), 0)
    target_masks = draw_target_masks(jax.random.fold_in(keys[10], 71), 0)
    emb_table = gaussian(keys[3], (TABLE, EMBED), 1.0, 6.0)
    w_in = gaussian(keys[4], (UNITS, EMBED + 2), (EMBED + 2) ** -0.5, 2.0, ((0, 4),), jnp.float32)
    b_in = gaussian(keys[5], (UNITS,), 0.5, 3.0, ((0, 4),), jnp.float32)
    w_mid = gaussian(keys[6], (UNITS, UNITS), UNITS ** -0.5, 0.75, ((0, 4),), jnp.float32)
    b_mid = gaussian(keys[7], (UNITS,), 0.5, 3.0, ((0, 4),), jnp.float32)
    w_out = gaussian(keys[8], (6, UNITS), UNITS ** -0.5, 0.75, ((1, 4),), jnp.float32)
    b_out = gaussian(keys[9], (6,), 1.0, 4.0, (), jnp.float32)
    return {"grain_id": grain_id, "init_masks": init_masks, "target_masks": target_masks, "emb_table": emb_table, "w_in": w_in, "b_in": b_in, "w_mid": w_mid, "b_mid": b_mid, "w_out": w_out, "b_out": b_out}


RATE_MAX = 0.15


def beside(padded, axis_pos, offset):
    index_list = [slice(None), slice(1, -1), slice(1, -1), slice(1, -1)]
    index_list[axis_pos] = slice(1 + offset, padded.shape[axis_pos] - 1 + offset)
    return padded[tuple(index_list)]


def interior(padded):
    return padded[:, 1:-1, 1:-1, 1:-1]


def diffuse(field_pad, rate_pad):
    centre = interior(field_pad)
    summed = centre
    rate_centre = interior(rate_pad)
    for direction in range(3):
        axis_pos = 3 - direction
        rate_here = rate_centre[direction::3]
        for offset in (1, -1):
            rate_next = beside(rate_pad, axis_pos, offset)[direction::3]
            summed = summed + 0.5 * (rate_here + rate_next) * (beside(field_pad, axis_pos, offset) - centre)
    return summed


def rate_cotangent(state_pad, adjoint_pad):
    centre_state = interior(state_pad)
    centre_adjoint = interior(adjoint_pad)
    pieces_list = []
    for direction in range(3):
        axis_pos = 3 - direction
        summed = jnp.zeros_like(centre_state)
        for offset in (1, -1):
            summed = summed + (beside(state_pad, axis_pos, offset) - centre_state) * (beside(adjoint_pad, axis_pos, offset) - centre_adjoint)
        pieces_list.append(-0.5 * summed)
    stacked = jnp.stack(pieces_list, axis=1)
    return stacked.reshape((6,) + stacked.shape[2:])


def embed_lookup(emb_table, grain_flat):
    table_rows = emb_table.shape[0]
    one_hot = (grain_flat[None, :] == lax.broadcasted_iota(jnp.int32, (table_rows, 1), 0)).astype(jnp.bfloat16)
    looked = jnp.dot(emb_table.T, one_hot, preferred_element_type=jnp.float32)
    return looked.astype(jnp.bfloat16)


def forward_layers(params, features):
    w_in, b_in, w_mid, b_mid, w_out, b_out = params
    act_one = jnp.tanh(jnp.dot(w_in, features, preferred_element_type=jnp.float32) + b_in.astype(jnp.float32)[:, None])
    hid_one = act_one.astype(jnp.bfloat16)
    act_two = jnp.tanh(jnp.dot(w_mid, hid_one, preferred_element_type=jnp.float32) + b_mid.astype(jnp.float32)[:, None])
    hid_two = act_two.astype(jnp.bfloat16)
    logits = jnp.dot(w_out, hid_two, preferred_element_type=jnp.float32) + b_out.astype(jnp.float32)[:, None]
    return RATE_MAX * jax.nn.sigmoid(logits), act_one, hid_one, act_two, hid_two


def backward_layers(params, features, rate_grad, forward_values):
    w_in, b_in, w_mid, b_mid, w_out, b_out = params
    rate_values, act_one, hid_one, act_two, hid_two = forward_values
    out_grad = (rate_grad * rate_values * (1.0 - rate_values / RATE_MAX)).astype(jnp.bfloat16)
    two_grad = (jnp.dot(w_out.T, out_grad, preferred_element_type=jnp.float32) * (1.0 - act_two * act_two)).astype(jnp.bfloat16)
    one_grad = (jnp.dot(w_mid.T, two_grad, preferred_element_type=jnp.float32) * (1.0 - act_one * act_one)).astype(jnp.bfloat16)
    grad_terms = (
        jnp.dot(one_grad, features.T, preferred_element_type=jnp.float32),
        jnp.sum(one_grad, axis=1, dtype=jnp.float32),
        jnp.dot(two_grad, hid_one.T, preferred_element_type=jnp.float32),
        jnp.sum(two_grad, axis=1, dtype=jnp.float32),
        jnp.dot(out_grad, hid_two.T, preferred_element_type=jnp.float32),
        jnp.sum(out_grad, axis=1, dtype=jnp.float32),
    )
    state_grad = jnp.dot(w_in[:, -2:].T, one_grad, preferred_element_type=jnp.float32)
    return grad_terms, state_grad


def wrap_pad(field):
    return jnp.pad(field, ((0, 0), (1, 1), (1, 1), (1, 1)), mode="wrap")


def reference(grain_id, init_masks, target_masks, emb_table, w_in, b_in, w_mid, b_mid, w_out, b_out):
    params = (w_in.astype(jnp.bfloat16), b_in.astype(jnp.bfloat16), w_mid.astype(jnp.bfloat16),
              b_mid.astype(jnp.bfloat16), w_out.astype(jnp.bfloat16), b_out.astype(jnp.bfloat16))
    block_count = NZ // CZ
    block_cells = CZ * NY * NX
    embedding = lax.map(lambda grains: embed_lookup(emb_table, grains), grain_id.reshape(block_count, block_cells))

    def to_blocks(field):
        return field.reshape(field.shape[0], block_count, block_cells).transpose(1, 0, 2)

    def from_blocks(stacked):
        return stacked.transpose(1, 0, 2).reshape(stacked.shape[1], NZ, NY, NX)

    def forward_block(inputs_pair):
        features = jnp.concatenate([inputs_pair[0], inputs_pair[1].astype(jnp.bfloat16)], axis=0)
        return forward_layers(params, features)[0]

    def backward_block(inputs_triple):
        embed_part, state_part, grad_part = inputs_triple
        features = jnp.concatenate([embed_part, state_part.astype(jnp.bfloat16)], axis=0)
        forward_values = forward_layers(params, features)
        grad_terms, state_grad = backward_layers(params, features, grad_part, forward_values)
        return grad_terms, state_grad, forward_values[0]

    state_now = init_masks.astype(jnp.float32)
    history = []
    for step_index in range(STEPS):
        history.append(state_now)
        rate_values = from_blocks(lax.map(forward_block, (embedding, to_blocks(state_now))))
        state_now = diffuse(wrap_pad(state_now), wrap_pad(rate_values))
    misfit = state_now - target_masks.astype(jnp.float32)
    total_cells = NZ * NY * NX
    loss_total = jnp.sum(misfit * misfit) / (4.0 * total_cells)
    adjoint = misfit / (2.0 * total_cells)
    grad_sums = None
    for step_index in reversed(range(STEPS)):
        state_pad = wrap_pad(history[step_index])
        adjoint_pad = wrap_pad(adjoint)
        rate_grad = rate_cotangent(state_pad, adjoint_pad)
        block_terms, state_grad, rate_blocks = lax.map(
            backward_block, (embedding, to_blocks(history[step_index]), to_blocks(rate_grad)))
        step_terms = tuple(jnp.sum(block_term, axis=0) for block_term in block_terms)
        if grad_sums is None:
            grad_sums = step_terms
        else:
            grad_sums = tuple(earlier + later_term for earlier, later_term in zip(grad_sums, step_terms))
        adjoint = diffuse(adjoint_pad, wrap_pad(from_blocks(rate_blocks))) + from_blocks(state_grad)
    start_sensitivity = adjoint * (2.0 * total_cells)
    return (state_now, loss_total, grad_sums[0], grad_sums[1], grad_sums[2], grad_sums[3], grad_sums[4], grad_sums[5], start_sensitivity)
```

```python
import jax
import jax.numpy as jnp
from jax import lax
from jax.sharding import PartitionSpec as P

STEPS = 4


RATE_MAX = 0.15

AXES = (("rep", 3), ("gy", 2), ("blk", 1))


def ring_perms(axis):
    count = lax.axis_size(axis)
    forward = [(i, (i + 1) % count) for i in range(count)]
    backward = [((i + 1) % count, i) for i in range(count)]
    return forward, backward


def exchange_faces(fields):
    faces = []
    for direction, (axis, dim) in enumerate(AXES):
        block = fields[direction]
        forward, backward = ring_perms(axis)
        size = block.shape[dim]
        low = lax.ppermute(lax.slice_in_dim(block, size - 1, size, axis=dim), axis, forward)
        high = lax.ppermute(lax.slice_in_dim(block, 0, 1, axis=dim), axis, backward)
        faces.append((low, high))
    return faces


def shifted(block, low, high, dim, offset):
    size = block.shape[dim]
    if offset == 1:
        return jnp.concatenate([lax.slice_in_dim(block, 1, size, axis=dim), high], axis=dim)
    return jnp.concatenate([low, lax.slice_in_dim(block, 0, size - 1, axis=dim)], axis=dim)


def diffuse(field, field_faces, rates, rate_faces):
    summed = field
    for direction, (axis, dim) in enumerate(AXES):
        rate_here = rates[direction::3]
        for offset in (1, -1):
            low, high = field_faces[direction]
            rlow, rhigh = rate_faces[direction]
            rate_next = shifted(rate_here, rlow, rhigh, dim, offset)
            summed = summed + 0.5 * (rate_here + rate_next) * (
                shifted(field, low, high, dim, offset) - field
            )
    return summed


def rate_cotangent(state, state_faces, adjoint, adjoint_faces):
    pieces_list = []
    for direction, (axis, dim) in enumerate(AXES):
        summed = jnp.zeros_like(state)
        for offset in (1, -1):
            slow, shigh = state_faces[direction]
            alow, ahigh = adjoint_faces[direction]
            summed = summed + (shifted(state, slow, shigh, dim, offset) - state) * (
                shifted(adjoint, alow, ahigh, dim, offset) - adjoint
            )
        pieces_list.append(-0.5 * summed)
    stacked = jnp.stack(pieces_list, axis=1)
    return stacked.reshape((6,) + stacked.shape[2:])


def embed_lookup(emb_table, grain_flat):
    table_rows = emb_table.shape[0]
    one_hot = (grain_flat[None, :] == lax.broadcasted_iota(jnp.int32, (table_rows, 1), 0)).astype(
        jnp.bfloat16
    )
    looked = jnp.dot(emb_table.T, one_hot, preferred_element_type=jnp.float32)
    return looked.astype(jnp.bfloat16)


def forward_layers(params, features):
    w_in, b_in, w_mid, b_mid, w_out, b_out = params
    act_one = jnp.tanh(
        jnp.dot(w_in, features, preferred_element_type=jnp.float32)
        + b_in.astype(jnp.float32)[:, None]
    )
    hid_one = act_one.astype(jnp.bfloat16)
    act_two = jnp.tanh(
        jnp.dot(w_mid, hid_one, preferred_element_type=jnp.float32)
        + b_mid.astype(jnp.float32)[:, None]
    )
    hid_two = act_two.astype(jnp.bfloat16)
    logits = (
        jnp.dot(w_out, hid_two, preferred_element_type=jnp.float32)
        + b_out.astype(jnp.float32)[:, None]
    )
    return (RATE_MAX * jax.nn.sigmoid(logits), act_one, hid_one, act_two, hid_two)


def backward_layers(params, features, rate_grad, forward_values):
    w_in, b_in, w_mid, b_mid, w_out, b_out = params
    rate_values, act_one, hid_one, act_two, hid_two = forward_values
    out_grad = (rate_grad * rate_values * (1.0 - rate_values / RATE_MAX)).astype(jnp.bfloat16)
    two_grad = (
        jnp.dot(w_out.T, out_grad, preferred_element_type=jnp.float32) * (1.0 - act_two * act_two)
    ).astype(jnp.bfloat16)
    one_grad = (
        jnp.dot(w_mid.T, two_grad, preferred_element_type=jnp.float32) * (1.0 - act_one * act_one)
    ).astype(jnp.bfloat16)
    grad_terms = (
        jnp.dot(one_grad, features.T, preferred_element_type=jnp.float32),
        jnp.sum(one_grad, axis=1, dtype=jnp.float32),
        jnp.dot(two_grad, hid_one.T, preferred_element_type=jnp.float32),
        jnp.sum(two_grad, axis=1, dtype=jnp.float32),
        jnp.dot(out_grad, hid_two.T, preferred_element_type=jnp.float32),
        jnp.sum(out_grad, axis=1, dtype=jnp.float32),
    )
    state_grad = jnp.dot(w_in[:, -2:].T, one_grad, preferred_element_type=jnp.float32)
    return (grad_terms, state_grad)


def gather_params(w_in, b_in, w_mid, b_mid, w_out, b_out):
    n_in = w_in.shape[1]
    n_mid = w_mid.shape[1]
    packed = jnp.concatenate(
        [w_in, b_in[:, None], w_mid, b_mid[:, None], w_out.T], axis=1
    ).astype(jnp.bfloat16)
    full = lax.all_gather(packed, "rep", axis=0, tiled=True)
    col = 0
    w_in_b = full[:, col:col + n_in]
    col += n_in
    b_in_b = full[:, col]
    col += 1
    w_mid_b = full[:, col:col + n_mid]
    col += n_mid
    b_mid_b = full[:, col]
    col += 1
    w_out_b = full[:, col:].T
    return (w_in_b, b_in_b, w_mid_b, b_mid_b, w_out_b, b_out.astype(jnp.bfloat16))


def per_device(
    grain_id, init_masks, target_masks, emb_table, w_in, b_in, w_mid, b_mid, w_out, b_out
):
    params = gather_params(w_in, b_in, w_mid, b_mid, w_out, b_out)
    depth_cells, row_cells, col_cells = grain_id.shape
    cell_count = depth_cells * row_cells * col_cells
    block_shape = (depth_cells, row_cells, col_cells)
    embedding = embed_lookup(emb_table, grain_id.reshape(cell_count))
    state_now = init_masks.astype(jnp.float32)
    history = []
    for step_index in range(STEPS):
        features = jnp.concatenate(
            [embedding, state_now.reshape(2, cell_count).astype(jnp.bfloat16)], axis=0
        )
        rate_values = forward_layers(params, features)[0].reshape((6,) + block_shape)
        faces = exchange_faces(
            [jnp.concatenate([state_now, rate_values[d::3]], axis=0) for d in range(3)]
        )
        state_faces = [(low[:2], high[:2]) for low, high in faces]
        rate_faces = [(low[2:], high[2:]) for low, high in faces]
        history.append((state_now, state_faces, rate_values, rate_faces))
        state_now = diffuse(state_now, state_faces, rate_values, rate_faces)
    misfit = state_now - target_masks.astype(jnp.float32)
    total_cells = float(
        cell_count * lax.axis_size("blk") * lax.axis_size("gy") * lax.axis_size("rep")
    )
    loss_part = jnp.sum(misfit * misfit) / (4.0 * total_cells)
    adjoint = misfit / (2.0 * total_cells)
    grad_sums = None
    for step_index in reversed(range(STEPS)):
        state_t, state_faces, rate_values, rate_faces = history[step_index]
        adjoint_faces = exchange_faces([adjoint] * 3)
        rate_grad = rate_cotangent(state_t, state_faces, adjoint, adjoint_faces).reshape(
            6, cell_count
        )
        features = jnp.concatenate(
            [embedding, state_t.reshape(2, cell_count).astype(jnp.bfloat16)], axis=0
        )
        forward_values = forward_layers(params, features)
        step_terms, state_grad = backward_layers(params, features, rate_grad, forward_values)
        if grad_sums is None:
            grad_sums = step_terms
        else:
            grad_sums = tuple(
                (earlier + later_term for earlier, later_term in zip(grad_sums, step_terms))
            )
        adjoint = diffuse(adjoint, adjoint_faces, rate_values, rate_faces) + state_grad.reshape(
            (2,) + block_shape
        )
    start_sensitivity = adjoint * (2.0 * total_cells)
    pieces = list(grad_sums) + [loss_part[None]]
    flat = jnp.concatenate([piece.reshape(-1) for piece in pieces])
    summed_flat = lax.psum(flat, ("blk", "gy", "rep"))
    summed = []
    start = 0
    for piece in pieces:
        summed.append(summed_flat[start:start + piece.size].reshape(piece.shape))
        start += piece.size
    position = lax.axis_index("rep")
    share_width = w_in.shape[0]
    grad_w_in = lax.dynamic_slice_in_dim(summed[0], position * share_width, share_width, 0)
    grad_b_in = lax.dynamic_slice_in_dim(summed[1], position * share_width, share_width, 0)
    grad_w_mid = lax.dynamic_slice_in_dim(summed[2], position * share_width, share_width, 0)
    grad_b_mid = lax.dynamic_slice_in_dim(summed[3], position * share_width, share_width, 0)
    grad_w_out = lax.dynamic_slice_in_dim(summed[4], position * share_width, share_width, 1)
    grad_b_out = summed[5]
    loss_total = summed[6][0]
    return (
        state_now,
        loss_total,
        grad_w_in,
        grad_b_in,
        grad_w_mid,
        grad_b_mid,
        grad_w_out,
        grad_b_out,
        start_sensitivity,
    )


def solution(mesh):
    in_specs = (
        P("blk", "gy", "rep"),
        P(None, "blk", "gy", "rep"),
        P(None, "blk", "gy", "rep"),
        P(),
        P("rep", None),
        P("rep"),
        P("rep", None),
        P("rep"),
        P(None, "rep"),
        P(),
    )
    out_specs = (
        P(None, "blk", "gy", "rep"),
        P(),
        P("rep", None),
        P("rep"),
        P("rep", None),
        P("rep"),
        P(None, "rep"),
        P(),
        P(None, "blk", "gy", "rep"),
    )
    return jax.shard_map(
        per_device, mesh=mesh, in_specs=in_specs, out_specs=out_specs, check_vma=False
    )
```

```python
import functools

import jax
import jax.numpy as jnp
from jax import lax
from jax.experimental import pallas as pl
from jax.experimental.pallas import tpu as pltpu
from jax.sharding import PartitionSpec as P

STEPS = 4


RATE_MAX = 0.15

AXES = (("rep", 3), ("gy", 2), ("blk", 1))
MESH_AXES = ("blk", "gy", "rep")
COLLECTIVE_IDS = {4: 0, 2: 1}


def _halo_kernel(sizes, rows, *refs):
    sends = refs[0:3]
    outs = refs[3:6]
    landing = refs[6:9]
    send_sems, recv_sems = refs[9], refs[10]
    here = [lax.axis_index(name) for name in MESH_AXES]

    def neighbour(axis, step):
        coords = list(here)
        position = MESH_AXES.index(axis)
        coords[position] = lax.rem(here[position] + step + sizes[position], sizes[position])
        return tuple(coords)

    targets = []
    for axis, dim in AXES:
        targets.append((neighbour(axis, 1), neighbour(axis, -1)))
    barrier = pltpu.get_barrier_semaphore()
    for plus, minus in targets:
        for peer in (plus, minus):
            pl.semaphore_signal(barrier, 1, device_id=peer, device_id_type=pl.DeviceIdType.MESH)
    pl.semaphore_wait(barrier, 6)
    copies = []
    for direction in range(3):
        plus, minus = targets[direction]
        for slot, peer in ((0, plus), (1, minus)):
            index = 2 * direction + slot
            copy = pltpu.make_async_remote_copy(
                src_ref=sends[direction].at[slot],
                dst_ref=landing[direction].at[slot],
                send_sem=send_sems.at[index],
                recv_sem=recv_sems.at[index],
                device_id=peer,
                device_id_type=pl.DeviceIdType.MESH,
            )
            copy.start()
            copies.append(copy)
    for copy in copies:
        copy.wait()
    for direction in range(3):
        outs[direction][...] = landing[direction][...]


def pack_layer(layer):
    flat = layer.reshape(-1)
    rows = -(-flat.size // 128)
    flat = jnp.pad(flat, (0, rows * 128 - flat.size))
    return flat.reshape(rows, 128)


def exchange_faces(fields):
    sends = []
    layer_shapes = []
    for direction, (axis, dim) in enumerate(AXES):
        block = fields[direction]
        size = block.shape[dim]
        last = lax.slice_in_dim(block, size - 1, size, axis=dim)
        first = lax.slice_in_dim(block, 0, 1, axis=dim)
        layer_shapes.append(last.shape)
        sends.append(jnp.stack([pack_layer(last), pack_layer(first)]))
    sizes = tuple(lax.axis_size(name) for name in MESH_AXES)
    rows = tuple(send.shape[1] for send in sends)
    vmem = pl.BlockSpec(memory_space=pltpu.VMEM)
    received = pl.pallas_call(
        functools.partial(_halo_kernel, sizes, rows),
        out_shape=tuple(jax.ShapeDtypeStruct(send.shape, send.dtype) for send in sends),
        in_specs=[vmem] * 3,
        out_specs=(vmem,) * 3,
        scratch_shapes=[pltpu.VMEM(send.shape, send.dtype) for send in sends]
        + [pltpu.SemaphoreType.DMA((6,)), pltpu.SemaphoreType.DMA((6,))],
        compiler_params=pltpu.CompilerParams(
            collective_id=COLLECTIVE_IDS[fields[0].shape[0]], has_side_effects=True
        ),
    )(*sends)
    faces = []
    for direction in range(3):
        shape = layer_shapes[direction]
        count = 1
        for extent in shape:
            count *= extent
        pair = received[direction].reshape(2, -1)[:, :count]
        faces.append((pair[0].reshape(shape), pair[1].reshape(shape)))
    return faces


def shifted(block, low, high, dim, offset):
    size = block.shape[dim]
    if offset == 1:
        return jnp.concatenate([lax.slice_in_dim(block, 1, size, axis=dim), high], axis=dim)
    return jnp.concatenate([low, lax.slice_in_dim(block, 0, size - 1, axis=dim)], axis=dim)


def diffuse(field, field_faces, rates, rate_faces):
    summed = field
    for direction, (axis, dim) in enumerate(AXES):
        rate_here = rates[direction::3]
        for offset in (1, -1):
            low, high = field_faces[direction]
            rlow, rhigh = rate_faces[direction]
            rate_next = shifted(rate_here, rlow, rhigh, dim, offset)
            summed = summed + 0.5 * (rate_here + rate_next) * (
                shifted(field, low, high, dim, offset) - field
            )
    return summed


def rate_cotangent(state, state_faces, adjoint, adjoint_faces):
    pieces_list = []
    for direction, (axis, dim) in enumerate(AXES):
        summed = jnp.zeros_like(state)
        for offset in (1, -1):
            slow, shigh = state_faces[direction]
            alow, ahigh = adjoint_faces[direction]
            summed = summed + (shifted(state, slow, shigh, dim, offset) - state) * (
                shifted(adjoint, alow, ahigh, dim, offset) - adjoint
            )
        pieces_list.append(-0.5 * summed)
    stacked = jnp.stack(pieces_list, axis=1)
    return stacked.reshape((6,) + stacked.shape[2:])


def embed_lookup(emb_table, grain_flat):
    table_rows = emb_table.shape[0]
    one_hot = (grain_flat[None, :] == lax.broadcasted_iota(jnp.int32, (table_rows, 1), 0)).astype(
        jnp.bfloat16
    )
    looked = jnp.dot(emb_table.T, one_hot, preferred_element_type=jnp.float32)
    return looked.astype(jnp.bfloat16)


def forward_layers(params, features):
    w_in, b_in, w_mid, b_mid, w_out, b_out = params
    act_one = jnp.tanh(
        jnp.dot(w_in, features, preferred_element_type=jnp.float32)
        + b_in.astype(jnp.float32)[:, None]
    )
    hid_one = act_one.astype(jnp.bfloat16)
    act_two = jnp.tanh(
        jnp.dot(w_mid, hid_one, preferred_element_type=jnp.float32)
        + b_mid.astype(jnp.float32)[:, None]
    )
    hid_two = act_two.astype(jnp.bfloat16)
    logits = (
        jnp.dot(w_out, hid_two, preferred_element_type=jnp.float32)
        + b_out.astype(jnp.float32)[:, None]
    )
    return (RATE_MAX * jax.nn.sigmoid(logits), act_one, hid_one, act_two, hid_two)


def backward_layers(params, features, rate_grad, forward_values):
    w_in, b_in, w_mid, b_mid, w_out, b_out = params
    rate_values, act_one, hid_one, act_two, hid_two = forward_values
    out_grad = (rate_grad * rate_values * (1.0 - rate_values / RATE_MAX)).astype(jnp.bfloat16)
    two_grad = (
        jnp.dot(w_out.T, out_grad, preferred_element_type=jnp.float32) * (1.0 - act_two * act_two)
    ).astype(jnp.bfloat16)
    one_grad = (
        jnp.dot(w_mid.T, two_grad, preferred_element_type=jnp.float32) * (1.0 - act_one * act_one)
    ).astype(jnp.bfloat16)
    grad_terms = (
        jnp.dot(one_grad, features.T, preferred_element_type=jnp.float32),
        jnp.sum(one_grad, axis=1, dtype=jnp.float32),
        jnp.dot(two_grad, hid_one.T, preferred_element_type=jnp.float32),
        jnp.sum(two_grad, axis=1, dtype=jnp.float32),
        jnp.dot(out_grad, hid_two.T, preferred_element_type=jnp.float32),
        jnp.sum(out_grad, axis=1, dtype=jnp.float32),
    )
    state_grad = jnp.dot(w_in[:, -2:].T, one_grad, preferred_element_type=jnp.float32)
    return (grad_terms, state_grad)


def gather_params(w_in, b_in, w_mid, b_mid, w_out, b_out):
    n_in = w_in.shape[1]
    n_mid = w_mid.shape[1]
    packed = jnp.concatenate(
        [w_in, b_in[:, None], w_mid, b_mid[:, None], w_out.T], axis=1
    ).astype(jnp.bfloat16)
    full = lax.all_gather(packed, "rep", axis=0, tiled=True)
    col = 0
    w_in_b = full[:, col:col + n_in]
    col += n_in
    b_in_b = full[:, col]
    col += 1
    w_mid_b = full[:, col:col + n_mid]
    col += n_mid
    b_mid_b = full[:, col]
    col += 1
    w_out_b = full[:, col:].T
    return (w_in_b, b_in_b, w_mid_b, b_mid_b, w_out_b, b_out.astype(jnp.bfloat16))


def per_device(
    grain_id, init_masks, target_masks, emb_table, w_in, b_in, w_mid, b_mid, w_out, b_out
):
    params = gather_params(w_in, b_in, w_mid, b_mid, w_out, b_out)
    depth_cells, row_cells, col_cells = grain_id.shape
    cell_count = depth_cells * row_cells * col_cells
    block_shape = (depth_cells, row_cells, col_cells)
    embedding = embed_lookup(emb_table, grain_id.reshape(cell_count))
    state_now = init_masks.astype(jnp.float32)
    history = []
    for step_index in range(STEPS):
        features = jnp.concatenate(
            [embedding, state_now.reshape(2, cell_count).astype(jnp.bfloat16)], axis=0
        )
        rate_values = forward_layers(params, features)[0].reshape((6,) + block_shape)
        faces = exchange_faces(
            [jnp.concatenate([state_now, rate_values[d::3]], axis=0) for d in range(3)]
        )
        state_faces = [(low[:2], high[:2]) for low, high in faces]
        rate_faces = [(low[2:], high[2:]) for low, high in faces]
        history.append((state_now, state_faces, rate_values, rate_faces))
        state_now = diffuse(state_now, state_faces, rate_values, rate_faces)
    misfit = state_now - target_masks.astype(jnp.float32)
    total_cells = float(
        cell_count * lax.axis_size("blk") * lax.axis_size("gy") * lax.axis_size("rep")
    )
    loss_part = jnp.sum(misfit * misfit) / (4.0 * total_cells)
    adjoint = misfit / (2.0 * total_cells)
    grad_sums = None
    for step_index in reversed(range(STEPS)):
        state_t, state_faces, rate_values, rate_faces = history[step_index]
        adjoint_faces = exchange_faces([adjoint] * 3)
        rate_grad = rate_cotangent(state_t, state_faces, adjoint, adjoint_faces).reshape(
            6, cell_count
        )
        features = jnp.concatenate(
            [embedding, state_t.reshape(2, cell_count).astype(jnp.bfloat16)], axis=0
        )
        forward_values = forward_layers(params, features)
        step_terms, state_grad = backward_layers(params, features, rate_grad, forward_values)
        if grad_sums is None:
            grad_sums = step_terms
        else:
            grad_sums = tuple(
                (earlier + later_term for earlier, later_term in zip(grad_sums, step_terms))
            )
        adjoint = diffuse(adjoint, adjoint_faces, rate_values, rate_faces) + state_grad.reshape(
            (2,) + block_shape
        )
    start_sensitivity = adjoint * (2.0 * total_cells)
    pieces = list(grad_sums) + [loss_part[None]]
    flat = jnp.concatenate([piece.reshape(-1) for piece in pieces])
    summed_flat = lax.psum(flat, ("blk", "gy", "rep"))
    summed = []
    start = 0
    for piece in pieces:
        summed.append(summed_flat[start:start + piece.size].reshape(piece.shape))
        start += piece.size
    position = lax.axis_index("rep")
    share_width = w_in.shape[0]
    grad_w_in = lax.dynamic_slice_in_dim(summed[0], position * share_width, share_width, 0)
    grad_b_in = lax.dynamic_slice_in_dim(summed[1], position * share_width, share_width, 0)
    grad_w_mid = lax.dynamic_slice_in_dim(summed[2], position * share_width, share_width, 0)
    grad_b_mid = lax.dynamic_slice_in_dim(summed[3], position * share_width, share_width, 0)
    grad_w_out = lax.dynamic_slice_in_dim(summed[4], position * share_width, share_width, 1)
    grad_b_out = summed[5]
    loss_total = summed[6][0]
    return (
        state_now,
        loss_total,
        grad_w_in,
        grad_b_in,
        grad_w_mid,
        grad_b_mid,
        grad_w_out,
        grad_b_out,
        start_sensitivity,
    )


def solution(mesh):
    in_specs = (
        P("blk", "gy", "rep"),
        P(None, "blk", "gy", "rep"),
        P(None, "blk", "gy", "rep"),
        P(),
        P("rep", None),
        P("rep"),
        P("rep", None),
        P("rep"),
        P(None, "rep"),
        P(),
    )
    out_specs = (
        P(None, "blk", "gy", "rep"),
        P(),
        P("rep", None),
        P("rep"),
        P("rep", None),
        P("rep"),
        P(None, "rep"),
        P(),
        P(None, "blk", "gy", "rep"),
    )
    return jax.shard_map(
        per_device, mesh=mesh, in_specs=in_specs, out_specs=out_specs, check_vma=False
    )
```

```python
import functools

import jax
import jax.numpy as jnp
from jax import lax
from jax.experimental import pallas as pl
from jax.experimental.pallas import tpu as pltpu
from jax.sharding import PartitionSpec as P

STEPS = 4


RATE_MAX = 0.15

AXES = (("rep", 3), ("gy", 2), ("blk", 1))
MESH_AXES = ("blk", "gy", "rep")
COLLECTIVE_IDS = {4: 0, 2: 1}


def _halo_kernel(sizes, rows, *refs):
    sends = refs[0:3]
    outs = refs[3:6]
    landing = refs[6:9]
    send_sems, recv_sems = refs[9], refs[10]
    here = [lax.axis_index(name) for name in MESH_AXES]

    def neighbour(axis, step):
        coords = list(here)
        position = MESH_AXES.index(axis)
        coords[position] = lax.rem(here[position] + step + sizes[position], sizes[position])
        return tuple(coords)

    targets = []
    for axis, dim in AXES:
        targets.append((neighbour(axis, 1), neighbour(axis, -1)))
    barrier = pltpu.get_barrier_semaphore()
    for plus, minus in targets:
        for peer in (plus, minus):
            pl.semaphore_signal(barrier, 1, device_id=peer, device_id_type=pl.DeviceIdType.MESH)
    pl.semaphore_wait(barrier, 6)
    copies = []
    for direction in range(3):
        plus, minus = targets[direction]
        for slot, peer in ((0, plus), (1, minus)):
            index = 2 * direction + slot
            copy = pltpu.make_async_remote_copy(
                src_ref=sends[direction].at[slot],
                dst_ref=landing[direction].at[slot],
                send_sem=send_sems.at[index],
                recv_sem=recv_sems.at[index],
                device_id=peer,
                device_id_type=pl.DeviceIdType.MESH,
            )
            copy.start()
            copies.append(copy)
    for copy in copies:
        copy.wait()
    for direction in range(3):
        outs[direction][...] = landing[direction][...]


def _allreduce_kernel(partners, partial_ref, out_ref, acc, landing, send_sems, recv_sems):
    barrier = pltpu.get_barrier_semaphore()
    for peer in partners:
        pl.semaphore_signal(barrier, 1, device_id=peer, device_id_type=pl.DeviceIdType.MESH)
    pl.semaphore_wait(barrier, len(partners))
    acc[...] = partial_ref[...]
    for index, peer in enumerate(partners):
        copy = pltpu.make_async_remote_copy(
            src_ref=acc,
            dst_ref=landing.at[index],
            send_sem=send_sems.at[index],
            recv_sem=recv_sems.at[index],
            device_id=peer,
            device_id_type=pl.DeviceIdType.MESH,
        )
        copy.start()
        copy.wait()
        acc[...] = acc[...] + landing[index]
    out_ref[...] = acc[...]


def _doubling_partners():
    here = [lax.axis_index(name) for name in MESH_AXES]
    partners = []
    for name in ("rep", "gy", "blk"):
        position = MESH_AXES.index(name)
        size = lax.axis_size(name)
        bit = 1
        while bit < size:
            digit = lax.rem(here[position] // bit, 2)
            coords = list(here)
            coords[position] = here[position] + bit * (1 - 2 * digit)
            partners.append(tuple(coords))
            bit *= 2
    return partners


def _power_of_two(count):
    return count & (count - 1) == 0


def sum_everywhere(flat):
    if not all(_power_of_two(lax.axis_size(name)) for name in MESH_AXES):
        return lax.psum(flat, MESH_AXES)
    size = flat.shape[0]
    rows = -(-size // 1024) * 8
    block = jnp.pad(flat, (0, rows * 128 - size)).reshape(rows, 128)
    rounds = sum(lax.axis_size(name).bit_length() - 1 for name in MESH_AXES)
    vmem = pl.BlockSpec(memory_space=pltpu.VMEM)

    def kernel(*refs):
        _allreduce_kernel(_doubling_partners(), *refs)

    summed = pl.pallas_call(
        kernel,
        out_shape=jax.ShapeDtypeStruct(block.shape, block.dtype),
        in_specs=[vmem],
        out_specs=vmem,
        scratch_shapes=[
            pltpu.VMEM(block.shape, block.dtype),
            pltpu.VMEM((rounds,) + block.shape, block.dtype),
            pltpu.SemaphoreType.DMA((rounds,)),
            pltpu.SemaphoreType.DMA((rounds,)),
        ],
        compiler_params=pltpu.CompilerParams(collective_id=2, has_side_effects=True),
    )(block)
    return summed.reshape(-1)[:size]


def pack_layer(layer):
    flat = layer.reshape(-1)
    rows = -(-flat.size // 128)
    flat = jnp.pad(flat, (0, rows * 128 - flat.size))
    return flat.reshape(rows, 128)


def exchange_faces(fields):
    sends = []
    layer_shapes = []
    for direction, (axis, dim) in enumerate(AXES):
        block = fields[direction]
        size = block.shape[dim]
        last = lax.slice_in_dim(block, size - 1, size, axis=dim)
        first = lax.slice_in_dim(block, 0, 1, axis=dim)
        layer_shapes.append(last.shape)
        sends.append(jnp.stack([pack_layer(last), pack_layer(first)]))
    sizes = tuple(lax.axis_size(name) for name in MESH_AXES)
    rows = tuple(send.shape[1] for send in sends)
    vmem = pl.BlockSpec(memory_space=pltpu.VMEM)
    received = pl.pallas_call(
        functools.partial(_halo_kernel, sizes, rows),
        out_shape=tuple(jax.ShapeDtypeStruct(send.shape, send.dtype) for send in sends),
        in_specs=[vmem] * 3,
        out_specs=(vmem,) * 3,
        scratch_shapes=[pltpu.VMEM(send.shape, send.dtype) for send in sends]
        + [pltpu.SemaphoreType.DMA((6,)), pltpu.SemaphoreType.DMA((6,))],
        compiler_params=pltpu.CompilerParams(
            collective_id=COLLECTIVE_IDS[fields[0].shape[0]], has_side_effects=True
        ),
    )(*sends)
    faces = []
    for direction in range(3):
        shape = layer_shapes[direction]
        count = 1
        for extent in shape:
            count *= extent
        pair = received[direction].reshape(2, -1)[:, :count]
        faces.append((pair[0].reshape(shape), pair[1].reshape(shape)))
    return faces


def shifted(block, low, high, dim, offset):
    size = block.shape[dim]
    if offset == 1:
        return jnp.concatenate([lax.slice_in_dim(block, 1, size, axis=dim), high], axis=dim)
    return jnp.concatenate([low, lax.slice_in_dim(block, 0, size - 1, axis=dim)], axis=dim)


def diffuse(field, field_faces, rates, rate_faces):
    summed = field
    for direction, (axis, dim) in enumerate(AXES):
        rate_here = rates[direction::3]
        for offset in (1, -1):
            low, high = field_faces[direction]
            rlow, rhigh = rate_faces[direction]
            rate_next = shifted(rate_here, rlow, rhigh, dim, offset)
            summed = summed + 0.5 * (rate_here + rate_next) * (
                shifted(field, low, high, dim, offset) - field
            )
    return summed


def rate_cotangent(state, state_faces, adjoint, adjoint_faces):
    pieces_list = []
    for direction, (axis, dim) in enumerate(AXES):
        summed = jnp.zeros_like(state)
        for offset in (1, -1):
            slow, shigh = state_faces[direction]
            alow, ahigh = adjoint_faces[direction]
            summed = summed + (shifted(state, slow, shigh, dim, offset) - state) * (
                shifted(adjoint, alow, ahigh, dim, offset) - adjoint
            )
        pieces_list.append(-0.5 * summed)
    stacked = jnp.stack(pieces_list, axis=1)
    return stacked.reshape((6,) + stacked.shape[2:])


def embed_lookup(emb_table, grain_flat):
    table_rows = emb_table.shape[0]
    one_hot = (grain_flat[None, :] == lax.broadcasted_iota(jnp.int32, (table_rows, 1), 0)).astype(
        jnp.bfloat16
    )
    looked = jnp.dot(emb_table.T, one_hot, preferred_element_type=jnp.float32)
    return looked.astype(jnp.bfloat16)


def forward_layers(params, features):
    w_in, b_in, w_mid, b_mid, w_out, b_out = params
    act_one = jnp.tanh(
        jnp.dot(w_in, features, preferred_element_type=jnp.float32)
        + b_in.astype(jnp.float32)[:, None]
    )
    hid_one = act_one.astype(jnp.bfloat16)
    act_two = jnp.tanh(
        jnp.dot(w_mid, hid_one, preferred_element_type=jnp.float32)
        + b_mid.astype(jnp.float32)[:, None]
    )
    hid_two = act_two.astype(jnp.bfloat16)
    logits = (
        jnp.dot(w_out, hid_two, preferred_element_type=jnp.float32)
        + b_out.astype(jnp.float32)[:, None]
    )
    return (RATE_MAX * jax.nn.sigmoid(logits), act_one, hid_one, act_two, hid_two)


def backward_layers(params, features, rate_grad, forward_values):
    w_in, b_in, w_mid, b_mid, w_out, b_out = params
    rate_values, act_one, hid_one, act_two, hid_two = forward_values
    out_grad = (rate_grad * rate_values * (1.0 - rate_values / RATE_MAX)).astype(jnp.bfloat16)
    two_grad = (
        jnp.dot(w_out.T, out_grad, preferred_element_type=jnp.float32) * (1.0 - act_two * act_two)
    ).astype(jnp.bfloat16)
    one_grad = (
        jnp.dot(w_mid.T, two_grad, preferred_element_type=jnp.float32) * (1.0 - act_one * act_one)
    ).astype(jnp.bfloat16)
    grad_terms = (
        jnp.dot(one_grad, features.T, preferred_element_type=jnp.float32),
        jnp.sum(one_grad, axis=1, dtype=jnp.float32),
        jnp.dot(two_grad, hid_one.T, preferred_element_type=jnp.float32),
        jnp.sum(two_grad, axis=1, dtype=jnp.float32),
        jnp.dot(out_grad, hid_two.T, preferred_element_type=jnp.float32),
        jnp.sum(out_grad, axis=1, dtype=jnp.float32),
    )
    state_grad = jnp.dot(w_in[:, -2:].T, one_grad, preferred_element_type=jnp.float32)
    return (grad_terms, state_grad)


def gather_params(w_in, b_in, w_mid, b_mid, w_out, b_out):
    n_in = w_in.shape[1]
    n_mid = w_mid.shape[1]
    packed = jnp.concatenate(
        [w_in, b_in[:, None], w_mid, b_mid[:, None], w_out.T], axis=1
    ).astype(jnp.bfloat16)
    full = lax.all_gather(packed, "rep", axis=0, tiled=True)
    col = 0
    w_in_b = full[:, col:col + n_in]
    col += n_in
    b_in_b = full[:, col]
    col += 1
    w_mid_b = full[:, col:col + n_mid]
    col += n_mid
    b_mid_b = full[:, col]
    col += 1
    w_out_b = full[:, col:].T
    return (w_in_b, b_in_b, w_mid_b, b_mid_b, w_out_b, b_out.astype(jnp.bfloat16))


def per_device(
    grain_id, init_masks, target_masks, emb_table, w_in, b_in, w_mid, b_mid, w_out, b_out
):
    params = gather_params(w_in, b_in, w_mid, b_mid, w_out, b_out)
    depth_cells, row_cells, col_cells = grain_id.shape
    cell_count = depth_cells * row_cells * col_cells
    block_shape = (depth_cells, row_cells, col_cells)
    embedding = embed_lookup(emb_table, grain_id.reshape(cell_count))
    state_now = init_masks.astype(jnp.float32)
    history = []
    for step_index in range(STEPS):
        features = jnp.concatenate(
            [embedding, state_now.reshape(2, cell_count).astype(jnp.bfloat16)], axis=0
        )
        rate_values = forward_layers(params, features)[0].reshape((6,) + block_shape)
        faces = exchange_faces(
            [jnp.concatenate([state_now, rate_values[d::3]], axis=0) for d in range(3)]
        )
        state_faces = [(low[:2], high[:2]) for low, high in faces]
        rate_faces = [(low[2:], high[2:]) for low, high in faces]
        history.append((state_now, state_faces, rate_values, rate_faces))
        state_now = diffuse(state_now, state_faces, rate_values, rate_faces)
    misfit = state_now - target_masks.astype(jnp.float32)
    total_cells = float(
        cell_count * lax.axis_size("blk") * lax.axis_size("gy") * lax.axis_size("rep")
    )
    loss_part = jnp.sum(misfit * misfit) / (4.0 * total_cells)
    adjoint = misfit / (2.0 * total_cells)
    grad_sums = None
    for step_index in reversed(range(STEPS)):
        state_t, state_faces, rate_values, rate_faces = history[step_index]
        adjoint_faces = exchange_faces([adjoint] * 3)
        rate_grad = rate_cotangent(state_t, state_faces, adjoint, adjoint_faces).reshape(
            6, cell_count
        )
        features = jnp.concatenate(
            [embedding, state_t.reshape(2, cell_count).astype(jnp.bfloat16)], axis=0
        )
        forward_values = forward_layers(params, features)
        step_terms, state_grad = backward_layers(params, features, rate_grad, forward_values)
        if grad_sums is None:
            grad_sums = step_terms
        else:
            grad_sums = tuple(
                (earlier + later_term for earlier, later_term in zip(grad_sums, step_terms))
            )
        adjoint = diffuse(adjoint, adjoint_faces, rate_values, rate_faces) + state_grad.reshape(
            (2,) + block_shape
        )
    start_sensitivity = adjoint * (2.0 * total_cells)
    pieces = list(grad_sums) + [loss_part[None]]
    flat = jnp.concatenate([piece.reshape(-1) for piece in pieces])
    summed_flat = sum_everywhere(flat)
    summed = []
    start = 0
    for piece in pieces:
        summed.append(summed_flat[start:start + piece.size].reshape(piece.shape))
        start += piece.size
    position = lax.axis_index("rep")
    share_width = w_in.shape[0]
    grad_w_in = lax.dynamic_slice_in_dim(summed[0], position * share_width, share_width, 0)
    grad_b_in = lax.dynamic_slice_in_dim(summed[1], position * share_width, share_width, 0)
    grad_w_mid = lax.dynamic_slice_in_dim(summed[2], position * share_width, share_width, 0)
    grad_b_mid = lax.dynamic_slice_in_dim(summed[3], position * share_width, share_width, 0)
    grad_w_out = lax.dynamic_slice_in_dim(summed[4], position * share_width, share_width, 1)
    grad_b_out = summed[5]
    loss_total = summed[6][0]
    return (
        state_now,
        loss_total,
        grad_w_in,
        grad_b_in,
        grad_w_mid,
        grad_b_mid,
        grad_w_out,
        grad_b_out,
        start_sensitivity,
    )


def solution(mesh):
    in_specs = (
        P("blk", "gy", "rep"),
        P(None, "blk", "gy", "rep"),
        P(None, "blk", "gy", "rep"),
        P(),
        P("rep", None),
        P("rep"),
        P("rep", None),
        P("rep"),
        P(None, "rep"),
        P(),
    )
    out_specs = (
        P(None, "blk", "gy", "rep"),
        P(),
        P("rep", None),
        P("rep"),
        P("rep", None),
        P("rep"),
        P(None, "rep"),
        P(),
        P(None, "blk", "gy", "rep"),
    )
    return jax.shard_map(
        per_device, mesh=mesh, in_specs=in_specs, out_specs=out_specs, check_vma=False
    )
```

```python
import functools

import jax
import jax.numpy as jnp
from jax import lax
from jax.experimental import pallas as pl
from jax.experimental.pallas import tpu as pltpu
from jax.sharding import PartitionSpec as P

STEPS = 4


RATE_MAX = 0.15

AXES = (("rep", 3), ("gy", 2), ("blk", 1))
MESH_AXES = ("blk", "gy", "rep")
RATE_ORDER = (0, 3, 1, 4, 2, 5)


def _neighbour_kernel(sizes, plan, n_fields, *refs):
    fields = refs[:n_fields]
    n_items = sum(len(items) for items in plan)
    outs = refs[n_fields:n_fields + 2 * n_items]
    landing = refs[n_fields + 2 * n_items:n_fields + 4 * n_items]
    send_sems, recv_sems = refs[-2], refs[-1]
    here = [lax.axis_index(name) for name in MESH_AXES]

    def neighbour(axis, step):
        coords = list(here)
        position = MESH_AXES.index(axis)
        coords[position] = lax.rem(here[position] + step + sizes[position], sizes[position])
        return tuple(coords)

    targets = [(neighbour(axis, 1), neighbour(axis, -1)) for axis, dim in AXES]
    barrier = pltpu.get_barrier_semaphore()
    for plus, minus in targets:
        for peer in (plus, minus):
            pl.semaphore_signal(barrier, 1, device_id=peer, device_id_type=pl.DeviceIdType.MESH)
    pl.semaphore_wait(barrier, 6)
    copies = []
    item = 0
    for direction, (axis, dim) in enumerate(AXES):
        plus, minus = targets[direction]
        for field, first, count in plan[direction]:
            group = fields[field].at[first:first + count]
            depth = fields[field].shape[1]
            if dim == 1:
                to_plus, to_minus = group.at[:, depth - 1], group.at[:, 0]
            else:
                to_plus, to_minus = group, group
            for slot, source, peer in ((0, to_plus, plus), (1, to_minus, minus)):
                index = 2 * item + slot
                copy = pltpu.make_async_remote_copy(
                    src_ref=source,
                    dst_ref=landing[index],
                    send_sem=send_sems.at[index],
                    recv_sem=recv_sems.at[index],
                    device_id=peer,
                    device_id_type=pl.DeviceIdType.MESH,
                )
                copy.start()
                copies.append(copy)
            item += 1
    for copy in copies:
        copy.wait()
    item = 0
    for direction, (axis, dim) in enumerate(AXES):
        for field, first, count in plan[direction]:
            group = fields[field].at[first:first + count]
            from_below, from_above = landing[2 * item], landing[2 * item + 1]
            out_plus, out_minus = outs[2 * item], outs[2 * item + 1]
            if dim == 1:
                depth = group.shape[1]
                out_plus[:, 0:depth - 1] = group[:, 1:depth]
                out_plus[:, depth - 1] = from_above[...]
                out_minus[:, 1:depth] = group[:, 0:depth - 1]
                out_minus[:, 0] = from_below[...]
            else:
                values = group[...]
                size = values.shape[dim]
                index = lax.broadcasted_iota(jnp.int32, values.shape, dim)
                out_plus[...] = pltpu.roll(
                    jnp.where(index == 0, from_above[...], values), size - 1, dim
                )
                out_minus[...] = pltpu.roll(
                    jnp.where(index == size - 1, from_below[...], values), 1, dim
                )
            item += 1


def exchange_neighbours(fields, plan, collective_id):
    sizes = tuple(lax.axis_size(name) for name in MESH_AXES)
    group_shapes = []
    landing_shapes = []
    for direction, (axis, dim) in enumerate(AXES):
        for field, first, count in plan[direction]:
            shape = (count,) + fields[field].shape[1:]
            group_shapes.append(shape)
            layer = shape[:1] + shape[2:] if dim == 1 else shape
            landing_shapes += [layer, layer]
    n_items = len(group_shapes)
    vmem = pl.BlockSpec(memory_space=pltpu.VMEM)
    out_shapes = []
    for shape in group_shapes:
        out_shapes += [jax.ShapeDtypeStruct(shape, jnp.float32)] * 2
    shifted = pl.pallas_call(
        functools.partial(_neighbour_kernel, sizes, plan, len(fields)),
        out_shape=tuple(out_shapes),
        in_specs=[vmem] * len(fields),
        out_specs=(vmem,) * len(out_shapes),
        scratch_shapes=[pltpu.VMEM(shape, jnp.float32) for shape in landing_shapes]
        + [pltpu.SemaphoreType.DMA((2 * n_items,)), pltpu.SemaphoreType.DMA((2 * n_items,))],
        compiler_params=pltpu.CompilerParams(collective_id=collective_id, has_side_effects=True),
    )(*fields)
    result = []
    item = 0
    for direction in range(3):
        pairs = []
        for _ in plan[direction]:
            pairs.append((shifted[2 * item], shifted[2 * item + 1]))
            item += 1
        result.append(pairs)
    return result


def _allreduce_kernel(partners, partial_ref, out_ref, acc, landing, send_sems, recv_sems):
    barrier = pltpu.get_barrier_semaphore()
    for peer in partners:
        pl.semaphore_signal(barrier, 1, device_id=peer, device_id_type=pl.DeviceIdType.MESH)
    pl.semaphore_wait(barrier, len(partners))
    acc[...] = partial_ref[...]
    for index, peer in enumerate(partners):
        copy = pltpu.make_async_remote_copy(
            src_ref=acc,
            dst_ref=landing.at[index],
            send_sem=send_sems.at[index],
            recv_sem=recv_sems.at[index],
            device_id=peer,
            device_id_type=pl.DeviceIdType.MESH,
        )
        copy.start()
        copy.wait()
        acc[...] = acc[...] + landing[index]
    out_ref[...] = acc[...]


def _doubling_partners():
    here = [lax.axis_index(name) for name in MESH_AXES]
    partners = []
    for name in ("rep", "gy", "blk"):
        position = MESH_AXES.index(name)
        size = lax.axis_size(name)
        bit = 1
        while bit < size:
            digit = lax.rem(here[position] // bit, 2)
            coords = list(here)
            coords[position] = here[position] + bit * (1 - 2 * digit)
            partners.append(tuple(coords))
            bit *= 2
    return partners


def _power_of_two(count):
    return count & (count - 1) == 0


def sum_everywhere(flat):
    if not all(_power_of_two(lax.axis_size(name)) for name in MESH_AXES):
        return lax.psum(flat, MESH_AXES)
    size = flat.shape[0]
    rows = -(-size // 1024) * 8
    block = jnp.pad(flat, (0, rows * 128 - size)).reshape(rows, 128)
    rounds = sum(lax.axis_size(name).bit_length() - 1 for name in MESH_AXES)
    vmem = pl.BlockSpec(memory_space=pltpu.VMEM)

    def kernel(*refs):
        _allreduce_kernel(_doubling_partners(), *refs)

    summed = pl.pallas_call(
        kernel,
        out_shape=jax.ShapeDtypeStruct(block.shape, block.dtype),
        in_specs=[vmem],
        out_specs=vmem,
        scratch_shapes=[
            pltpu.VMEM(block.shape, block.dtype),
            pltpu.VMEM((rounds,) + block.shape, block.dtype),
            pltpu.SemaphoreType.DMA((rounds,)),
            pltpu.SemaphoreType.DMA((rounds,)),
        ],
        compiler_params=pltpu.CompilerParams(collective_id=2, has_side_effects=True),
    )(block)
    return summed.reshape(-1)[:size]


def diffuse(field, field_nb, rates, rate_nb):
    summed = field
    for direction in range(3):
        rate_here = rates[2 * direction:2 * direction + 2]
        for side, offset in enumerate((1, -1)):
            summed = summed + 0.5 * (rate_here + rate_nb[direction][side]) * (
                field_nb[direction][side] - field
            )
    return summed


def rate_cotangent(state, state_nb, adjoint, adjoint_nb):
    pieces_list = []
    for direction in range(3):
        summed = jnp.zeros_like(state)
        for side, offset in enumerate((1, -1)):
            summed = summed + (state_nb[direction][side] - state) * (
                adjoint_nb[direction][side] - adjoint
            )
        pieces_list.append(-0.5 * summed)
    return jnp.concatenate(pieces_list, axis=0)


def embed_lookup(emb_table, grain_flat):
    table_rows = emb_table.shape[0]
    one_hot = (grain_flat[None, :] == lax.broadcasted_iota(jnp.int32, (table_rows, 1), 0)).astype(
        jnp.bfloat16
    )
    looked = jnp.dot(emb_table.T, one_hot, preferred_element_type=jnp.float32)
    return looked.astype(jnp.bfloat16)


def forward_layers(params, features):
    w_in, b_in, w_mid, b_mid, w_out, b_out = params
    act_one = jnp.tanh(
        jnp.dot(w_in, features, preferred_element_type=jnp.float32)
        + b_in.astype(jnp.float32)[:, None]
    )
    hid_one = act_one.astype(jnp.bfloat16)
    act_two = jnp.tanh(
        jnp.dot(w_mid, hid_one, preferred_element_type=jnp.float32)
        + b_mid.astype(jnp.float32)[:, None]
    )
    hid_two = act_two.astype(jnp.bfloat16)
    logits = (
        jnp.dot(w_out, hid_two, preferred_element_type=jnp.float32)
        + b_out.astype(jnp.float32)[:, None]
    )
    return (RATE_MAX * jax.nn.sigmoid(logits), act_one, hid_one, act_two, hid_two)


def backward_layers(params, features, rate_grad, forward_values):
    w_in, b_in, w_mid, b_mid, w_out, b_out = params
    rate_values, act_one, hid_one, act_two, hid_two = forward_values
    out_grad = (rate_grad * rate_values * (1.0 - rate_values / RATE_MAX)).astype(jnp.bfloat16)
    two_grad = (
        jnp.dot(w_out.T, out_grad, preferred_element_type=jnp.float32) * (1.0 - act_two * act_two)
    ).astype(jnp.bfloat16)
    one_grad = (
        jnp.dot(w_mid.T, two_grad, preferred_element_type=jnp.float32) * (1.0 - act_one * act_one)
    ).astype(jnp.bfloat16)
    grad_terms = (
        jnp.dot(one_grad, features.T, preferred_element_type=jnp.float32),
        jnp.sum(one_grad, axis=1, dtype=jnp.float32),
        jnp.dot(two_grad, hid_one.T, preferred_element_type=jnp.float32),
        jnp.sum(two_grad, axis=1, dtype=jnp.float32),
        jnp.dot(out_grad, hid_two.T, preferred_element_type=jnp.float32),
        jnp.sum(out_grad, axis=1, dtype=jnp.float32),
    )
    state_grad = jnp.dot(w_in[:, -2:].T, one_grad, preferred_element_type=jnp.float32)
    return (grad_terms, state_grad)


def gather_params(w_in, b_in, w_mid, b_mid, w_out, b_out):
    n_in = w_in.shape[1]
    n_mid = w_mid.shape[1]
    packed = jnp.concatenate(
        [w_in, b_in[:, None], w_mid, b_mid[:, None], w_out.T], axis=1
    ).astype(jnp.bfloat16)
    full = lax.all_gather(packed, "rep", axis=0, tiled=True)
    col = 0
    w_in_b = full[:, col:col + n_in]
    col += n_in
    b_in_b = full[:, col]
    col += 1
    w_mid_b = full[:, col:col + n_mid]
    col += n_mid
    b_mid_b = full[:, col]
    col += 1
    w_out_b = full[:, col:].T
    order = jnp.array(RATE_ORDER)
    return (w_in_b, b_in_b, w_mid_b, b_mid_b, w_out_b[order], b_out.astype(jnp.bfloat16)[order])


def per_device(
    grain_id, init_masks, target_masks, emb_table, w_in, b_in, w_mid, b_mid, w_out, b_out
):
    params = gather_params(w_in, b_in, w_mid, b_mid, w_out, b_out)
    depth_cells, row_cells, col_cells = grain_id.shape
    cell_count = depth_cells * row_cells * col_cells
    block_shape = (depth_cells, row_cells, col_cells)
    embedding = embed_lookup(emb_table, grain_id.reshape(cell_count))
    state_now = init_masks.astype(jnp.float32)
    history = []
    forward_plan = [[(0, 0, 2), (1, 2 * d, 2)] for d in range(3)]
    for step_index in range(STEPS):
        features = jnp.concatenate(
            [embedding, state_now.reshape(2, cell_count).astype(jnp.bfloat16)], axis=0
        )
        rate_values = forward_layers(params, features)[0].reshape((6,) + block_shape)
        neighbours = exchange_neighbours([state_now, rate_values], forward_plan, 0)
        state_nb = [pairs[0] for pairs in neighbours]
        rate_nb = [pairs[1] for pairs in neighbours]
        history.append((state_now, state_nb, rate_values, rate_nb))
        state_now = diffuse(state_now, state_nb, rate_values, rate_nb)
    misfit = state_now - target_masks.astype(jnp.float32)
    total_cells = float(
        cell_count * lax.axis_size("blk") * lax.axis_size("gy") * lax.axis_size("rep")
    )
    loss_part = jnp.sum(misfit * misfit) / (4.0 * total_cells)
    adjoint = misfit / (2.0 * total_cells)
    grad_sums = None
    for step_index in reversed(range(STEPS)):
        state_t, state_nb, rate_values, rate_nb = history[step_index]
        adjoint_nb = [
            pairs[0] for pairs in exchange_neighbours([adjoint], [[(0, 0, 2)]] * 3, 1)
        ]
        rate_grad = rate_cotangent(state_t, state_nb, adjoint, adjoint_nb).reshape(
            6, cell_count
        )
        features = jnp.concatenate(
            [embedding, state_t.reshape(2, cell_count).astype(jnp.bfloat16)], axis=0
        )
        forward_values = forward_layers(params, features)
        step_terms, state_grad = backward_layers(params, features, rate_grad, forward_values)
        if grad_sums is None:
            grad_sums = step_terms
        else:
            grad_sums = tuple(
                (earlier + later_term for earlier, later_term in zip(grad_sums, step_terms))
            )
        adjoint = diffuse(adjoint, adjoint_nb, rate_values, rate_nb) + state_grad.reshape(
            (2,) + block_shape
        )
    start_sensitivity = adjoint * (2.0 * total_cells)
    pieces = list(grad_sums) + [loss_part[None]]
    flat = jnp.concatenate([piece.reshape(-1) for piece in pieces])
    summed_flat = sum_everywhere(flat)
    summed = []
    start = 0
    for piece in pieces:
        summed.append(summed_flat[start:start + piece.size].reshape(piece.shape))
        start += piece.size
    position = lax.axis_index("rep")
    share_width = w_in.shape[0]
    grad_w_in = lax.dynamic_slice_in_dim(summed[0], position * share_width, share_width, 0)
    grad_b_in = lax.dynamic_slice_in_dim(summed[1], position * share_width, share_width, 0)
    grad_w_mid = lax.dynamic_slice_in_dim(summed[2], position * share_width, share_width, 0)
    grad_b_mid = lax.dynamic_slice_in_dim(summed[3], position * share_width, share_width, 0)
    back = jnp.array([RATE_ORDER.index(channel) for channel in range(6)])
    grad_w_out = lax.dynamic_slice_in_dim(summed[4][back], position * share_width, share_width, 1)
    grad_b_out = summed[5][back]
    loss_total = summed[6][0]
    return (
        state_now,
        loss_total,
        grad_w_in,
        grad_b_in,
        grad_w_mid,
        grad_b_mid,
        grad_w_out,
        grad_b_out,
        start_sensitivity,
    )


def solution(mesh):
    in_specs = (
        P("blk", "gy", "rep"),
        P(None, "blk", "gy", "rep"),
        P(None, "blk", "gy", "rep"),
        P(),
        P("rep", None),
        P("rep"),
        P("rep", None),
        P("rep"),
        P(None, "rep"),
        P(),
    )
    out_specs = (
        P(None, "blk", "gy", "rep"),
        P(),
        P("rep", None),
        P("rep"),
        P("rep", None),
        P("rep"),
        P(None, "rep"),
        P(),
        P(None, "blk", "gy", "rep"),
    )
    return jax.shard_map(
        per_device, mesh=mesh, in_specs=in_specs, out_specs=out_specs, check_vma=False
    )
```

```python
import functools

import jax
import jax.numpy as jnp
from jax import lax
from jax.experimental import pallas as pl
from jax.experimental.pallas import tpu as pltpu
from jax.sharding import PartitionSpec as P

STEPS = 4


RATE_MAX = 0.15

AXES = (("rep", 3), ("gy", 2), ("blk", 1))
MESH_AXES = ("blk", "gy", "rep")
RATE_ORDER = (0, 3, 1, 4, 2, 5)


def _neighbour_kernel(sizes, plan, n_fields, *refs):
    fields = refs[:n_fields]
    n_items = sum(len(items) for items in plan)
    outs = refs[n_fields:n_fields + 2 * n_items]
    landing = refs[n_fields + 2 * n_items:n_fields + 4 * n_items]
    send_sems, recv_sems = refs[-2], refs[-1]
    here = [lax.axis_index(name) for name in MESH_AXES]

    def neighbour(axis, step):
        coords = list(here)
        position = MESH_AXES.index(axis)
        coords[position] = lax.rem(here[position] + step + sizes[position], sizes[position])
        return tuple(coords)

    targets = [(neighbour(axis, 1), neighbour(axis, -1)) for axis, dim in AXES]
    barrier = pltpu.get_barrier_semaphore()
    for plus, minus in targets:
        for peer in (plus, minus):
            pl.semaphore_signal(barrier, 1, device_id=peer, device_id_type=pl.DeviceIdType.MESH)
    pl.semaphore_wait(barrier, 6)
    copies = []
    item = 0
    for direction, (axis, dim) in enumerate(AXES):
        plus, minus = targets[direction]
        for field, first, count in plan[direction]:
            group = fields[field].at[first:first + count]
            depth = fields[field].shape[1]
            if dim == 1:
                to_plus, to_minus = group.at[:, depth - 1], group.at[:, 0]
            else:
                to_plus, to_minus = group, group
            for slot, source, peer in ((0, to_plus, plus), (1, to_minus, minus)):
                index = 2 * item + slot
                copy = pltpu.make_async_remote_copy(
                    src_ref=source,
                    dst_ref=landing[index],
                    send_sem=send_sems.at[index],
                    recv_sem=recv_sems.at[index],
                    device_id=peer,
                    device_id_type=pl.DeviceIdType.MESH,
                )
                copy.start()
                copies.append(copy)
            item += 1
    for copy in copies:
        copy.wait()
    item = 0
    for direction, (axis, dim) in enumerate(AXES):
        for field, first, count in plan[direction]:
            group = fields[field].at[first:first + count]
            from_below, from_above = landing[2 * item], landing[2 * item + 1]
            out_plus, out_minus = outs[2 * item], outs[2 * item + 1]
            if dim == 1:
                depth = group.shape[1]
                out_plus[:, 0:depth - 1] = group[:, 1:depth]
                out_plus[:, depth - 1] = from_above[...]
                out_minus[:, 1:depth] = group[:, 0:depth - 1]
                out_minus[:, 0] = from_below[...]
            else:
                values = group[...]
                size = values.shape[dim]
                index = lax.broadcasted_iota(jnp.int32, values.shape, dim)
                out_plus[...] = pltpu.roll(
                    jnp.where(index == 0, from_above[...], values), size - 1, dim
                )
                out_minus[...] = pltpu.roll(
                    jnp.where(index == size - 1, from_below[...], values), 1, dim
                )
            item += 1


def exchange_neighbours(fields, plan, collective_id):
    sizes = tuple(lax.axis_size(name) for name in MESH_AXES)
    group_shapes = []
    landing_shapes = []
    for direction, (axis, dim) in enumerate(AXES):
        for field, first, count in plan[direction]:
            shape = (count,) + fields[field].shape[1:]
            group_shapes.append(shape)
            layer = shape[:1] + shape[2:] if dim == 1 else shape
            landing_shapes += [layer, layer]
    n_items = len(group_shapes)
    vmem = pl.BlockSpec(memory_space=pltpu.VMEM)
    out_shapes = []
    for shape in group_shapes:
        out_shapes += [jax.ShapeDtypeStruct(shape, jnp.float32)] * 2
    shifted = pl.pallas_call(
        functools.partial(_neighbour_kernel, sizes, plan, len(fields)),
        out_shape=tuple(out_shapes),
        in_specs=[vmem] * len(fields),
        out_specs=(vmem,) * len(out_shapes),
        scratch_shapes=[pltpu.VMEM(shape, jnp.float32) for shape in landing_shapes]
        + [pltpu.SemaphoreType.DMA((2 * n_items,)), pltpu.SemaphoreType.DMA((2 * n_items,))],
        compiler_params=pltpu.CompilerParams(collective_id=collective_id, has_side_effects=True),
    )(*fields)
    result = []
    item = 0
    for direction in range(3):
        pairs = []
        for _ in plan[direction]:
            pairs.append((shifted[2 * item], shifted[2 * item + 1]))
            item += 1
        result.append(pairs)
    return result


def _allreduce_kernel(stages, partial_ref, out_ref, acc, landing, send_sems, recv_sems):
    here = [lax.axis_index(name) for name in MESH_AXES]

    def member(name, stride, size, digit):
        position = MESH_AXES.index(name)
        own = lax.rem(here[position] // stride, size)
        coords = list(here)
        coords[position] = here[position] + (digit - own) * stride
        return tuple(coords), own

    barrier = pltpu.get_barrier_semaphore()
    partner_count = 0
    for name, stride, size in stages:
        for step in range(1, size):
            position = MESH_AXES.index(name)
            own = lax.rem(here[position] // stride, size)
            digit = lax.rem(own + step, size)
            peer, _ = member(name, stride, size, digit)
            pl.semaphore_signal(barrier, 1, device_id=peer, device_id_type=pl.DeviceIdType.MESH)
            partner_count += 1
    pl.semaphore_wait(barrier, partner_count)
    acc[...] = partial_ref[...]
    for stage, (name, stride, size) in enumerate(stages):
        position = MESH_AXES.index(name)
        own = lax.rem(here[position] // stride, size)
        landing[stage, own] = acc[...]
        sends = []
        receives = []
        for step in range(1, size):
            digit = lax.rem(own + step, size)
            peer, _ = member(name, stride, size, digit)
            copy = pltpu.make_async_remote_copy(
                src_ref=acc,
                dst_ref=landing.at[stage, own],
                send_sem=send_sems.at[stage, step],
                recv_sem=recv_sems.at[stage, own],
                device_id=peer,
                device_id_type=pl.DeviceIdType.MESH,
            )
            copy.start()
            sends.append(copy)
            receives.append(
                pltpu.make_async_remote_copy(
                    src_ref=acc,
                    dst_ref=landing.at[stage, digit],
                    send_sem=send_sems.at[stage, step],
                    recv_sem=recv_sems.at[stage, digit],
                    device_id=peer,
                    device_id_type=pl.DeviceIdType.MESH,
                )
            )
        for copy in sends:
            copy.wait_send()
        for copy in receives:
            copy.wait_recv()
        if size == 4:
            acc[...] = (landing[stage, 0] + landing[stage, 1]) + (
                landing[stage, 2] + landing[stage, 3]
            )
        else:
            acc[...] = landing[stage, 0] + landing[stage, 1]
    out_ref[...] = acc[...]


def _stages():
    stages = []
    for name in ("rep", "gy", "blk"):
        size = lax.axis_size(name)
        stride = 1
        while stride < size:
            group = 4 if size // stride >= 4 else 2
            stages.append((name, stride, group))
            stride *= group
    return stages


def _power_of_two(count):
    return count & (count - 1) == 0


def sum_everywhere(flat):
    if not all(_power_of_two(lax.axis_size(name)) for name in MESH_AXES):
        return lax.psum(flat, MESH_AXES)
    size = flat.shape[0]
    rows = -(-size // 1024) * 8
    block = jnp.pad(flat, (0, rows * 128 - size)).reshape(rows, 128)
    stages = _stages()
    vmem = pl.BlockSpec(memory_space=pltpu.VMEM)
    summed = pl.pallas_call(
        functools.partial(_allreduce_kernel, stages),
        out_shape=jax.ShapeDtypeStruct(block.shape, block.dtype),
        in_specs=[vmem],
        out_specs=vmem,
        scratch_shapes=[
            pltpu.VMEM(block.shape, block.dtype),
            pltpu.VMEM((len(stages), 4) + block.shape, block.dtype),
            pltpu.SemaphoreType.DMA((len(stages), 4)),
            pltpu.SemaphoreType.DMA((len(stages), 4)),
        ],
        compiler_params=pltpu.CompilerParams(collective_id=2, has_side_effects=True),
    )(block)
    return summed.reshape(-1)[:size]


def diffuse(field, field_nb, rates, rate_nb):
    summed = field
    for direction in range(3):
        rate_here = rates[2 * direction:2 * direction + 2]
        for side, offset in enumerate((1, -1)):
            summed = summed + 0.5 * (rate_here + rate_nb[direction][side]) * (
                field_nb[direction][side] - field
            )
    return summed


def rate_cotangent(state, state_nb, adjoint, adjoint_nb):
    pieces_list = []
    for direction in range(3):
        summed = jnp.zeros_like(state)
        for side, offset in enumerate((1, -1)):
            summed = summed + (state_nb[direction][side] - state) * (
                adjoint_nb[direction][side] - adjoint
            )
        pieces_list.append(-0.5 * summed)
    return jnp.concatenate(pieces_list, axis=0)


def embed_lookup(emb_table, grain_flat):
    table_rows = emb_table.shape[0]
    one_hot = (grain_flat[None, :] == lax.broadcasted_iota(jnp.int32, (table_rows, 1), 0)).astype(
        jnp.bfloat16
    )
    looked = jnp.dot(emb_table.T, one_hot, preferred_element_type=jnp.float32)
    return looked.astype(jnp.bfloat16)


def forward_layers(params, features):
    w_in, b_in, w_mid, b_mid, w_out, b_out = params
    act_one = jnp.tanh(
        jnp.dot(w_in, features, preferred_element_type=jnp.float32)
        + b_in.astype(jnp.float32)[:, None]
    )
    hid_one = act_one.astype(jnp.bfloat16)
    act_two = jnp.tanh(
        jnp.dot(w_mid, hid_one, preferred_element_type=jnp.float32)
        + b_mid.astype(jnp.float32)[:, None]
    )
    hid_two = act_two.astype(jnp.bfloat16)
    logits = (
        jnp.dot(w_out, hid_two, preferred_element_type=jnp.float32)
        + b_out.astype(jnp.float32)[:, None]
    )
    return (RATE_MAX * jax.nn.sigmoid(logits), act_one, hid_one, act_two, hid_two)


def backward_layers(params, features, rate_grad, forward_values):
    w_in, b_in, w_mid, b_mid, w_out, b_out = params
    rate_values, act_one, hid_one, act_two, hid_two = forward_values
    out_grad = (rate_grad * rate_values * (1.0 - rate_values / RATE_MAX)).astype(jnp.bfloat16)
    two_grad = (
        jnp.dot(w_out.T, out_grad, preferred_element_type=jnp.float32) * (1.0 - act_two * act_two)
    ).astype(jnp.bfloat16)
    one_grad = (
        jnp.dot(w_mid.T, two_grad, preferred_element_type=jnp.float32) * (1.0 - act_one * act_one)
    ).astype(jnp.bfloat16)
    grad_terms = (
        jnp.dot(one_grad, features.T, preferred_element_type=jnp.float32),
        jnp.sum(one_grad, axis=1, dtype=jnp.float32),
        jnp.dot(two_grad, hid_one.T, preferred_element_type=jnp.float32),
        jnp.sum(two_grad, axis=1, dtype=jnp.float32),
        jnp.dot(out_grad, hid_two.T, preferred_element_type=jnp.float32),
        jnp.sum(out_grad, axis=1, dtype=jnp.float32),
    )
    state_grad = jnp.dot(w_in[:, -2:].T, one_grad, preferred_element_type=jnp.float32)
    return (grad_terms, state_grad)


def gather_params(w_in, b_in, w_mid, b_mid, w_out, b_out):
    n_in = w_in.shape[1]
    n_mid = w_mid.shape[1]
    packed = jnp.concatenate(
        [w_in, b_in[:, None], w_mid, b_mid[:, None], w_out.T], axis=1
    ).astype(jnp.bfloat16)
    full = lax.all_gather(packed, "rep", axis=0, tiled=True)
    col = 0
    w_in_b = full[:, col:col + n_in]
    col += n_in
    b_in_b = full[:, col]
    col += 1
    w_mid_b = full[:, col:col + n_mid]
    col += n_mid
    b_mid_b = full[:, col]
    col += 1
    w_out_b = full[:, col:].T
    order = jnp.array(RATE_ORDER)
    return (w_in_b, b_in_b, w_mid_b, b_mid_b, w_out_b[order], b_out.astype(jnp.bfloat16)[order])


def per_device(
    grain_id, init_masks, target_masks, emb_table, w_in, b_in, w_mid, b_mid, w_out, b_out
):
    params = gather_params(w_in, b_in, w_mid, b_mid, w_out, b_out)
    depth_cells, row_cells, col_cells = grain_id.shape
    cell_count = depth_cells * row_cells * col_cells
    block_shape = (depth_cells, row_cells, col_cells)
    embedding = embed_lookup(emb_table, grain_id.reshape(cell_count))
    state_now = init_masks.astype(jnp.float32)
    history = []
    forward_plan = [[(0, 0, 2), (1, 2 * d, 2)] for d in range(3)]
    for step_index in range(STEPS):
        features = jnp.concatenate(
            [embedding, state_now.reshape(2, cell_count).astype(jnp.bfloat16)], axis=0
        )
        rate_values = forward_layers(params, features)[0].reshape((6,) + block_shape)
        neighbours = exchange_neighbours([state_now, rate_values], forward_plan, 0)
        state_nb = [pairs[0] for pairs in neighbours]
        rate_nb = [pairs[1] for pairs in neighbours]
        history.append((state_now, state_nb, rate_values, rate_nb))
        state_now = diffuse(state_now, state_nb, rate_values, rate_nb)
    misfit = state_now - target_masks.astype(jnp.float32)
    total_cells = float(
        cell_count * lax.axis_size("blk") * lax.axis_size("gy") * lax.axis_size("rep")
    )
    loss_part = jnp.sum(misfit * misfit) / (4.0 * total_cells)
    adjoint = misfit / (2.0 * total_cells)
    grad_sums = None
    for step_index in reversed(range(STEPS)):
        state_t, state_nb, rate_values, rate_nb = history[step_index]
        adjoint_nb = [
            pairs[0] for pairs in exchange_neighbours([adjoint], [[(0, 0, 2)]] * 3, 1)
        ]
        rate_grad = rate_cotangent(state_t, state_nb, adjoint, adjoint_nb).reshape(
            6, cell_count
        )
        features = jnp.concatenate(
            [embedding, state_t.reshape(2, cell_count).astype(jnp.bfloat16)], axis=0
        )
        forward_values = forward_layers(params, features)
        step_terms, state_grad = backward_layers(params, features, rate_grad, forward_values)
        if grad_sums is None:
            grad_sums = step_terms
        else:
            grad_sums = tuple(
                (earlier + later_term for earlier, later_term in zip(grad_sums, step_terms))
            )
        adjoint = diffuse(adjoint, adjoint_nb, rate_values, rate_nb) + state_grad.reshape(
            (2,) + block_shape
        )
    start_sensitivity = adjoint * (2.0 * total_cells)
    pieces = list(grad_sums) + [loss_part[None]]
    flat = jnp.concatenate([piece.reshape(-1) for piece in pieces])
    summed_flat = sum_everywhere(flat)
    summed = []
    start = 0
    for piece in pieces:
        summed.append(summed_flat[start:start + piece.size].reshape(piece.shape))
        start += piece.size
    position = lax.axis_index("rep")
    share_width = w_in.shape[0]
    grad_w_in = lax.dynamic_slice_in_dim(summed[0], position * share_width, share_width, 0)
    grad_b_in = lax.dynamic_slice_in_dim(summed[1], position * share_width, share_width, 0)
    grad_w_mid = lax.dynamic_slice_in_dim(summed[2], position * share_width, share_width, 0)
    grad_b_mid = lax.dynamic_slice_in_dim(summed[3], position * share_width, share_width, 0)
    back = jnp.array([RATE_ORDER.index(channel) for channel in range(6)])
    grad_w_out = lax.dynamic_slice_in_dim(summed[4][back], position * share_width, share_width, 1)
    grad_b_out = summed[5][back]
    loss_total = summed[6][0]
    return (
        state_now,
        loss_total,
        grad_w_in,
        grad_b_in,
        grad_w_mid,
        grad_b_mid,
        grad_w_out,
        grad_b_out,
        start_sensitivity,
    )


def solution(mesh):
    in_specs = (
        P("blk", "gy", "rep"),
        P(None, "blk", "gy", "rep"),
        P(None, "blk", "gy", "rep"),
        P(),
        P("rep", None),
        P("rep"),
        P("rep", None),
        P("rep"),
        P(None, "rep"),
        P(),
    )
    out_specs = (
        P(None, "blk", "gy", "rep"),
        P(),
        P("rep", None),
        P("rep"),
        P("rep", None),
        P("rep"),
        P(None, "rep"),
        P(),
        P(None, "blk", "gy", "rep"),
    )
    return jax.shard_map(
        per_device, mesh=mesh, in_specs=in_specs, out_specs=out_specs, check_vma=False
    )
```

```python
import functools

import jax
import jax.numpy as jnp
from jax import lax
from jax.experimental import pallas as pl
from jax.experimental.pallas import tpu as pltpu
from jax.sharding import PartitionSpec as P

STEPS = 4


RATE_MAX = 0.15

AXES = (("rep", 3), ("gy", 2), ("blk", 1))
MESH_AXES = ("blk", "gy", "rep")
RATE_ORDER = (0, 3, 1, 4, 2, 5)


def _neighbour_kernel(sizes, plan, n_fields, *refs):
    fields = refs[:n_fields]
    n_items = sum(len(items) for items in plan)
    outs = refs[n_fields:n_fields + 2 * n_items]
    landing = refs[n_fields + 2 * n_items:n_fields + 4 * n_items]
    send_sems, recv_sems = refs[-2], refs[-1]
    here = [lax.axis_index(name) for name in MESH_AXES]

    def neighbour(axis, step):
        coords = list(here)
        position = MESH_AXES.index(axis)
        coords[position] = lax.rem(here[position] + step + sizes[position], sizes[position])
        return tuple(coords)

    targets = [(neighbour(axis, 1), neighbour(axis, -1)) for axis, dim in AXES]
    barrier = pltpu.get_barrier_semaphore()
    for plus, minus in targets:
        for peer in (plus, minus):
            pl.semaphore_signal(barrier, 1, device_id=peer, device_id_type=pl.DeviceIdType.MESH)
    pl.semaphore_wait(barrier, 6)
    copies = []
    item = 0
    for direction, (axis, dim) in enumerate(AXES):
        plus, minus = targets[direction]
        for field, first, count in plan[direction]:
            group = fields[field].at[first:first + count]
            depth = fields[field].shape[1]
            if dim == 1:
                to_plus, to_minus = group.at[:, depth - 1], group.at[:, 0]
            else:
                to_plus, to_minus = group, group
            for slot, source, peer in ((0, to_plus, plus), (1, to_minus, minus)):
                index = 2 * item + slot
                copy = pltpu.make_async_remote_copy(
                    src_ref=source,
                    dst_ref=landing[index],
                    send_sem=send_sems.at[index],
                    recv_sem=recv_sems.at[index],
                    device_id=peer,
                    device_id_type=pl.DeviceIdType.MESH,
                )
                copy.start()
                copies.append(copy)
            item += 1
    for copy in copies:
        copy.wait()
    item = 0
    for direction, (axis, dim) in enumerate(AXES):
        for field, first, count in plan[direction]:
            group = fields[field].at[first:first + count]
            from_below, from_above = landing[2 * item], landing[2 * item + 1]
            out_plus, out_minus = outs[2 * item], outs[2 * item + 1]
            if dim == 1:
                depth = group.shape[1]
                out_plus[:, 0:depth - 1] = group[:, 1:depth]
                out_plus[:, depth - 1] = from_above[...]
                out_minus[:, 1:depth] = group[:, 0:depth - 1]
                out_minus[:, 0] = from_below[...]
            else:
                values = group[...]
                size = values.shape[dim]
                index = lax.broadcasted_iota(jnp.int32, values.shape, dim)
                out_plus[...] = pltpu.roll(
                    jnp.where(index == 0, from_above[...], values), size - 1, dim
                )
                out_minus[...] = pltpu.roll(
                    jnp.where(index == size - 1, from_below[...], values), 1, dim
                )
            item += 1


def exchange_neighbours(fields, plan, collective_id):
    sizes = tuple(lax.axis_size(name) for name in MESH_AXES)
    group_shapes = []
    landing_shapes = []
    for direction, (axis, dim) in enumerate(AXES):
        for field, first, count in plan[direction]:
            shape = (count,) + fields[field].shape[1:]
            group_shapes.append(shape)
            layer = shape[:1] + shape[2:] if dim == 1 else shape
            landing_shapes += [layer, layer]
    n_items = len(group_shapes)
    vmem = pl.BlockSpec(memory_space=pltpu.VMEM)
    out_shapes = []
    for shape in group_shapes:
        out_shapes += [jax.ShapeDtypeStruct(shape, jnp.float32)] * 2
    shifted = pl.pallas_call(
        functools.partial(_neighbour_kernel, sizes, plan, len(fields)),
        out_shape=tuple(out_shapes),
        in_specs=[vmem] * len(fields),
        out_specs=(vmem,) * len(out_shapes),
        scratch_shapes=[pltpu.VMEM(shape, jnp.float32) for shape in landing_shapes]
        + [pltpu.SemaphoreType.DMA((2 * n_items,)), pltpu.SemaphoreType.DMA((2 * n_items,))],
        compiler_params=pltpu.CompilerParams(collective_id=collective_id, has_side_effects=True),
    )(*fields)
    result = []
    item = 0
    for direction in range(3):
        pairs = []
        for _ in plan[direction]:
            pairs.append((shifted[2 * item], shifted[2 * item + 1]))
            item += 1
        result.append(pairs)
    return result


def _allreduce_kernel(stages, partial_ref, out_ref, acc, landing, send_sems, recv_sems):
    here = [lax.axis_index(name) for name in MESH_AXES]

    def member(name, stride, size, digit):
        position = MESH_AXES.index(name)
        own = lax.rem(here[position] // stride, size)
        coords = list(here)
        coords[position] = here[position] + (digit - own) * stride
        return tuple(coords), own

    barrier = pltpu.get_barrier_semaphore()
    partner_count = 0
    for name, stride, size in stages:
        for step in range(1, size):
            position = MESH_AXES.index(name)
            own = lax.rem(here[position] // stride, size)
            digit = lax.rem(own + step, size)
            peer, _ = member(name, stride, size, digit)
            pl.semaphore_signal(barrier, 1, device_id=peer, device_id_type=pl.DeviceIdType.MESH)
            partner_count += 1
    pl.semaphore_wait(barrier, partner_count)
    acc[...] = partial_ref[...]
    for stage, (name, stride, size) in enumerate(stages):
        position = MESH_AXES.index(name)
        own = lax.rem(here[position] // stride, size)
        landing[stage, own] = acc[...]
        sends = []
        receives = []
        for step in range(1, size):
            digit = lax.rem(own + step, size)
            peer, _ = member(name, stride, size, digit)
            copy = pltpu.make_async_remote_copy(
                src_ref=acc,
                dst_ref=landing.at[stage, own],
                send_sem=send_sems.at[stage, step],
                recv_sem=recv_sems.at[stage, own],
                device_id=peer,
                device_id_type=pl.DeviceIdType.MESH,
            )
            copy.start()
            sends.append(copy)
            receives.append(
                pltpu.make_async_remote_copy(
                    src_ref=acc,
                    dst_ref=landing.at[stage, digit],
                    send_sem=send_sems.at[stage, step],
                    recv_sem=recv_sems.at[stage, digit],
                    device_id=peer,
                    device_id_type=pl.DeviceIdType.MESH,
                )
            )
        for copy in sends:
            copy.wait_send()
        for copy in receives:
            copy.wait_recv()
        if size == 4:
            acc[...] = (landing[stage, 0] + landing[stage, 1]) + (
                landing[stage, 2] + landing[stage, 3]
            )
        else:
            acc[...] = landing[stage, 0] + landing[stage, 1]
    out_ref[...] = acc[...]


def _stages():
    stages = []
    for name in ("rep", "gy", "blk"):
        size = lax.axis_size(name)
        stride = 1
        while stride < size:
            group = 4 if size // stride >= 4 else 2
            stages.append((name, stride, group))
            stride *= group
    return stages


def _power_of_two(count):
    return count & (count - 1) == 0


def sum_everywhere(flat):
    if not all(_power_of_two(lax.axis_size(name)) for name in MESH_AXES):
        return lax.psum(flat, MESH_AXES)
    size = flat.shape[0]
    rows = -(-size // 1024) * 8
    block = jnp.pad(flat, (0, rows * 128 - size)).reshape(rows, 128)
    stages = _stages()
    vmem = pl.BlockSpec(memory_space=pltpu.VMEM)
    summed = pl.pallas_call(
        functools.partial(_allreduce_kernel, stages),
        out_shape=jax.ShapeDtypeStruct(block.shape, block.dtype),
        in_specs=[vmem],
        out_specs=vmem,
        scratch_shapes=[
            pltpu.VMEM(block.shape, block.dtype),
            pltpu.VMEM((len(stages), 4) + block.shape, block.dtype),
            pltpu.SemaphoreType.DMA((len(stages), 4)),
            pltpu.SemaphoreType.DMA((len(stages), 4)),
        ],
        compiler_params=pltpu.CompilerParams(collective_id=2, has_side_effects=True),
    )(block)
    return summed.reshape(-1)[:size]


def diffuse(field, field_nb, rates, rate_nb):
    summed = field
    for direction in range(3):
        rate_here = rates[2 * direction:2 * direction + 2]
        for side, offset in enumerate((1, -1)):
            summed = summed + 0.5 * (rate_here + rate_nb[direction][side]) * (
                field_nb[direction][side] - field
            )
    return summed


def rate_cotangent(state, state_nb, adjoint, adjoint_nb):
    pieces_list = []
    for direction in range(3):
        summed = jnp.zeros_like(state)
        for side, offset in enumerate((1, -1)):
            summed = summed + (state_nb[direction][side] - state) * (
                adjoint_nb[direction][side] - adjoint
            )
        pieces_list.append(-0.5 * summed)
    return jnp.concatenate(pieces_list, axis=0)


def embed_lookup(emb_table, grain_flat):
    table_rows = emb_table.shape[0]
    one_hot = (grain_flat[None, :] == lax.broadcasted_iota(jnp.int32, (table_rows, 1), 0)).astype(
        jnp.bfloat16
    )
    looked = jnp.dot(emb_table.T, one_hot, preferred_element_type=jnp.float32)
    return looked.astype(jnp.bfloat16)


def forward_layers(params, features):
    w_in, b_in, w_mid, b_mid, w_out, b_out = params
    act_one = jnp.tanh(
        jnp.dot(w_in, features, preferred_element_type=jnp.float32)
        + b_in.astype(jnp.float32)[:, None]
    )
    hid_one = act_one.astype(jnp.bfloat16)
    act_two = jnp.tanh(
        jnp.dot(w_mid, hid_one, preferred_element_type=jnp.float32)
        + b_mid.astype(jnp.float32)[:, None]
    )
    hid_two = act_two.astype(jnp.bfloat16)
    logits = (
        jnp.dot(w_out, hid_two, preferred_element_type=jnp.float32)
        + b_out.astype(jnp.float32)[:, None]
    )
    return (RATE_MAX * jax.nn.sigmoid(logits), act_one, hid_one, act_two, hid_two)


def backward_layers(params, rate_grad, forward_values):
    w_in, b_in, w_mid, b_mid, w_out, b_out = params
    rate_values, act_one, hid_one, act_two, hid_two = forward_values
    out_grad = (rate_grad * rate_values * (1.0 - rate_values / RATE_MAX)).astype(jnp.bfloat16)
    two_grad = (
        jnp.dot(w_out.T, out_grad, preferred_element_type=jnp.float32) * (1.0 - act_two * act_two)
    ).astype(jnp.bfloat16)
    one_grad = (
        jnp.dot(w_mid.T, two_grad, preferred_element_type=jnp.float32) * (1.0 - act_one * act_one)
    ).astype(jnp.bfloat16)
    state_grad = jnp.dot(w_in[:, -2:].T, one_grad, preferred_element_type=jnp.float32)
    return (out_grad, two_grad, one_grad), state_grad


def gradient_sums(grads, inputs):
    terms = []
    for grad_list, input_list in zip(grads, inputs):
        grad = jnp.concatenate(grad_list, axis=1)
        ones = jnp.ones((1, grad.shape[1]), jnp.bfloat16)
        layer_input = jnp.concatenate(input_list, axis=1)
        layer_input = jnp.concatenate([layer_input, ones], axis=0)
        both = jnp.dot(grad, layer_input.T, preferred_element_type=jnp.float32)
        terms += [both[:, :-1], both[:, -1]]
    return terms


def gather_params(w_in, b_in, w_mid, b_mid, w_out, b_out):
    n_in = w_in.shape[1]
    n_mid = w_mid.shape[1]
    packed = jnp.concatenate(
        [w_in, b_in[:, None], w_mid, b_mid[:, None], w_out.T], axis=1
    ).astype(jnp.bfloat16)
    full = lax.all_gather(packed, "rep", axis=0, tiled=True)
    col = 0
    w_in_b = full[:, col:col + n_in]
    col += n_in
    b_in_b = full[:, col]
    col += 1
    w_mid_b = full[:, col:col + n_mid]
    col += n_mid
    b_mid_b = full[:, col]
    col += 1
    w_out_b = full[:, col:].T
    order = jnp.array(RATE_ORDER)
    return (w_in_b, b_in_b, w_mid_b, b_mid_b, w_out_b[order], b_out.astype(jnp.bfloat16)[order])


def per_device(
    grain_id, init_masks, target_masks, emb_table, w_in, b_in, w_mid, b_mid, w_out, b_out
):
    params = gather_params(w_in, b_in, w_mid, b_mid, w_out, b_out)
    depth_cells, row_cells, col_cells = grain_id.shape
    cell_count = depth_cells * row_cells * col_cells
    block_shape = (depth_cells, row_cells, col_cells)
    embedding = embed_lookup(emb_table, grain_id.reshape(cell_count))
    state_now = init_masks.astype(jnp.float32)
    history = []
    forward_plan = [[(0, 0, 2), (1, 2 * d, 2)] for d in range(3)]
    for step_index in range(STEPS):
        features = jnp.concatenate(
            [embedding, state_now.reshape(2, cell_count).astype(jnp.bfloat16)], axis=0
        )
        rate_values = forward_layers(params, features)[0].reshape((6,) + block_shape)
        neighbours = exchange_neighbours([state_now, rate_values], forward_plan, 0)
        state_nb = [pairs[0] for pairs in neighbours]
        rate_nb = [pairs[1] for pairs in neighbours]
        history.append((state_now, state_nb, rate_values, rate_nb))
        state_now = diffuse(state_now, state_nb, rate_values, rate_nb)
    misfit = state_now - target_masks.astype(jnp.float32)
    total_cells = float(
        cell_count * lax.axis_size("blk") * lax.axis_size("gy") * lax.axis_size("rep")
    )
    loss_part = jnp.sum(misfit * misfit) / (4.0 * total_cells)
    adjoint = misfit / (2.0 * total_cells)
    grads = ([], [], [])
    inputs = ([], [], [])
    for step_index in reversed(range(STEPS)):
        state_t, state_nb, rate_values, rate_nb = history[step_index]
        adjoint_nb = [
            pairs[0] for pairs in exchange_neighbours([adjoint], [[(0, 0, 2)]] * 3, 1)
        ]
        rate_grad = rate_cotangent(state_t, state_nb, adjoint, adjoint_nb).reshape(
            6, cell_count
        )
        features = jnp.concatenate(
            [embedding, state_t.reshape(2, cell_count).astype(jnp.bfloat16)], axis=0
        )
        forward_values = forward_layers(params, features)
        step_grads, state_grad = backward_layers(params, rate_grad, forward_values)
        for index, (grad, layer_input) in enumerate(
            zip(reversed(step_grads), (features, forward_values[2], forward_values[4]))
        ):
            grads[index].append(grad)
            inputs[index].append(layer_input)
        adjoint = diffuse(adjoint, adjoint_nb, rate_values, rate_nb) + state_grad.reshape(
            (2,) + block_shape
        )
    grad_sums = gradient_sums(grads, inputs)
    start_sensitivity = adjoint * (2.0 * total_cells)
    pieces = list(grad_sums) + [loss_part[None]]
    flat = jnp.concatenate([piece.reshape(-1) for piece in pieces])
    summed_flat = sum_everywhere(flat)
    summed = []
    start = 0
    for piece in pieces:
        summed.append(summed_flat[start:start + piece.size].reshape(piece.shape))
        start += piece.size
    position = lax.axis_index("rep")
    share_width = w_in.shape[0]
    grad_w_in = lax.dynamic_slice_in_dim(summed[0], position * share_width, share_width, 0)
    grad_b_in = lax.dynamic_slice_in_dim(summed[1], position * share_width, share_width, 0)
    grad_w_mid = lax.dynamic_slice_in_dim(summed[2], position * share_width, share_width, 0)
    grad_b_mid = lax.dynamic_slice_in_dim(summed[3], position * share_width, share_width, 0)
    back = jnp.array([RATE_ORDER.index(channel) for channel in range(6)])
    grad_w_out = lax.dynamic_slice_in_dim(summed[4][back], position * share_width, share_width, 1)
    grad_b_out = summed[5][back]
    loss_total = summed[6][0]
    return (
        state_now,
        loss_total,
        grad_w_in,
        grad_b_in,
        grad_w_mid,
        grad_b_mid,
        grad_w_out,
        grad_b_out,
        start_sensitivity,
    )


def solution(mesh):
    in_specs = (
        P("blk", "gy", "rep"),
        P(None, "blk", "gy", "rep"),
        P(None, "blk", "gy", "rep"),
        P(),
        P("rep", None),
        P("rep"),
        P("rep", None),
        P("rep"),
        P(None, "rep"),
        P(),
    )
    out_specs = (
        P(None, "blk", "gy", "rep"),
        P(),
        P("rep", None),
        P("rep"),
        P("rep", None),
        P("rep"),
        P(None, "rep"),
        P(),
        P(None, "blk", "gy", "rep"),
    )
    return jax.shard_map(
        per_device, mesh=mesh, in_specs=in_specs, out_specs=out_specs, check_vma=False
    )
```

```python
import functools

import jax
import jax.numpy as jnp
from jax import lax
from jax.experimental import pallas as pl
from jax.experimental.pallas import tpu as pltpu
from jax.sharding import PartitionSpec as P

STEPS = 4


RATE_MAX = 0.15

AXES = (("rep", 3), ("gy", 2), ("blk", 1))
MESH_AXES = ("blk", "gy", "rep")
RATE_ORDER = (0, 3, 1, 4, 2, 5)


def _neighbour_kernel(sizes, plan, n_fields, *refs):
    fields = refs[:n_fields]
    n_items = sum(len(items) for items in plan)
    outs = refs[n_fields:n_fields + 2 * n_items]
    landing = refs[n_fields + 2 * n_items:n_fields + 4 * n_items]
    send_sems, recv_sems = refs[-2], refs[-1]
    here = [lax.axis_index(name) for name in MESH_AXES]

    def neighbour(axis, step):
        coords = list(here)
        position = MESH_AXES.index(axis)
        coords[position] = lax.rem(here[position] + step + sizes[position], sizes[position])
        return tuple(coords)

    targets = [(neighbour(axis, 1), neighbour(axis, -1)) for axis, dim in AXES]
    barrier = pltpu.get_barrier_semaphore()
    for plus, minus in targets:
        for peer in (plus, minus):
            pl.semaphore_signal(barrier, 1, device_id=peer, device_id_type=pl.DeviceIdType.MESH)
    pl.semaphore_wait(barrier, 6)
    copies = []
    item = 0
    for direction, (axis, dim) in enumerate(AXES):
        plus, minus = targets[direction]
        for field, first, count in plan[direction]:
            group = fields[field].at[first:first + count]
            depth = fields[field].shape[1]
            if dim == 1:
                to_plus, to_minus = group.at[:, depth - 1], group.at[:, 0]
            else:
                to_plus, to_minus = group, group
            for slot, source, peer in ((0, to_plus, plus), (1, to_minus, minus)):
                index = 2 * item + slot
                copy = pltpu.make_async_remote_copy(
                    src_ref=source,
                    dst_ref=landing[index],
                    send_sem=send_sems.at[index],
                    recv_sem=recv_sems.at[index],
                    device_id=peer,
                    device_id_type=pl.DeviceIdType.MESH,
                )
                copy.start()
                copies.append(copy)
            item += 1
    for copy in copies:
        copy.wait()
    item = 0
    for direction, (axis, dim) in enumerate(AXES):
        for field, first, count in plan[direction]:
            group = fields[field].at[first:first + count]
            from_below, from_above = landing[2 * item], landing[2 * item + 1]
            out_plus, out_minus = outs[2 * item], outs[2 * item + 1]
            if dim == 1:
                depth = group.shape[1]
                out_plus[:, 0:depth - 1] = group[:, 1:depth]
                out_plus[:, depth - 1] = from_above[...]
                out_minus[:, 1:depth] = group[:, 0:depth - 1]
                out_minus[:, 0] = from_below[...]
            else:
                values = group[...]
                size = values.shape[dim]
                index = lax.broadcasted_iota(jnp.int32, values.shape, dim)
                out_plus[...] = pltpu.roll(
                    jnp.where(index == 0, from_above[...], values), size - 1, dim
                )
                out_minus[...] = pltpu.roll(
                    jnp.where(index == size - 1, from_below[...], values), 1, dim
                )
            item += 1


def exchange_neighbours(fields, plan, collective_id):
    sizes = tuple(lax.axis_size(name) for name in MESH_AXES)
    group_shapes = []
    landing_shapes = []
    for direction, (axis, dim) in enumerate(AXES):
        for field, first, count in plan[direction]:
            shape = (count,) + fields[field].shape[1:]
            group_shapes.append(shape)
            layer = shape[:1] + shape[2:] if dim == 1 else shape
            landing_shapes += [layer, layer]
    n_items = len(group_shapes)
    vmem = pl.BlockSpec(memory_space=pltpu.VMEM)
    out_shapes = []
    for shape in group_shapes:
        out_shapes += [jax.ShapeDtypeStruct(shape, jnp.float32)] * 2
    shifted = pl.pallas_call(
        functools.partial(_neighbour_kernel, sizes, plan, len(fields)),
        out_shape=tuple(out_shapes),
        in_specs=[vmem] * len(fields),
        out_specs=(vmem,) * len(out_shapes),
        scratch_shapes=[pltpu.VMEM(shape, jnp.float32) for shape in landing_shapes]
        + [pltpu.SemaphoreType.DMA((2 * n_items,)), pltpu.SemaphoreType.DMA((2 * n_items,))],
        compiler_params=pltpu.CompilerParams(collective_id=collective_id, has_side_effects=True),
    )(*fields)
    result = []
    item = 0
    for direction in range(3):
        pairs = []
        for _ in plan[direction]:
            pairs.append((shifted[2 * item], shifted[2 * item + 1]))
            item += 1
        result.append(pairs)
    return result


def _allreduce_kernel(stages, partial_ref, out_ref, acc, landing, send_sems, recv_sems):
    here = [lax.axis_index(name) for name in MESH_AXES]

    def member(name, stride, size, digit):
        position = MESH_AXES.index(name)
        own = lax.rem(here[position] // stride, size)
        coords = list(here)
        coords[position] = here[position] + (digit - own) * stride
        return tuple(coords), own

    barrier = pltpu.get_barrier_semaphore()
    partner_count = 0
    for name, stride, size in stages:
        for step in range(1, size):
            position = MESH_AXES.index(name)
            own = lax.rem(here[position] // stride, size)
            digit = lax.rem(own + step, size)
            peer, _ = member(name, stride, size, digit)
            pl.semaphore_signal(barrier, 1, device_id=peer, device_id_type=pl.DeviceIdType.MESH)
            partner_count += 1
    pl.semaphore_wait(barrier, partner_count)
    acc[...] = partial_ref[...]
    for stage, (name, stride, size) in enumerate(stages):
        position = MESH_AXES.index(name)
        own = lax.rem(here[position] // stride, size)
        landing[stage, own] = acc[...]
        sends = []
        receives = []
        for step in range(1, size):
            digit = lax.rem(own + step, size)
            peer, _ = member(name, stride, size, digit)
            copy = pltpu.make_async_remote_copy(
                src_ref=acc,
                dst_ref=landing.at[stage, own],
                send_sem=send_sems.at[stage, step],
                recv_sem=recv_sems.at[stage, own],
                device_id=peer,
                device_id_type=pl.DeviceIdType.MESH,
            )
            copy.start()
            sends.append(copy)
            receives.append(
                pltpu.make_async_remote_copy(
                    src_ref=acc,
                    dst_ref=landing.at[stage, digit],
                    send_sem=send_sems.at[stage, step],
                    recv_sem=recv_sems.at[stage, digit],
                    device_id=peer,
                    device_id_type=pl.DeviceIdType.MESH,
                )
            )
        for copy in sends:
            copy.wait_send()
        for copy in receives:
            copy.wait_recv()
        if size == 4:
            acc[...] = (landing[stage, 0] + landing[stage, 1]) + (
                landing[stage, 2] + landing[stage, 3]
            )
        else:
            acc[...] = landing[stage, 0] + landing[stage, 1]
    out_ref[...] = acc[...]


def _stages():
    stages = []
    for name in ("rep", "gy", "blk"):
        size = lax.axis_size(name)
        stride = 1
        while stride < size:
            group = 4 if size // stride >= 4 else 2
            stages.append((name, stride, group))
            stride *= group
    return stages


def _power_of_two(count):
    return count & (count - 1) == 0


def sum_everywhere(block):
    if not all(_power_of_two(lax.axis_size(name)) for name in MESH_AXES):
        return lax.psum(block, MESH_AXES)
    stages = _stages()
    vmem = pl.BlockSpec(memory_space=pltpu.VMEM)
    summed = pl.pallas_call(
        functools.partial(_allreduce_kernel, stages),
        out_shape=jax.ShapeDtypeStruct(block.shape, block.dtype),
        in_specs=[vmem],
        out_specs=vmem,
        scratch_shapes=[
            pltpu.VMEM(block.shape, block.dtype),
            pltpu.VMEM((len(stages), 4) + block.shape, block.dtype),
            pltpu.SemaphoreType.DMA((len(stages), 4)),
            pltpu.SemaphoreType.DMA((len(stages), 4)),
        ],
        compiler_params=pltpu.CompilerParams(collective_id=2, has_side_effects=True),
    )(block)
    return summed


def diffuse(field, field_nb, rates, rate_nb):
    summed = field
    for direction in range(3):
        rate_here = rates[2 * direction:2 * direction + 2]
        for side, offset in enumerate((1, -1)):
            summed = summed + 0.5 * (rate_here + rate_nb[direction][side]) * (
                field_nb[direction][side] - field
            )
    return summed


def rate_cotangent(state, state_nb, adjoint, adjoint_nb):
    pieces_list = []
    for direction in range(3):
        summed = jnp.zeros_like(state)
        for side, offset in enumerate((1, -1)):
            summed = summed + (state_nb[direction][side] - state) * (
                adjoint_nb[direction][side] - adjoint
            )
        pieces_list.append(-0.5 * summed)
    return jnp.concatenate(pieces_list, axis=0)


def embed_lookup(emb_table, grain_flat):
    table_rows = emb_table.shape[0]
    one_hot = (grain_flat[None, :] == lax.broadcasted_iota(jnp.int32, (table_rows, 1), 0)).astype(
        jnp.bfloat16
    )
    looked = jnp.dot(emb_table.T, one_hot, preferred_element_type=jnp.float32)
    return looked.astype(jnp.bfloat16)


def forward_layers(params, features):
    w_in, b_in, w_mid, b_mid, w_out, b_out = params
    act_one = jnp.tanh(
        jnp.dot(w_in, features, preferred_element_type=jnp.float32)
        + b_in.astype(jnp.float32)[:, None]
    )
    hid_one = act_one.astype(jnp.bfloat16)
    act_two = jnp.tanh(
        jnp.dot(w_mid, hid_one, preferred_element_type=jnp.float32)
        + b_mid.astype(jnp.float32)[:, None]
    )
    hid_two = act_two.astype(jnp.bfloat16)
    logits = (
        jnp.dot(w_out, hid_two, preferred_element_type=jnp.float32)
        + b_out.astype(jnp.float32)[:, None]
    )
    return (RATE_MAX * jax.nn.sigmoid(logits), act_one, hid_one, act_two, hid_two)


def backward_layers(params, rate_grad, forward_values):
    w_in, b_in, w_mid, b_mid, w_out, b_out = params
    rate_values, act_one, hid_one, act_two, hid_two = forward_values
    out_grad = (rate_grad * rate_values * (1.0 - rate_values / RATE_MAX)).astype(jnp.bfloat16)
    two_grad = (
        jnp.dot(w_out.T, out_grad, preferred_element_type=jnp.float32) * (1.0 - act_two * act_two)
    ).astype(jnp.bfloat16)
    one_grad = (
        jnp.dot(w_mid.T, two_grad, preferred_element_type=jnp.float32) * (1.0 - act_one * act_one)
    ).astype(jnp.bfloat16)
    state_grad = jnp.dot(w_in[:, -2:].T, one_grad, preferred_element_type=jnp.float32)
    return (out_grad, two_grad, one_grad), state_grad


def gradient_sums(grads, inputs):
    terms = []
    for grad_list, input_list in zip(grads, inputs):
        grad = jnp.concatenate(grad_list, axis=1)
        ones = jnp.ones((1, grad.shape[1]), jnp.bfloat16)
        layer_input = jnp.concatenate(input_list, axis=1)
        layer_input = jnp.concatenate([layer_input, ones], axis=0)
        terms.append(jnp.dot(grad, layer_input.T, preferred_element_type=jnp.float32))
    return terms


def gather_params(w_in, b_in, w_mid, b_mid, w_out, b_out):
    n_in = w_in.shape[1]
    n_mid = w_mid.shape[1]
    packed = jnp.concatenate(
        [w_in, b_in[:, None], w_mid, b_mid[:, None], w_out.T], axis=1
    ).astype(jnp.bfloat16)
    full = lax.all_gather(packed, "rep", axis=0, tiled=True)
    col = 0
    w_in_b = full[:, col:col + n_in]
    col += n_in
    b_in_b = full[:, col]
    col += 1
    w_mid_b = full[:, col:col + n_mid]
    col += n_mid
    b_mid_b = full[:, col]
    col += 1
    w_out_b = full[:, col:].T
    order = jnp.array(RATE_ORDER)
    return (w_in_b, b_in_b, w_mid_b, b_mid_b, w_out_b[order], b_out.astype(jnp.bfloat16)[order])


def per_device(
    grain_id, init_masks, target_masks, emb_table, w_in, b_in, w_mid, b_mid, w_out, b_out
):
    params = gather_params(w_in, b_in, w_mid, b_mid, w_out, b_out)
    depth_cells, row_cells, col_cells = grain_id.shape
    cell_count = depth_cells * row_cells * col_cells
    block_shape = (depth_cells, row_cells, col_cells)
    embedding = embed_lookup(emb_table, grain_id.reshape(cell_count))
    state_now = init_masks.astype(jnp.float32)
    history = []
    forward_plan = [[(0, 0, 2), (1, 2 * d, 2)] for d in range(3)]
    for step_index in range(STEPS):
        features = jnp.concatenate(
            [embedding, state_now.reshape(2, cell_count).astype(jnp.bfloat16)], axis=0
        )
        rate_values = forward_layers(params, features)[0].reshape((6,) + block_shape)
        neighbours = exchange_neighbours([state_now, rate_values], forward_plan, 0)
        state_nb = [pairs[0] for pairs in neighbours]
        rate_nb = [pairs[1] for pairs in neighbours]
        history.append((state_now, state_nb, rate_values, rate_nb))
        state_now = diffuse(state_now, state_nb, rate_values, rate_nb)
    misfit = state_now - target_masks.astype(jnp.float32)
    total_cells = float(
        cell_count * lax.axis_size("blk") * lax.axis_size("gy") * lax.axis_size("rep")
    )
    loss_part = jnp.sum(misfit * misfit) / (4.0 * total_cells)
    adjoint = misfit / (2.0 * total_cells)
    grads = ([], [], [])
    inputs = ([], [], [])
    for step_index in reversed(range(STEPS)):
        state_t, state_nb, rate_values, rate_nb = history[step_index]
        adjoint_nb = [
            pairs[0] for pairs in exchange_neighbours([adjoint], [[(0, 0, 2)]] * 3, 1)
        ]
        rate_grad = rate_cotangent(state_t, state_nb, adjoint, adjoint_nb).reshape(
            6, cell_count
        )
        features = jnp.concatenate(
            [embedding, state_t.reshape(2, cell_count).astype(jnp.bfloat16)], axis=0
        )
        forward_values = forward_layers(params, features)
        step_grads, state_grad = backward_layers(params, rate_grad, forward_values)
        for index, (grad, layer_input) in enumerate(
            zip(reversed(step_grads), (features, forward_values[2], forward_values[4]))
        ):
            grads[index].append(grad)
            inputs[index].append(layer_input)
        adjoint = diffuse(adjoint, adjoint_nb, rate_values, rate_nb) + state_grad.reshape(
            (2,) + block_shape
        )
    grad_sums = gradient_sums(grads, inputs)
    start_sensitivity = adjoint * (2.0 * total_cells)
    in_both, mid_both, out_both = grad_sums
    back = jnp.array([RATE_ORDER.index(channel) for channel in range(6)])
    out_both = out_both[back]
    units = in_both.shape[0]
    per_unit = jnp.concatenate([in_both, mid_both, out_both[:, :-1].T], axis=1)
    width = per_unit.shape[1]
    last = jnp.concatenate([out_both[:, -1], loss_part[None]])
    rows = -(-(units + 1) // 8) * 8
    packed = jnp.zeros((rows, 128), jnp.float32)
    packed = packed.at[:units, :width].set(per_unit)
    packed = packed.at[units, :last.shape[0]].set(last)
    summed = sum_everywhere(packed)
    share_width = w_in.shape[0]
    position = lax.axis_index("rep")
    mine = lax.dynamic_slice_in_dim(summed, position * share_width, share_width, 0)
    n_in = w_in.shape[1]
    n_mid = w_mid.shape[1]
    grad_w_in = mine[:, :n_in]
    grad_b_in = mine[:, n_in]
    grad_w_mid = mine[:, n_in + 1:n_in + 1 + n_mid]
    grad_b_mid = mine[:, n_in + 1 + n_mid]
    grad_w_out = mine[:, n_in + 2 + n_mid:width].T
    grad_b_out = summed[units, :6]
    loss_total = summed[units, 6]
    return (
        state_now,
        loss_total,
        grad_w_in,
        grad_b_in,
        grad_w_mid,
        grad_b_mid,
        grad_w_out,
        grad_b_out,
        start_sensitivity,
    )


def solution(mesh):
    in_specs = (
        P("blk", "gy", "rep"),
        P(None, "blk", "gy", "rep"),
        P(None, "blk", "gy", "rep"),
        P(),
        P("rep", None),
        P("rep"),
        P("rep", None),
        P("rep"),
        P(None, "rep"),
        P(),
    )
    out_specs = (
        P(None, "blk", "gy", "rep"),
        P(),
        P("rep", None),
        P("rep"),
        P("rep", None),
        P("rep"),
        P(None, "rep"),
        P(),
        P(None, "blk", "gy", "rep"),
    )
    return jax.shard_map(
        per_device, mesh=mesh, in_specs=in_specs, out_specs=out_specs, check_vma=False
    )
```

```python
import functools

import jax
import jax.numpy as jnp
from jax import lax
from jax.experimental import pallas as pl
from jax.experimental.pallas import tpu as pltpu
from jax.sharding import PartitionSpec as P

STEPS = 4


RATE_MAX = 0.15

AXES = (("rep", 3), ("gy", 2), ("blk", 1))
MESH_AXES = ("blk", "gy", "rep")
RATE_ORDER = (0, 3, 1, 4, 2, 5)


def _neighbour_kernel(sizes, plan, n_fields, *refs):
    fields = refs[:n_fields]
    n_items = sum(len(items) for items in plan)
    outs = refs[n_fields:n_fields + 2 * n_items]
    landing = refs[n_fields + 2 * n_items:n_fields + 4 * n_items]
    send_sems, recv_sems = refs[-2], refs[-1]
    here = [lax.axis_index(name) for name in MESH_AXES]

    def neighbour(axis, step):
        coords = list(here)
        position = MESH_AXES.index(axis)
        coords[position] = lax.rem(here[position] + step + sizes[position], sizes[position])
        return tuple(coords)

    targets = [(neighbour(axis, 1), neighbour(axis, -1)) for axis, dim in AXES]
    barrier = pltpu.get_barrier_semaphore()
    for plus, minus in targets:
        for peer in (plus, minus):
            pl.semaphore_signal(barrier, 1, device_id=peer, device_id_type=pl.DeviceIdType.MESH)
    pl.semaphore_wait(barrier, 6)
    copies = []
    item = 0
    for direction, (axis, dim) in enumerate(AXES):
        plus, minus = targets[direction]
        for field, first, count in plan[direction]:
            group = fields[field].at[first:first + count]
            depth = fields[field].shape[1]
            if dim == 1:
                to_plus, to_minus = group.at[:, depth - 1], group.at[:, 0]
            else:
                to_plus, to_minus = group, group
            for slot, source, peer in ((0, to_plus, plus), (1, to_minus, minus)):
                index = 2 * item + slot
                copy = pltpu.make_async_remote_copy(
                    src_ref=source,
                    dst_ref=landing[index],
                    send_sem=send_sems.at[index],
                    recv_sem=recv_sems.at[index],
                    device_id=peer,
                    device_id_type=pl.DeviceIdType.MESH,
                )
                copy.start()
                copies.append(copy)
            item += 1
    for copy in copies:
        copy.wait()
    item = 0
    for direction, (axis, dim) in enumerate(AXES):
        for field, first, count in plan[direction]:
            group = fields[field].at[first:first + count]
            from_below, from_above = landing[2 * item], landing[2 * item + 1]
            out_plus, out_minus = outs[2 * item], outs[2 * item + 1]
            if dim == 1:
                depth = group.shape[1]
                out_plus[:, 0:depth - 1] = group[:, 1:depth]
                out_plus[:, depth - 1] = from_above[...]
                out_minus[:, 1:depth] = group[:, 0:depth - 1]
                out_minus[:, 0] = from_below[...]
            else:
                values = group[...]
                size = values.shape[dim]
                index = lax.broadcasted_iota(jnp.int32, values.shape, dim)
                out_plus[...] = pltpu.roll(
                    jnp.where(index == 0, from_above[...], values), size - 1, dim
                )
                out_minus[...] = pltpu.roll(
                    jnp.where(index == size - 1, from_below[...], values), 1, dim
                )
            item += 1


def exchange_neighbours(fields, plan, collective_id):
    sizes = tuple(lax.axis_size(name) for name in MESH_AXES)
    group_shapes = []
    landing_shapes = []
    for direction, (axis, dim) in enumerate(AXES):
        for field, first, count in plan[direction]:
            shape = (count,) + fields[field].shape[1:]
            group_shapes.append(shape)
            layer = shape[:1] + shape[2:] if dim == 1 else shape
            landing_shapes += [layer, layer]
    n_items = len(group_shapes)
    vmem = pl.BlockSpec(memory_space=pltpu.VMEM)
    out_shapes = []
    for shape in group_shapes:
        out_shapes += [jax.ShapeDtypeStruct(shape, jnp.float32)] * 2
    shifted = pl.pallas_call(
        functools.partial(_neighbour_kernel, sizes, plan, len(fields)),
        out_shape=tuple(out_shapes),
        in_specs=[vmem] * len(fields),
        out_specs=(vmem,) * len(out_shapes),
        scratch_shapes=[pltpu.VMEM(shape, jnp.float32) for shape in landing_shapes]
        + [pltpu.SemaphoreType.DMA((2 * n_items,)), pltpu.SemaphoreType.DMA((2 * n_items,))],
        compiler_params=pltpu.CompilerParams(collective_id=collective_id, has_side_effects=True),
    )(*fields)
    result = []
    item = 0
    for direction in range(3):
        pairs = []
        for _ in plan[direction]:
            pairs.append((shifted[2 * item], shifted[2 * item + 1]))
            item += 1
        result.append(pairs)
    return result


def _allreduce_kernel(stages, partial_ref, out_ref, acc, landing, send_sems, recv_sems):
    here = [lax.axis_index(name) for name in MESH_AXES]

    def member(name, stride, size, digit):
        position = MESH_AXES.index(name)
        own = lax.rem(here[position] // stride, size)
        coords = list(here)
        coords[position] = here[position] + (digit - own) * stride
        return tuple(coords), own

    barrier = pltpu.get_barrier_semaphore()
    partner_count = 0
    for name, stride, size in stages:
        for step in range(1, size):
            position = MESH_AXES.index(name)
            own = lax.rem(here[position] // stride, size)
            digit = lax.rem(own + step, size)
            peer, _ = member(name, stride, size, digit)
            pl.semaphore_signal(barrier, 1, device_id=peer, device_id_type=pl.DeviceIdType.MESH)
            partner_count += 1
    pl.semaphore_wait(barrier, partner_count)
    acc[...] = partial_ref[...]
    for stage, (name, stride, size) in enumerate(stages):
        position = MESH_AXES.index(name)
        own = lax.rem(here[position] // stride, size)
        landing[stage, own] = acc[...]
        sends = []
        receives = []
        for step in range(1, size):
            digit = lax.rem(own + step, size)
            peer, _ = member(name, stride, size, digit)
            copy = pltpu.make_async_remote_copy(
                src_ref=acc,
                dst_ref=landing.at[stage, own],
                send_sem=send_sems.at[stage, step],
                recv_sem=recv_sems.at[stage, own],
                device_id=peer,
                device_id_type=pl.DeviceIdType.MESH,
            )
            copy.start()
            sends.append(copy)
            receives.append(
                pltpu.make_async_remote_copy(
                    src_ref=acc,
                    dst_ref=landing.at[stage, digit],
                    send_sem=send_sems.at[stage, step],
                    recv_sem=recv_sems.at[stage, digit],
                    device_id=peer,
                    device_id_type=pl.DeviceIdType.MESH,
                )
            )
        for copy in sends:
            copy.wait_send()
        for copy in receives:
            copy.wait_recv()
        if size == 4:
            acc[...] = (landing[stage, 0] + landing[stage, 1]) + (
                landing[stage, 2] + landing[stage, 3]
            )
        else:
            acc[...] = landing[stage, 0] + landing[stage, 1]
    out_ref[...] = acc[...]


def _stages():
    stages = []
    for name in ("rep", "gy", "blk"):
        size = lax.axis_size(name)
        stride = 1
        while stride < size:
            group = 4 if size // stride >= 4 else 2
            stages.append((name, stride, group))
            stride *= group
    return stages


def _gather_kernel(size, part_ref, out_ref, landing, send_sems, recv_sems):
    here = [lax.axis_index(name) for name in MESH_AXES]
    position = MESH_AXES.index("rep")
    own = here[position]

    def member(step):
        coords = list(here)
        coords[position] = lax.rem(own + step, size)
        return tuple(coords)

    barrier = pltpu.get_barrier_semaphore()
    for step in range(1, size):
        pl.semaphore_signal(barrier, 1, device_id=member(step), device_id_type=pl.DeviceIdType.MESH)
    pl.semaphore_wait(barrier, size - 1)
    sends = []
    receives = []
    for step in range(1, size):
        source = lax.rem(own + size - step, size)
        copy = pltpu.make_async_remote_copy(
            src_ref=part_ref,
            dst_ref=landing.at[own],
            send_sem=send_sems.at[step],
            recv_sem=recv_sems.at[own],
            device_id=member(step),
            device_id_type=pl.DeviceIdType.MESH,
        )
        copy.start()
        sends.append(copy)
        receives.append(
            pltpu.make_async_remote_copy(
                src_ref=part_ref,
                dst_ref=landing.at[source],
                send_sem=send_sems.at[step],
                recv_sem=recv_sems.at[source],
                device_id=member(step),
                device_id_type=pl.DeviceIdType.MESH,
            )
        )
    landing[own] = part_ref[...]
    for copy in sends:
        copy.wait_send()
    for copy in receives:
        copy.wait_recv()
    out_ref[...] = landing[...]


def gather_rep(part):
    size = lax.axis_size("rep")
    if size == 1:
        return part
    vmem = pl.BlockSpec(memory_space=pltpu.VMEM)
    gathered = pl.pallas_call(
        functools.partial(_gather_kernel, size),
        out_shape=jax.ShapeDtypeStruct((size,) + part.shape, part.dtype),
        in_specs=[vmem],
        out_specs=vmem,
        scratch_shapes=[
            pltpu.VMEM((size,) + part.shape, part.dtype),
            pltpu.SemaphoreType.DMA((size,)),
            pltpu.SemaphoreType.DMA((size,)),
        ],
        compiler_params=pltpu.CompilerParams(collective_id=3, has_side_effects=True),
    )(part)
    return gathered.reshape((size * part.shape[0],) + part.shape[1:])


def _power_of_two(count):
    return count & (count - 1) == 0


def sum_everywhere(block):
    if not all(_power_of_two(lax.axis_size(name)) for name in MESH_AXES):
        return lax.psum(block, MESH_AXES)
    stages = _stages()
    vmem = pl.BlockSpec(memory_space=pltpu.VMEM)
    summed = pl.pallas_call(
        functools.partial(_allreduce_kernel, stages),
        out_shape=jax.ShapeDtypeStruct(block.shape, block.dtype),
        in_specs=[vmem],
        out_specs=vmem,
        scratch_shapes=[
            pltpu.VMEM(block.shape, block.dtype),
            pltpu.VMEM((len(stages), 4) + block.shape, block.dtype),
            pltpu.SemaphoreType.DMA((len(stages), 4)),
            pltpu.SemaphoreType.DMA((len(stages), 4)),
        ],
        compiler_params=pltpu.CompilerParams(collective_id=2, has_side_effects=True),
    )(block)
    return summed


def diffuse(field, field_nb, rates, rate_nb):
    summed = field
    for direction in range(3):
        rate_here = rates[2 * direction:2 * direction + 2]
        for side, offset in enumerate((1, -1)):
            summed = summed + 0.5 * (rate_here + rate_nb[direction][side]) * (
                field_nb[direction][side] - field
            )
    return summed


def rate_cotangent(state, state_nb, adjoint, adjoint_nb):
    pieces_list = []
    for direction in range(3):
        summed = jnp.zeros_like(state)
        for side, offset in enumerate((1, -1)):
            summed = summed + (state_nb[direction][side] - state) * (
                adjoint_nb[direction][side] - adjoint
            )
        pieces_list.append(-0.5 * summed)
    return jnp.concatenate(pieces_list, axis=0)


def embed_lookup(emb_table, grain_flat):
    table_rows = emb_table.shape[0]
    one_hot = (grain_flat[None, :] == lax.broadcasted_iota(jnp.int32, (table_rows, 1), 0)).astype(
        jnp.bfloat16
    )
    looked = jnp.dot(emb_table.T, one_hot, preferred_element_type=jnp.float32)
    return looked.astype(jnp.bfloat16)


def forward_layers(params, features):
    w_in, b_in, w_mid, b_mid, w_out, b_out = params
    act_one = jnp.tanh(
        jnp.dot(w_in, features, preferred_element_type=jnp.float32)
        + b_in.astype(jnp.float32)[:, None]
    )
    hid_one = act_one.astype(jnp.bfloat16)
    act_two = jnp.tanh(
        jnp.dot(w_mid, hid_one, preferred_element_type=jnp.float32)
        + b_mid.astype(jnp.float32)[:, None]
    )
    hid_two = act_two.astype(jnp.bfloat16)
    logits = (
        jnp.dot(w_out, hid_two, preferred_element_type=jnp.float32)
        + b_out.astype(jnp.float32)[:, None]
    )
    return (RATE_MAX * jax.nn.sigmoid(logits), act_one, hid_one, act_two, hid_two)


def backward_layers(params, rate_grad, forward_values):
    w_in, b_in, w_mid, b_mid, w_out, b_out = params
    rate_values, act_one, hid_one, act_two, hid_two = forward_values
    out_grad = (rate_grad * rate_values * (1.0 - rate_values / RATE_MAX)).astype(jnp.bfloat16)
    two_grad = (
        jnp.dot(w_out.T, out_grad, preferred_element_type=jnp.float32) * (1.0 - act_two * act_two)
    ).astype(jnp.bfloat16)
    one_grad = (
        jnp.dot(w_mid.T, two_grad, preferred_element_type=jnp.float32) * (1.0 - act_one * act_one)
    ).astype(jnp.bfloat16)
    state_grad = jnp.dot(w_in[:, -2:].T, one_grad, preferred_element_type=jnp.float32)
    return (out_grad, two_grad, one_grad), state_grad


def gradient_sums(grads, inputs):
    terms = []
    for grad_list, input_list in zip(grads, inputs):
        grad = jnp.concatenate(grad_list, axis=1)
        ones = jnp.ones((1, grad.shape[1]), jnp.bfloat16)
        layer_input = jnp.concatenate(input_list, axis=1)
        layer_input = jnp.concatenate([layer_input, ones], axis=0)
        terms.append(jnp.dot(grad, layer_input.T, preferred_element_type=jnp.float32))
    return terms


def gather_params(w_in, b_in, w_mid, b_mid, w_out, b_out):
    n_in = w_in.shape[1]
    n_mid = w_mid.shape[1]
    packed = jnp.concatenate(
        [w_in, b_in[:, None], w_mid, b_mid[:, None], w_out.T], axis=1
    ).astype(jnp.bfloat16)
    packed = jnp.pad(packed, ((0, 0), (0, -packed.shape[1] % 128)))
    full = gather_rep(packed)
    col = 0
    w_in_b = full[:, col:col + n_in]
    col += n_in
    b_in_b = full[:, col]
    col += 1
    w_mid_b = full[:, col:col + n_mid]
    col += n_mid
    b_mid_b = full[:, col]
    col += 1
    w_out_b = full[:, col:col + w_out.shape[0]].T
    order = jnp.array(RATE_ORDER)
    return (w_in_b, b_in_b, w_mid_b, b_mid_b, w_out_b[order], b_out.astype(jnp.bfloat16)[order])


def per_device(
    grain_id, init_masks, target_masks, emb_table, w_in, b_in, w_mid, b_mid, w_out, b_out
):
    params = gather_params(w_in, b_in, w_mid, b_mid, w_out, b_out)
    depth_cells, row_cells, col_cells = grain_id.shape
    cell_count = depth_cells * row_cells * col_cells
    block_shape = (depth_cells, row_cells, col_cells)
    embedding = embed_lookup(emb_table, grain_id.reshape(cell_count))
    state_now = init_masks.astype(jnp.float32)
    history = []
    forward_plan = [[(0, 0, 2), (1, 2 * d, 2)] for d in range(3)]
    for step_index in range(STEPS):
        features = jnp.concatenate(
            [embedding, state_now.reshape(2, cell_count).astype(jnp.bfloat16)], axis=0
        )
        rate_values = forward_layers(params, features)[0].reshape((6,) + block_shape)
        neighbours = exchange_neighbours([state_now, rate_values], forward_plan, 0)
        state_nb = [pairs[0] for pairs in neighbours]
        rate_nb = [pairs[1] for pairs in neighbours]
        history.append((state_now, state_nb, rate_values, rate_nb))
        state_now = diffuse(state_now, state_nb, rate_values, rate_nb)
    misfit = state_now - target_masks.astype(jnp.float32)
    total_cells = float(
        cell_count * lax.axis_size("blk") * lax.axis_size("gy") * lax.axis_size("rep")
    )
    loss_part = jnp.sum(misfit * misfit) / (4.0 * total_cells)
    adjoint = misfit / (2.0 * total_cells)
    grads = ([], [], [])
    inputs = ([], [], [])
    for step_index in reversed(range(STEPS)):
        state_t, state_nb, rate_values, rate_nb = history[step_index]
        adjoint_nb = [
            pairs[0] for pairs in exchange_neighbours([adjoint], [[(0, 0, 2)]] * 3, 1)
        ]
        rate_grad = rate_cotangent(state_t, state_nb, adjoint, adjoint_nb).reshape(
            6, cell_count
        )
        features = jnp.concatenate(
            [embedding, state_t.reshape(2, cell_count).astype(jnp.bfloat16)], axis=0
        )
        forward_values = forward_layers(params, features)
        step_grads, state_grad = backward_layers(params, rate_grad, forward_values)
        for index, (grad, layer_input) in enumerate(
            zip(reversed(step_grads), (features, forward_values[2], forward_values[4]))
        ):
            grads[index].append(grad)
            inputs[index].append(layer_input)
        adjoint = diffuse(adjoint, adjoint_nb, rate_values, rate_nb) + state_grad.reshape(
            (2,) + block_shape
        )
    grad_sums = gradient_sums(grads, inputs)
    start_sensitivity = adjoint * (2.0 * total_cells)
    in_both, mid_both, out_both = grad_sums
    back = jnp.array([RATE_ORDER.index(channel) for channel in range(6)])
    out_both = out_both[back]
    units = in_both.shape[0]
    per_unit = jnp.concatenate([in_both, mid_both, out_both[:, :-1].T], axis=1)
    width = per_unit.shape[1]
    last = jnp.concatenate([out_both[:, -1], loss_part[None]])
    rows = -(-(units + 1) // 8) * 8
    packed = jnp.zeros((rows, 128), jnp.float32)
    packed = packed.at[:units, :width].set(per_unit)
    packed = packed.at[units, :last.shape[0]].set(last)
    summed = sum_everywhere(packed)
    share_width = w_in.shape[0]
    position = lax.axis_index("rep")
    mine = lax.dynamic_slice_in_dim(summed, position * share_width, share_width, 0)
    n_in = w_in.shape[1]
    n_mid = w_mid.shape[1]
    grad_w_in = mine[:, :n_in]
    grad_b_in = mine[:, n_in]
    grad_w_mid = mine[:, n_in + 1:n_in + 1 + n_mid]
    grad_b_mid = mine[:, n_in + 1 + n_mid]
    grad_w_out = mine[:, n_in + 2 + n_mid:width].T
    grad_b_out = summed[units, :6]
    loss_total = summed[units, 6]
    return (
        state_now,
        loss_total,
        grad_w_in,
        grad_b_in,
        grad_w_mid,
        grad_b_mid,
        grad_w_out,
        grad_b_out,
        start_sensitivity,
    )


def solution(mesh):
    in_specs = (
        P("blk", "gy", "rep"),
        P(None, "blk", "gy", "rep"),
        P(None, "blk", "gy", "rep"),
        P(),
        P("rep", None),
        P("rep"),
        P("rep", None),
        P("rep"),
        P(None, "rep"),
        P(),
    )
    out_specs = (
        P(None, "blk", "gy", "rep"),
        P(),
        P("rep", None),
        P("rep"),
        P("rep", None),
        P("rep"),
        P(None, "rep"),
        P(),
        P(None, "blk", "gy", "rep"),
    )
    return jax.shard_map(
        per_device, mesh=mesh, in_specs=in_specs, out_specs=out_specs, check_vma=False
    )
```

```python
import functools

import jax
import jax.numpy as jnp
from jax import lax
from jax.experimental import pallas as pl
from jax.experimental.pallas import tpu as pltpu
from jax.sharding import PartitionSpec as P

STEPS = 4


RATE_MAX = 0.15

AXES = (("rep", 3), ("gy", 2), ("blk", 1))
MESH_AXES = ("blk", "gy", "rep")
RATE_ORDER = (0, 3, 1, 4, 2, 5)


def _neighbour_kernel(sizes, plan, n_fields, *refs):
    fields = refs[:n_fields]
    n_items = sum(len(items) for items in plan)
    outs = refs[n_fields:n_fields + 2 * n_items]
    landing = refs[n_fields + 2 * n_items:n_fields + 4 * n_items]
    send_sems, recv_sems = refs[-2], refs[-1]
    here = [lax.axis_index(name) for name in MESH_AXES]

    def neighbour(axis, step):
        coords = list(here)
        position = MESH_AXES.index(axis)
        coords[position] = lax.rem(here[position] + step + sizes[position], sizes[position])
        return tuple(coords)

    targets = [(neighbour(axis, 1), neighbour(axis, -1)) for axis, dim in AXES]
    barrier = pltpu.get_barrier_semaphore()
    for plus, minus in targets:
        for peer in (plus, minus):
            pl.semaphore_signal(barrier, 1, device_id=peer, device_id_type=pl.DeviceIdType.MESH)
    pl.semaphore_wait(barrier, 6)
    copies = []
    item = 0
    for direction, (axis, dim) in enumerate(AXES):
        plus, minus = targets[direction]
        for field, first, count in plan[direction]:
            group = fields[field].at[first:first + count]
            depth = fields[field].shape[1]
            if dim == 1:
                to_plus, to_minus = group.at[:, depth - 1], group.at[:, 0]
            else:
                to_plus, to_minus = group, group
            for slot, source, peer in ((0, to_plus, plus), (1, to_minus, minus)):
                index = 2 * item + slot
                copy = pltpu.make_async_remote_copy(
                    src_ref=source,
                    dst_ref=landing[index],
                    send_sem=send_sems.at[index],
                    recv_sem=recv_sems.at[index],
                    device_id=peer,
                    device_id_type=pl.DeviceIdType.MESH,
                )
                copy.start()
                copies.append(copy)
            item += 1
    for copy in copies:
        copy.wait()
    item = 0
    for direction, (axis, dim) in enumerate(AXES):
        for field, first, count in plan[direction]:
            group = fields[field].at[first:first + count]
            from_below, from_above = landing[2 * item], landing[2 * item + 1]
            out_plus, out_minus = outs[2 * item], outs[2 * item + 1]
            if dim == 1:
                depth = group.shape[1]
                out_plus[:, 0:depth - 1] = group[:, 1:depth]
                out_plus[:, depth - 1] = from_above[...]
                out_minus[:, 1:depth] = group[:, 0:depth - 1]
                out_minus[:, 0] = from_below[...]
            else:
                values = group[...]
                size = values.shape[dim]
                index = lax.broadcasted_iota(jnp.int32, values.shape, dim)
                out_plus[...] = pltpu.roll(
                    jnp.where(index == 0, from_above[...], values), size - 1, dim
                )
                out_minus[...] = pltpu.roll(
                    jnp.where(index == size - 1, from_below[...], values), 1, dim
                )
            item += 1


def exchange_neighbours(fields, plan, collective_id):
    sizes = tuple(lax.axis_size(name) for name in MESH_AXES)
    group_shapes = []
    landing_shapes = []
    for direction, (axis, dim) in enumerate(AXES):
        for field, first, count in plan[direction]:
            shape = (count,) + fields[field].shape[1:]
            group_shapes.append(shape)
            layer = shape[:1] + shape[2:] if dim == 1 else shape
            landing_shapes += [layer, layer]
    n_items = len(group_shapes)
    vmem = pl.BlockSpec(memory_space=pltpu.VMEM)
    out_shapes = []
    for shape in group_shapes:
        out_shapes += [jax.ShapeDtypeStruct(shape, jnp.float32)] * 2
    shifted = pl.pallas_call(
        functools.partial(_neighbour_kernel, sizes, plan, len(fields)),
        out_shape=tuple(out_shapes),
        in_specs=[vmem] * len(fields),
        out_specs=(vmem,) * len(out_shapes),
        scratch_shapes=[pltpu.VMEM(shape, jnp.float32) for shape in landing_shapes]
        + [pltpu.SemaphoreType.DMA((2 * n_items,)), pltpu.SemaphoreType.DMA((2 * n_items,))],
        compiler_params=pltpu.CompilerParams(collective_id=collective_id, has_side_effects=True),
    )(*fields)
    result = []
    item = 0
    for direction in range(3):
        pairs = []
        for _ in plan[direction]:
            pairs.append((shifted[2 * item], shifted[2 * item + 1]))
            item += 1
        result.append(pairs)
    return result


def _allreduce_kernel(stages, partial_ref, mine_ref, last_ref, acc, landing, send_sems, recv_sems):
    here = [lax.axis_index(name) for name in MESH_AXES]

    def member(name, stride, size, digit):
        position = MESH_AXES.index(name)
        own = lax.rem(here[position] // stride, size)
        coords = list(here)
        coords[position] = here[position] + (digit - own) * stride
        return tuple(coords), own

    barrier = pltpu.get_barrier_semaphore()
    partner_count = 0
    for name, stride, size in stages:
        for step in range(1, size):
            position = MESH_AXES.index(name)
            own = lax.rem(here[position] // stride, size)
            digit = lax.rem(own + step, size)
            peer, _ = member(name, stride, size, digit)
            pl.semaphore_signal(barrier, 1, device_id=peer, device_id_type=pl.DeviceIdType.MESH)
            partner_count += 1
    pl.semaphore_wait(barrier, partner_count)
    acc[...] = partial_ref[...]
    for stage, (name, stride, size) in enumerate(stages):
        position = MESH_AXES.index(name)
        own = lax.rem(here[position] // stride, size)
        landing[stage, own] = acc[...]
        sends = []
        receives = []
        for step in range(1, size):
            digit = lax.rem(own + step, size)
            peer, _ = member(name, stride, size, digit)
            copy = pltpu.make_async_remote_copy(
                src_ref=acc,
                dst_ref=landing.at[stage, own],
                send_sem=send_sems.at[stage, step],
                recv_sem=recv_sems.at[stage, own],
                device_id=peer,
                device_id_type=pl.DeviceIdType.MESH,
            )
            copy.start()
            sends.append(copy)
            receives.append(
                pltpu.make_async_remote_copy(
                    src_ref=acc,
                    dst_ref=landing.at[stage, digit],
                    send_sem=send_sems.at[stage, step],
                    recv_sem=recv_sems.at[stage, digit],
                    device_id=peer,
                    device_id_type=pl.DeviceIdType.MESH,
                )
            )
        for copy in sends:
            copy.wait_send()
        for copy in receives:
            copy.wait_recv()
        if size == 4:
            acc[...] = (landing[stage, 0] + landing[stage, 1]) + (
                landing[stage, 2] + landing[stage, 3]
            )
        else:
            acc[...] = landing[stage, 0] + landing[stage, 1]
    share = mine_ref.shape[0]
    start = pl.multiple_of(here[MESH_AXES.index("rep")] * share, 8)
    mine_ref[...] = acc[pl.ds(start, share), :]
    last_ref[...] = acc[acc.shape[0] - last_ref.shape[0]:, :]


def _stages():
    stages = []
    for name in ("rep", "gy", "blk"):
        size = lax.axis_size(name)
        stride = 1
        while stride < size:
            group = 4 if size // stride >= 4 else 2
            stages.append((name, stride, group))
            stride *= group
    return stages


def _power_of_two(count):
    return count & (count - 1) == 0


def sum_everywhere(block, share):
    if not all(_power_of_two(lax.axis_size(name)) for name in MESH_AXES):
        summed = lax.psum(block, MESH_AXES)
        mine = lax.dynamic_slice_in_dim(summed, lax.axis_index("rep") * share, share, 0)
        return mine, summed[-8:]
    stages = _stages()
    vmem = pl.BlockSpec(memory_space=pltpu.VMEM)
    summed = pl.pallas_call(
        functools.partial(_allreduce_kernel, stages),
        out_shape=(
            jax.ShapeDtypeStruct((share, block.shape[1]), block.dtype),
            jax.ShapeDtypeStruct((8, block.shape[1]), block.dtype),
        ),
        in_specs=[vmem],
        out_specs=(vmem, vmem),
        scratch_shapes=[
            pltpu.VMEM(block.shape, block.dtype),
            pltpu.VMEM((len(stages), 4) + block.shape, block.dtype),
            pltpu.SemaphoreType.DMA((len(stages), 4)),
            pltpu.SemaphoreType.DMA((len(stages), 4)),
        ],
        compiler_params=pltpu.CompilerParams(collective_id=2, has_side_effects=True),
    )(block)
    return summed


def diffuse(field, field_nb, rates, rate_nb):
    summed = field
    for direction in range(3):
        rate_here = rates[2 * direction:2 * direction + 2]
        for side, offset in enumerate((1, -1)):
            summed = summed + 0.5 * (rate_here + rate_nb[direction][side]) * (
                field_nb[direction][side] - field
            )
    return summed


def rate_cotangent(state, state_nb, adjoint, adjoint_nb):
    pieces_list = []
    for direction in range(3):
        summed = jnp.zeros_like(state)
        for side, offset in enumerate((1, -1)):
            summed = summed + (state_nb[direction][side] - state) * (
                adjoint_nb[direction][side] - adjoint
            )
        pieces_list.append(-0.5 * summed)
    return jnp.concatenate(pieces_list, axis=0)


def embed_lookup(emb_table, grain_flat):
    table_rows = emb_table.shape[0]
    one_hot = (grain_flat[None, :] == lax.broadcasted_iota(jnp.int32, (table_rows, 1), 0)).astype(
        jnp.bfloat16
    )
    looked = jnp.dot(emb_table.T, one_hot, preferred_element_type=jnp.float32)
    return looked.astype(jnp.bfloat16)


def forward_layers(params, features):
    w_in, b_in, w_mid, b_mid, w_out, b_out = params
    act_one = jnp.tanh(
        jnp.dot(w_in, features, preferred_element_type=jnp.float32)
        + b_in.astype(jnp.float32)[:, None]
    )
    hid_one = act_one.astype(jnp.bfloat16)
    act_two = jnp.tanh(
        jnp.dot(w_mid, hid_one, preferred_element_type=jnp.float32)
        + b_mid.astype(jnp.float32)[:, None]
    )
    hid_two = act_two.astype(jnp.bfloat16)
    logits = (
        jnp.dot(w_out, hid_two, preferred_element_type=jnp.float32)
        + b_out.astype(jnp.float32)[:, None]
    )
    return (RATE_MAX * jax.nn.sigmoid(logits), act_one, hid_one, act_two, hid_two)


def backward_layers(params, rate_grad, forward_values):
    w_in, b_in, w_mid, b_mid, w_out, b_out = params
    rate_values, act_one, hid_one, act_two, hid_two = forward_values
    out_grad = (rate_grad * rate_values * (1.0 - rate_values / RATE_MAX)).astype(jnp.bfloat16)
    two_grad = (
        jnp.dot(w_out.T, out_grad, preferred_element_type=jnp.float32) * (1.0 - act_two * act_two)
    ).astype(jnp.bfloat16)
    one_grad = (
        jnp.dot(w_mid.T, two_grad, preferred_element_type=jnp.float32) * (1.0 - act_one * act_one)
    ).astype(jnp.bfloat16)
    state_grad = jnp.dot(w_in[:, -2:].T, one_grad, preferred_element_type=jnp.float32)
    return (out_grad, two_grad, one_grad), state_grad


def gradient_sums(grads, inputs):
    terms = []
    for grad_list, input_list in zip(grads, inputs):
        grad = jnp.concatenate(grad_list, axis=1)
        ones = jnp.ones((1, grad.shape[1]), jnp.bfloat16)
        layer_input = jnp.concatenate(input_list, axis=1)
        layer_input = jnp.concatenate([layer_input, ones], axis=0)
        terms.append(jnp.dot(grad, layer_input.T, preferred_element_type=jnp.float32))
    return terms


def gather_params(w_in, b_in, w_mid, b_mid, w_out, b_out):
    n_in = w_in.shape[1]
    n_mid = w_mid.shape[1]
    packed = jnp.concatenate(
        [w_in, b_in[:, None], w_mid, b_mid[:, None], w_out.T], axis=1
    ).astype(jnp.bfloat16)
    full = lax.all_gather(packed, "rep", axis=0, tiled=True)
    col = 0
    w_in_b = full[:, col:col + n_in]
    col += n_in
    b_in_b = full[:, col]
    col += 1
    w_mid_b = full[:, col:col + n_mid]
    col += n_mid
    b_mid_b = full[:, col]
    col += 1
    w_out_b = full[:, col:].T
    order = jnp.array(RATE_ORDER)
    return (w_in_b, b_in_b, w_mid_b, b_mid_b, w_out_b[order], b_out.astype(jnp.bfloat16)[order])


def per_device(
    grain_id, init_masks, target_masks, emb_table, w_in, b_in, w_mid, b_mid, w_out, b_out
):
    params = gather_params(w_in, b_in, w_mid, b_mid, w_out, b_out)
    depth_cells, row_cells, col_cells = grain_id.shape
    cell_count = depth_cells * row_cells * col_cells
    block_shape = (depth_cells, row_cells, col_cells)
    embedding = embed_lookup(emb_table, grain_id.reshape(cell_count))
    state_now = init_masks.astype(jnp.float32)
    history = []
    forward_plan = [[(0, 0, 2), (1, 2 * d, 2)] for d in range(3)]
    for step_index in range(STEPS):
        features = jnp.concatenate(
            [embedding, state_now.reshape(2, cell_count).astype(jnp.bfloat16)], axis=0
        )
        rate_values = forward_layers(params, features)[0].reshape((6,) + block_shape)
        neighbours = exchange_neighbours([state_now, rate_values], forward_plan, 0)
        state_nb = [pairs[0] for pairs in neighbours]
        rate_nb = [pairs[1] for pairs in neighbours]
        history.append((state_now, state_nb, rate_values, rate_nb))
        state_now = diffuse(state_now, state_nb, rate_values, rate_nb)
    misfit = state_now - target_masks.astype(jnp.float32)
    total_cells = float(
        cell_count * lax.axis_size("blk") * lax.axis_size("gy") * lax.axis_size("rep")
    )
    loss_part = jnp.sum(misfit * misfit) / (4.0 * total_cells)
    adjoint = misfit / (2.0 * total_cells)
    grads = ([], [], [])
    inputs = ([], [], [])
    for step_index in reversed(range(STEPS)):
        state_t, state_nb, rate_values, rate_nb = history[step_index]
        adjoint_nb = [
            pairs[0] for pairs in exchange_neighbours([adjoint], [[(0, 0, 2)]] * 3, 1)
        ]
        rate_grad = rate_cotangent(state_t, state_nb, adjoint, adjoint_nb).reshape(
            6, cell_count
        )
        features = jnp.concatenate(
            [embedding, state_t.reshape(2, cell_count).astype(jnp.bfloat16)], axis=0
        )
        forward_values = forward_layers(params, features)
        step_grads, state_grad = backward_layers(params, rate_grad, forward_values)
        for index, (grad, layer_input) in enumerate(
            zip(reversed(step_grads), (features, forward_values[2], forward_values[4]))
        ):
            grads[index].append(grad)
            inputs[index].append(layer_input)
        adjoint = diffuse(adjoint, adjoint_nb, rate_values, rate_nb) + state_grad.reshape(
            (2,) + block_shape
        )
    grad_sums = gradient_sums(grads, inputs)
    start_sensitivity = adjoint * (2.0 * total_cells)
    in_both, mid_both, out_both = grad_sums
    back = jnp.array([RATE_ORDER.index(channel) for channel in range(6)])
    out_both = out_both[back]
    units = in_both.shape[0]
    per_unit = jnp.concatenate([in_both, mid_both, out_both[:, :-1].T], axis=1)
    width = per_unit.shape[1]
    last = jnp.concatenate([out_both[:, -1], loss_part[None]])
    rows = -(-(units + 1) // 8) * 8
    packed = jnp.zeros((rows, 128), jnp.float32)
    packed = packed.at[:units, :width].set(per_unit)
    packed = packed.at[units, :last.shape[0]].set(last)
    share_width = w_in.shape[0]
    mine, last_rows = sum_everywhere(packed, share_width)
    n_in = w_in.shape[1]
    n_mid = w_mid.shape[1]
    grad_w_in = mine[:, :n_in]
    grad_b_in = mine[:, n_in]
    grad_w_mid = mine[:, n_in + 1:n_in + 1 + n_mid]
    grad_b_mid = mine[:, n_in + 1 + n_mid]
    grad_w_out = mine[:, n_in + 2 + n_mid:width].T
    grad_b_out = last_rows[units - (rows - 8), :6]
    loss_total = last_rows[units - (rows - 8), 6]
    return (
        state_now,
        loss_total,
        grad_w_in,
        grad_b_in,
        grad_w_mid,
        grad_b_mid,
        grad_w_out,
        grad_b_out,
        start_sensitivity,
    )


def solution(mesh):
    in_specs = (
        P("blk", "gy", "rep"),
        P(None, "blk", "gy", "rep"),
        P(None, "blk", "gy", "rep"),
        P(),
        P("rep", None),
        P("rep"),
        P("rep", None),
        P("rep"),
        P(None, "rep"),
        P(),
    )
    out_specs = (
        P(None, "blk", "gy", "rep"),
        P(),
        P("rep", None),
        P("rep"),
        P("rep", None),
        P("rep"),
        P(None, "rep"),
        P(),
        P(None, "blk", "gy", "rep"),
    )
    return jax.shard_map(
        per_device, mesh=mesh, in_specs=in_specs, out_specs=out_specs, check_vma=False
    )
```

```python
import functools

import jax
import jax.numpy as jnp
from jax import lax
from jax.experimental import pallas as pl
from jax.experimental.pallas import tpu as pltpu
from jax.sharding import PartitionSpec as P

STEPS = 4


RATE_MAX = 0.15

AXES = (("rep", 3), ("gy", 2), ("blk", 1))
MESH_AXES = ("blk", "gy", "rep")
RATE_ORDER = (0, 3, 1, 4, 2, 5)


def _neighbour_kernel(sizes, plan, n_fields, *refs):
    fields = refs[:n_fields]
    n_items = sum(len(items) for items in plan)
    outs = refs[n_fields:n_fields + 2 * n_items]
    landing = refs[n_fields + 2 * n_items:n_fields + 4 * n_items]
    staged = refs[n_fields + 4 * n_items:n_fields + 6 * n_items]
    send_sems, recv_sems = refs[-2], refs[-1]
    here = [lax.axis_index(name) for name in MESH_AXES]

    def neighbour(axis, step):
        coords = list(here)
        position = MESH_AXES.index(axis)
        coords[position] = lax.rem(here[position] + step + sizes[position], sizes[position])
        return tuple(coords)

    targets = [(neighbour(axis, 1), neighbour(axis, -1)) for axis, dim in AXES]
    barrier = pltpu.get_barrier_semaphore()
    for plus, minus in targets:
        for peer in (plus, minus):
            pl.semaphore_signal(barrier, 1, device_id=peer, device_id_type=pl.DeviceIdType.MESH)
    pl.semaphore_wait(barrier, 6)
    copies = []
    item = 0
    for direction, (axis, dim) in enumerate(AXES):
        plus, minus = targets[direction]
        for field, first, count in plan[direction]:
            group = fields[field].at[first:first + count]
            depth = fields[field].shape[1]
            if dim == 1:
                to_plus, to_minus = group.at[:, depth - 1], group.at[:, 0]
            elif dim == 2:
                rows = group.shape[2]
                staged[2 * item][...] = group[:, :, rows - 1, :]
                staged[2 * item + 1][...] = group[:, :, 0, :]
                to_plus, to_minus = staged[2 * item], staged[2 * item + 1]
            else:
                to_plus, to_minus = group, group
            for slot, source, peer in ((0, to_plus, plus), (1, to_minus, minus)):
                index = 2 * item + slot
                copy = pltpu.make_async_remote_copy(
                    src_ref=source,
                    dst_ref=landing[index],
                    send_sem=send_sems.at[index],
                    recv_sem=recv_sems.at[index],
                    device_id=peer,
                    device_id_type=pl.DeviceIdType.MESH,
                )
                copy.start()
                copies.append(copy)
            item += 1
    for copy in copies:
        copy.wait()
    item = 0
    for direction, (axis, dim) in enumerate(AXES):
        for field, first, count in plan[direction]:
            group = fields[field].at[first:first + count]
            from_below, from_above = landing[2 * item], landing[2 * item + 1]
            out_plus, out_minus = outs[2 * item], outs[2 * item + 1]
            if dim == 1:
                depth = group.shape[1]
                out_plus[:, 0:depth - 1] = group[:, 1:depth]
                out_plus[:, depth - 1] = from_above[...]
                out_minus[:, 1:depth] = group[:, 0:depth - 1]
                out_minus[:, 0] = from_below[...]
            else:
                values = group[...]
                size = values.shape[dim]
                index = lax.broadcasted_iota(jnp.int32, values.shape, dim)
                above, below = from_above[...], from_below[...]
                if dim == 2:
                    above = jnp.broadcast_to(above[:, :, None, :], values.shape)
                    below = jnp.broadcast_to(below[:, :, None, :], values.shape)
                out_plus[...] = pltpu.roll(jnp.where(index == 0, above, values), size - 1, dim)
                out_minus[...] = pltpu.roll(
                    jnp.where(index == size - 1, below, values), 1, dim
                )
            item += 1


def exchange_neighbours(fields, plan, collective_id):
    sizes = tuple(lax.axis_size(name) for name in MESH_AXES)
    group_shapes = []
    landing_shapes = []
    for direction, (axis, dim) in enumerate(AXES):
        for field, first, count in plan[direction]:
            shape = (count,) + fields[field].shape[1:]
            group_shapes.append(shape)
            if dim == 1:
                layer = shape[:1] + shape[2:]
            elif dim == 2:
                layer = shape[:2] + shape[3:]
            else:
                layer = shape
            landing_shapes += [layer, layer]
    n_items = len(group_shapes)
    vmem = pl.BlockSpec(memory_space=pltpu.VMEM)
    out_shapes = []
    for shape in group_shapes:
        out_shapes += [jax.ShapeDtypeStruct(shape, jnp.float32)] * 2
    shifted = pl.pallas_call(
        functools.partial(_neighbour_kernel, sizes, plan, len(fields)),
        out_shape=tuple(out_shapes),
        in_specs=[vmem] * len(fields),
        out_specs=(vmem,) * len(out_shapes),
        scratch_shapes=[pltpu.VMEM(shape, jnp.float32) for shape in landing_shapes]
        + [pltpu.VMEM(shape, jnp.float32) for shape in landing_shapes]
        + [pltpu.SemaphoreType.DMA((2 * n_items,)), pltpu.SemaphoreType.DMA((2 * n_items,))],
        compiler_params=pltpu.CompilerParams(collective_id=collective_id, has_side_effects=True),
    )(*fields)
    result = []
    item = 0
    for direction in range(3):
        pairs = []
        for _ in plan[direction]:
            pairs.append((shifted[2 * item], shifted[2 * item + 1]))
            item += 1
        result.append(pairs)
    return result


def _allreduce_kernel(stages, partial_ref, mine_ref, last_ref, acc, landing, send_sems, recv_sems):
    here = [lax.axis_index(name) for name in MESH_AXES]

    def member(name, stride, size, digit):
        position = MESH_AXES.index(name)
        own = lax.rem(here[position] // stride, size)
        coords = list(here)
        coords[position] = here[position] + (digit - own) * stride
        return tuple(coords), own

    barrier = pltpu.get_barrier_semaphore()
    partner_count = 0
    for name, stride, size in stages:
        for step in range(1, size):
            position = MESH_AXES.index(name)
            own = lax.rem(here[position] // stride, size)
            digit = lax.rem(own + step, size)
            peer, _ = member(name, stride, size, digit)
            pl.semaphore_signal(barrier, 1, device_id=peer, device_id_type=pl.DeviceIdType.MESH)
            partner_count += 1
    pl.semaphore_wait(barrier, partner_count)
    acc[...] = partial_ref[...]
    for stage, (name, stride, size) in enumerate(stages):
        position = MESH_AXES.index(name)
        own = lax.rem(here[position] // stride, size)
        landing[stage, own] = acc[...]
        sends = []
        receives = []
        for step in range(1, size):
            digit = lax.rem(own + step, size)
            peer, _ = member(name, stride, size, digit)
            copy = pltpu.make_async_remote_copy(
                src_ref=acc,
                dst_ref=landing.at[stage, own],
                send_sem=send_sems.at[stage, step],
                recv_sem=recv_sems.at[stage, own],
                device_id=peer,
                device_id_type=pl.DeviceIdType.MESH,
            )
            copy.start()
            sends.append(copy)
            receives.append(
                pltpu.make_async_remote_copy(
                    src_ref=acc,
                    dst_ref=landing.at[stage, digit],
                    send_sem=send_sems.at[stage, step],
                    recv_sem=recv_sems.at[stage, digit],
                    device_id=peer,
                    device_id_type=pl.DeviceIdType.MESH,
                )
            )
        for copy in sends:
            copy.wait_send()
        for copy in receives:
            copy.wait_recv()
        if size == 4:
            acc[...] = (landing[stage, 0] + landing[stage, 1]) + (
                landing[stage, 2] + landing[stage, 3]
            )
        else:
            acc[...] = landing[stage, 0] + landing[stage, 1]
    share = mine_ref.shape[0]
    start = pl.multiple_of(here[MESH_AXES.index("rep")] * share, 8)
    mine_ref[...] = acc[pl.ds(start, share), :]
    last_ref[...] = acc[acc.shape[0] - last_ref.shape[0]:, :]


def _stages():
    stages = []
    for name in ("rep", "gy", "blk"):
        size = lax.axis_size(name)
        stride = 1
        while stride < size:
            group = 4 if size // stride >= 4 else 2
            stages.append((name, stride, group))
            stride *= group
    return stages


def _power_of_two(count):
    return count & (count - 1) == 0


def sum_everywhere(block, share):
    if not all(_power_of_two(lax.axis_size(name)) for name in MESH_AXES):
        summed = lax.psum(block, MESH_AXES)
        mine = lax.dynamic_slice_in_dim(summed, lax.axis_index("rep") * share, share, 0)
        return mine, summed[-8:]
    stages = _stages()
    vmem = pl.BlockSpec(memory_space=pltpu.VMEM)
    summed = pl.pallas_call(
        functools.partial(_allreduce_kernel, stages),
        out_shape=(
            jax.ShapeDtypeStruct((share, block.shape[1]), block.dtype),
            jax.ShapeDtypeStruct((8, block.shape[1]), block.dtype),
        ),
        in_specs=[vmem],
        out_specs=(vmem, vmem),
        scratch_shapes=[
            pltpu.VMEM(block.shape, block.dtype),
            pltpu.VMEM((len(stages), 4) + block.shape, block.dtype),
            pltpu.SemaphoreType.DMA((len(stages), 4)),
            pltpu.SemaphoreType.DMA((len(stages), 4)),
        ],
        compiler_params=pltpu.CompilerParams(collective_id=2, has_side_effects=True),
    )(block)
    return summed


def diffuse(field, field_nb, rates, rate_nb):
    summed = field
    for direction in range(3):
        rate_here = rates[2 * direction:2 * direction + 2]
        for side, offset in enumerate((1, -1)):
            summed = summed + 0.5 * (rate_here + rate_nb[direction][side]) * (
                field_nb[direction][side] - field
            )
    return summed


def rate_cotangent(state, state_nb, adjoint, adjoint_nb):
    pieces_list = []
    for direction in range(3):
        summed = jnp.zeros_like(state)
        for side, offset in enumerate((1, -1)):
            summed = summed + (state_nb[direction][side] - state) * (
                adjoint_nb[direction][side] - adjoint
            )
        pieces_list.append(-0.5 * summed)
    return jnp.concatenate(pieces_list, axis=0)


def embed_lookup(emb_table, grain_flat):
    table_rows = emb_table.shape[0]
    one_hot = (grain_flat[None, :] == lax.broadcasted_iota(jnp.int32, (table_rows, 1), 0)).astype(
        jnp.bfloat16
    )
    looked = jnp.dot(emb_table.T, one_hot, preferred_element_type=jnp.float32)
    return looked.astype(jnp.bfloat16)


def forward_layers(params, features):
    w_in, b_in, w_mid, b_mid, w_out, b_out = params
    act_one = jnp.tanh(
        jnp.dot(w_in, features, preferred_element_type=jnp.float32)
        + b_in.astype(jnp.float32)[:, None]
    )
    hid_one = act_one.astype(jnp.bfloat16)
    act_two = jnp.tanh(
        jnp.dot(w_mid, hid_one, preferred_element_type=jnp.float32)
        + b_mid.astype(jnp.float32)[:, None]
    )
    hid_two = act_two.astype(jnp.bfloat16)
    logits = (
        jnp.dot(w_out, hid_two, preferred_element_type=jnp.float32)
        + b_out.astype(jnp.float32)[:, None]
    )
    return (RATE_MAX * jax.nn.sigmoid(logits), act_one, hid_one, act_two, hid_two)


def backward_layers(params, rate_grad, forward_values):
    w_in, b_in, w_mid, b_mid, w_out, b_out = params
    rate_values, act_one, hid_one, act_two, hid_two = forward_values
    out_grad = (rate_grad * rate_values * (1.0 - rate_values / RATE_MAX)).astype(jnp.bfloat16)
    two_grad = (
        jnp.dot(w_out.T, out_grad, preferred_element_type=jnp.float32) * (1.0 - act_two * act_two)
    ).astype(jnp.bfloat16)
    one_grad = (
        jnp.dot(w_mid.T, two_grad, preferred_element_type=jnp.float32) * (1.0 - act_one * act_one)
    ).astype(jnp.bfloat16)
    state_grad = jnp.dot(w_in[:, -2:].T, one_grad, preferred_element_type=jnp.float32)
    return (out_grad, two_grad, one_grad), state_grad


def gradient_sums(grads, inputs):
    terms = []
    for grad_list, input_list in zip(grads, inputs):
        grad = jnp.concatenate(grad_list, axis=1)
        ones = jnp.ones((1, grad.shape[1]), jnp.bfloat16)
        layer_input = jnp.concatenate(input_list, axis=1)
        layer_input = jnp.concatenate([layer_input, ones], axis=0)
        terms.append(jnp.dot(grad, layer_input.T, preferred_element_type=jnp.float32))
    return terms


def gather_params(w_in, b_in, w_mid, b_mid, w_out, b_out):
    n_in = w_in.shape[1]
    n_mid = w_mid.shape[1]
    packed = jnp.concatenate(
        [w_in, b_in[:, None], w_mid, b_mid[:, None], w_out.T], axis=1
    ).astype(jnp.bfloat16)
    full = lax.all_gather(packed, "rep", axis=0, tiled=True)
    col = 0
    w_in_b = full[:, col:col + n_in]
    col += n_in
    b_in_b = full[:, col]
    col += 1
    w_mid_b = full[:, col:col + n_mid]
    col += n_mid
    b_mid_b = full[:, col]
    col += 1
    w_out_b = full[:, col:].T
    order = jnp.array(RATE_ORDER)
    return (w_in_b, b_in_b, w_mid_b, b_mid_b, w_out_b[order], b_out.astype(jnp.bfloat16)[order])


def per_device(
    grain_id, init_masks, target_masks, emb_table, w_in, b_in, w_mid, b_mid, w_out, b_out
):
    params = gather_params(w_in, b_in, w_mid, b_mid, w_out, b_out)
    depth_cells, row_cells, col_cells = grain_id.shape
    cell_count = depth_cells * row_cells * col_cells
    block_shape = (depth_cells, row_cells, col_cells)
    embedding = embed_lookup(emb_table, grain_id.reshape(cell_count))
    state_now = init_masks.astype(jnp.float32)
    history = []
    forward_plan = [[(0, 0, 2), (1, 2 * d, 2)] for d in range(3)]
    for step_index in range(STEPS):
        features = jnp.concatenate(
            [embedding, state_now.reshape(2, cell_count).astype(jnp.bfloat16)], axis=0
        )
        rate_values = forward_layers(params, features)[0].reshape((6,) + block_shape)
        neighbours = exchange_neighbours([state_now, rate_values], forward_plan, 0)
        state_nb = [pairs[0] for pairs in neighbours]
        rate_nb = [pairs[1] for pairs in neighbours]
        history.append((state_now, state_nb, rate_values, rate_nb))
        state_now = diffuse(state_now, state_nb, rate_values, rate_nb)
    misfit = state_now - target_masks.astype(jnp.float32)
    total_cells = float(
        cell_count * lax.axis_size("blk") * lax.axis_size("gy") * lax.axis_size("rep")
    )
    loss_part = jnp.sum(misfit * misfit) / (4.0 * total_cells)
    adjoint = misfit / (2.0 * total_cells)
    grads = ([], [], [])
    inputs = ([], [], [])
    for step_index in reversed(range(STEPS)):
        state_t, state_nb, rate_values, rate_nb = history[step_index]
        adjoint_nb = [
            pairs[0] for pairs in exchange_neighbours([adjoint], [[(0, 0, 2)]] * 3, 1)
        ]
        rate_grad = rate_cotangent(state_t, state_nb, adjoint, adjoint_nb).reshape(
            6, cell_count
        )
        features = jnp.concatenate(
            [embedding, state_t.reshape(2, cell_count).astype(jnp.bfloat16)], axis=0
        )
        forward_values = forward_layers(params, features)
        step_grads, state_grad = backward_layers(params, rate_grad, forward_values)
        for index, (grad, layer_input) in enumerate(
            zip(reversed(step_grads), (features, forward_values[2], forward_values[4]))
        ):
            grads[index].append(grad)
            inputs[index].append(layer_input)
        adjoint = diffuse(adjoint, adjoint_nb, rate_values, rate_nb) + state_grad.reshape(
            (2,) + block_shape
        )
    grad_sums = gradient_sums(grads, inputs)
    start_sensitivity = adjoint * (2.0 * total_cells)
    in_both, mid_both, out_both = grad_sums
    back = jnp.array([RATE_ORDER.index(channel) for channel in range(6)])
    out_both = out_both[back]
    units = in_both.shape[0]
    per_unit = jnp.concatenate([in_both, mid_both, out_both[:, :-1].T], axis=1)
    width = per_unit.shape[1]
    last = jnp.concatenate([out_both[:, -1], loss_part[None]])
    rows = -(-(units + 1) // 8) * 8
    packed = jnp.zeros((rows, 128), jnp.float32)
    packed = packed.at[:units, :width].set(per_unit)
    packed = packed.at[units, :last.shape[0]].set(last)
    share_width = w_in.shape[0]
    mine, last_rows = sum_everywhere(packed, share_width)
    n_in = w_in.shape[1]
    n_mid = w_mid.shape[1]
    grad_w_in = mine[:, :n_in]
    grad_b_in = mine[:, n_in]
    grad_w_mid = mine[:, n_in + 1:n_in + 1 + n_mid]
    grad_b_mid = mine[:, n_in + 1 + n_mid]
    grad_w_out = mine[:, n_in + 2 + n_mid:width].T
    grad_b_out = last_rows[units - (rows - 8), :6]
    loss_total = last_rows[units - (rows - 8), 6]
    return (
        state_now,
        loss_total,
        grad_w_in,
        grad_b_in,
        grad_w_mid,
        grad_b_mid,
        grad_w_out,
        grad_b_out,
        start_sensitivity,
    )


def solution(mesh):
    in_specs = (
        P("blk", "gy", "rep"),
        P(None, "blk", "gy", "rep"),
        P(None, "blk", "gy", "rep"),
        P(),
        P("rep", None),
        P("rep"),
        P("rep", None),
        P("rep"),
        P(None, "rep"),
        P(),
    )
    out_specs = (
        P(None, "blk", "gy", "rep"),
        P(),
        P("rep", None),
        P("rep"),
        P("rep", None),
        P("rep"),
        P(None, "rep"),
        P(),
        P(None, "blk", "gy", "rep"),
    )
    return jax.shard_map(
        per_device, mesh=mesh, in_specs=in_specs, out_specs=out_specs, check_vma=False
    )
```

```python
import functools

import jax
import jax.numpy as jnp
from jax import lax
from jax.experimental import pallas as pl
from jax.experimental.pallas import tpu as pltpu
from jax.sharding import PartitionSpec as P

STEPS = 4


RATE_MAX = 0.15

AXES = (("rep", 3), ("gy", 2), ("blk", 1))
MESH_AXES = ("blk", "gy", "rep")
RATE_ORDER = (0, 3, 1, 4, 2, 5)


def _neighbour_kernel(sizes, plan, n_fields, *refs):
    fields = refs[:n_fields]
    n_items = sum(len(items) for items in plan)
    stacked = refs[n_fields]
    outs = [stacked.at[index] for index in range(2 * n_items)]
    landing = refs[n_fields + 1:n_fields + 1 + 2 * n_items]
    staged = refs[n_fields + 1 + 2 * n_items:n_fields + 1 + 4 * n_items]
    send_sems, recv_sems = refs[-2], refs[-1]
    here = [lax.axis_index(name) for name in MESH_AXES]

    def neighbour(axis, step):
        coords = list(here)
        position = MESH_AXES.index(axis)
        coords[position] = lax.rem(here[position] + step + sizes[position], sizes[position])
        return tuple(coords)

    targets = [(neighbour(axis, 1), neighbour(axis, -1)) for axis, dim in AXES]
    barrier = pltpu.get_barrier_semaphore()
    for plus, minus in targets:
        for peer in (plus, minus):
            pl.semaphore_signal(barrier, 1, device_id=peer, device_id_type=pl.DeviceIdType.MESH)
    pl.semaphore_wait(barrier, 6)
    copies = []
    item = 0
    for direction, (axis, dim) in enumerate(AXES):
        plus, minus = targets[direction]
        for field, first, count in plan[direction]:
            group = fields[field].at[first:first + count]
            depth = fields[field].shape[1]
            if dim == 1:
                to_plus, to_minus = group.at[:, depth - 1], group.at[:, 0]
            elif dim == 2:
                rows = group.shape[2]
                staged[2 * item][...] = group[:, :, rows - 1, :]
                staged[2 * item + 1][...] = group[:, :, 0, :]
                to_plus, to_minus = staged[2 * item], staged[2 * item + 1]
            else:
                to_plus, to_minus = group, group
            for slot, source, peer in ((0, to_plus, plus), (1, to_minus, minus)):
                index = 2 * item + slot
                copy = pltpu.make_async_remote_copy(
                    src_ref=source,
                    dst_ref=landing[index],
                    send_sem=send_sems.at[index],
                    recv_sem=recv_sems.at[index],
                    device_id=peer,
                    device_id_type=pl.DeviceIdType.MESH,
                )
                copy.start()
                copies.append(copy)
            item += 1
    for copy in copies:
        copy.wait()
    item = 0
    for direction, (axis, dim) in enumerate(AXES):
        for field, first, count in plan[direction]:
            group = fields[field].at[first:first + count]
            from_below, from_above = landing[2 * item], landing[2 * item + 1]
            out_plus, out_minus = outs[2 * item], outs[2 * item + 1]
            if dim == 1:
                depth = group.shape[1]
                out_plus[:, 0:depth - 1] = group[:, 1:depth]
                out_plus[:, depth - 1] = from_above[...]
                out_minus[:, 1:depth] = group[:, 0:depth - 1]
                out_minus[:, 0] = from_below[...]
            else:
                values = group[...]
                size = values.shape[dim]
                index = lax.broadcasted_iota(jnp.int32, values.shape, dim)
                above, below = from_above[...], from_below[...]
                if dim == 2:
                    above = jnp.broadcast_to(above[:, :, None, :], values.shape)
                    below = jnp.broadcast_to(below[:, :, None, :], values.shape)
                out_plus[...] = pltpu.roll(jnp.where(index == 0, above, values), size - 1, dim)
                out_minus[...] = pltpu.roll(
                    jnp.where(index == size - 1, below, values), 1, dim
                )
            item += 1


def exchange_neighbours(fields, plan, collective_id):
    sizes = tuple(lax.axis_size(name) for name in MESH_AXES)
    group_shapes = []
    landing_shapes = []
    for direction, (axis, dim) in enumerate(AXES):
        for field, first, count in plan[direction]:
            shape = (count,) + fields[field].shape[1:]
            group_shapes.append(shape)
            if dim == 1:
                layer = shape[:1] + shape[2:]
            elif dim == 2:
                layer = shape[:2] + shape[3:]
            else:
                layer = shape
            landing_shapes += [layer, layer]
    n_items = len(group_shapes)
    assert all(shape == group_shapes[0] for shape in group_shapes)
    vmem = pl.BlockSpec(memory_space=pltpu.VMEM)
    shifted = pl.pallas_call(
        functools.partial(_neighbour_kernel, sizes, plan, len(fields)),
        out_shape=jax.ShapeDtypeStruct((2 * n_items,) + group_shapes[0], jnp.float32),
        in_specs=[vmem] * len(fields),
        out_specs=vmem,
        scratch_shapes=[pltpu.VMEM(shape, jnp.float32) for shape in landing_shapes]
        + [pltpu.VMEM(shape, jnp.float32) for shape in landing_shapes]
        + [pltpu.SemaphoreType.DMA((2 * n_items,)), pltpu.SemaphoreType.DMA((2 * n_items,))],
        compiler_params=pltpu.CompilerParams(collective_id=collective_id, has_side_effects=True),
    )(*fields)
    result = []
    item = 0
    for direction in range(3):
        pairs = []
        for _ in plan[direction]:
            pairs.append((shifted[2 * item], shifted[2 * item + 1]))
            item += 1
        result.append(pairs)
    return result


def _allreduce_kernel(stages, partial_ref, mine_ref, last_ref, acc, landing, send_sems, recv_sems):
    here = [lax.axis_index(name) for name in MESH_AXES]

    def member(name, stride, size, digit):
        position = MESH_AXES.index(name)
        own = lax.rem(here[position] // stride, size)
        coords = list(here)
        coords[position] = here[position] + (digit - own) * stride
        return tuple(coords), own

    barrier = pltpu.get_barrier_semaphore()
    partner_count = 0
    for name, stride, size in stages:
        for step in range(1, size):
            position = MESH_AXES.index(name)
            own = lax.rem(here[position] // stride, size)
            digit = lax.rem(own + step, size)
            peer, _ = member(name, stride, size, digit)
            pl.semaphore_signal(barrier, 1, device_id=peer, device_id_type=pl.DeviceIdType.MESH)
            partner_count += 1
    pl.semaphore_wait(barrier, partner_count)
    acc[...] = partial_ref[...]
    for stage, (name, stride, size) in enumerate(stages):
        position = MESH_AXES.index(name)
        own = lax.rem(here[position] // stride, size)
        landing[stage, own] = acc[...]
        sends = []
        receives = []
        for step in range(1, size):
            digit = lax.rem(own + step, size)
            peer, _ = member(name, stride, size, digit)
            copy = pltpu.make_async_remote_copy(
                src_ref=acc,
                dst_ref=landing.at[stage, own],
                send_sem=send_sems.at[stage, step],
                recv_sem=recv_sems.at[stage, own],
                device_id=peer,
                device_id_type=pl.DeviceIdType.MESH,
            )
            copy.start()
            sends.append(copy)
            receives.append(
                pltpu.make_async_remote_copy(
                    src_ref=acc,
                    dst_ref=landing.at[stage, digit],
                    send_sem=send_sems.at[stage, step],
                    recv_sem=recv_sems.at[stage, digit],
                    device_id=peer,
                    device_id_type=pl.DeviceIdType.MESH,
                )
            )
        for copy in sends:
            copy.wait_send()
        for copy in receives:
            copy.wait_recv()
        if size == 4:
            acc[...] = (landing[stage, 0] + landing[stage, 1]) + (
                landing[stage, 2] + landing[stage, 3]
            )
        else:
            acc[...] = landing[stage, 0] + landing[stage, 1]
    share = mine_ref.shape[0]
    start = pl.multiple_of(here[MESH_AXES.index("rep")] * share, 8)
    mine_ref[...] = acc[pl.ds(start, share), :]
    last_ref[...] = acc[acc.shape[0] - last_ref.shape[0]:, :]


def _stages():
    stages = []
    for name in ("rep", "gy", "blk"):
        size = lax.axis_size(name)
        stride = 1
        while stride < size:
            group = 4 if size // stride >= 4 else 2
            stages.append((name, stride, group))
            stride *= group
    return stages


def _power_of_two(count):
    return count & (count - 1) == 0


def sum_everywhere(block, share):
    if not all(_power_of_two(lax.axis_size(name)) for name in MESH_AXES):
        summed = lax.psum(block, MESH_AXES)
        mine = lax.dynamic_slice_in_dim(summed, lax.axis_index("rep") * share, share, 0)
        return mine, summed[-8:]
    stages = _stages()
    vmem = pl.BlockSpec(memory_space=pltpu.VMEM)
    summed = pl.pallas_call(
        functools.partial(_allreduce_kernel, stages),
        out_shape=(
            jax.ShapeDtypeStruct((share, block.shape[1]), block.dtype),
            jax.ShapeDtypeStruct((8, block.shape[1]), block.dtype),
        ),
        in_specs=[vmem],
        out_specs=(vmem, vmem),
        scratch_shapes=[
            pltpu.VMEM(block.shape, block.dtype),
            pltpu.VMEM((len(stages), 4) + block.shape, block.dtype),
            pltpu.SemaphoreType.DMA((len(stages), 4)),
            pltpu.SemaphoreType.DMA((len(stages), 4)),
        ],
        compiler_params=pltpu.CompilerParams(collective_id=2, has_side_effects=True),
    )(block)
    return summed


def diffuse(field, field_nb, rates, rate_nb):
    summed = field
    for direction in range(3):
        rate_here = rates[2 * direction:2 * direction + 2]
        for side, offset in enumerate((1, -1)):
            summed = summed + 0.5 * (rate_here + rate_nb[direction][side]) * (
                field_nb[direction][side] - field
            )
    return summed


def rate_cotangent(state, state_nb, adjoint, adjoint_nb):
    pieces_list = []
    for direction in range(3):
        summed = jnp.zeros_like(state)
        for side, offset in enumerate((1, -1)):
            summed = summed + (state_nb[direction][side] - state) * (
                adjoint_nb[direction][side] - adjoint
            )
        pieces_list.append(-0.5 * summed)
    return jnp.concatenate(pieces_list, axis=0)


def embed_lookup(emb_table, grain_flat):
    table_rows = emb_table.shape[0]
    one_hot = (grain_flat[None, :] == lax.broadcasted_iota(jnp.int32, (table_rows, 1), 0)).astype(
        jnp.bfloat16
    )
    looked = jnp.dot(emb_table.T, one_hot, preferred_element_type=jnp.float32)
    return looked.astype(jnp.bfloat16)


def forward_layers(params, features):
    w_in, b_in, w_mid, b_mid, w_out, b_out = params
    act_one = jnp.tanh(
        jnp.dot(w_in, features, preferred_element_type=jnp.float32)
        + b_in.astype(jnp.float32)[:, None]
    )
    hid_one = act_one.astype(jnp.bfloat16)
    act_two = jnp.tanh(
        jnp.dot(w_mid, hid_one, preferred_element_type=jnp.float32)
        + b_mid.astype(jnp.float32)[:, None]
    )
    hid_two = act_two.astype(jnp.bfloat16)
    logits = (
        jnp.dot(w_out, hid_two, preferred_element_type=jnp.float32)
        + b_out.astype(jnp.float32)[:, None]
    )
    return (RATE_MAX * jax.nn.sigmoid(logits), act_one, hid_one, act_two, hid_two)


def backward_layers(params, rate_grad, forward_values):
    w_in, b_in, w_mid, b_mid, w_out, b_out = params
    rate_values, act_one, hid_one, act_two, hid_two = forward_values
    out_grad = (rate_grad * rate_values * (1.0 - rate_values / RATE_MAX)).astype(jnp.bfloat16)
    two_grad = (
        jnp.dot(w_out.T, out_grad, preferred_element_type=jnp.float32) * (1.0 - act_two * act_two)
    ).astype(jnp.bfloat16)
    one_grad = (
        jnp.dot(w_mid.T, two_grad, preferred_element_type=jnp.float32) * (1.0 - act_one * act_one)
    ).astype(jnp.bfloat16)
    state_grad = jnp.dot(w_in[:, -2:].T, one_grad, preferred_element_type=jnp.float32)
    return (out_grad, two_grad, one_grad), state_grad


def gradient_sums(grads, inputs):
    terms = []
    for grad_list, input_list in zip(grads, inputs):
        grad = jnp.concatenate(grad_list, axis=1)
        ones = jnp.ones((1, grad.shape[1]), jnp.bfloat16)
        layer_input = jnp.concatenate(input_list, axis=1)
        layer_input = jnp.concatenate([layer_input, ones], axis=0)
        terms.append(jnp.dot(grad, layer_input.T, preferred_element_type=jnp.float32))
    return terms


def gather_params(w_in, b_in, w_mid, b_mid, w_out, b_out):
    n_in = w_in.shape[1]
    n_mid = w_mid.shape[1]
    packed = jnp.concatenate(
        [w_in, b_in[:, None], w_mid, b_mid[:, None], w_out.T], axis=1
    ).astype(jnp.bfloat16)
    full = lax.all_gather(packed, "rep", axis=0, tiled=True)
    col = 0
    w_in_b = full[:, col:col + n_in]
    col += n_in
    b_in_b = full[:, col]
    col += 1
    w_mid_b = full[:, col:col + n_mid]
    col += n_mid
    b_mid_b = full[:, col]
    col += 1
    w_out_b = full[:, col:].T
    order = jnp.array(RATE_ORDER)
    return (w_in_b, b_in_b, w_mid_b, b_mid_b, w_out_b[order], b_out.astype(jnp.bfloat16)[order])


def per_device(
    grain_id, init_masks, target_masks, emb_table, w_in, b_in, w_mid, b_mid, w_out, b_out
):
    params = gather_params(w_in, b_in, w_mid, b_mid, w_out, b_out)
    depth_cells, row_cells, col_cells = grain_id.shape
    cell_count = depth_cells * row_cells * col_cells
    block_shape = (depth_cells, row_cells, col_cells)
    embedding = embed_lookup(emb_table, grain_id.reshape(cell_count))
    state_now = init_masks.astype(jnp.float32)
    history = []
    forward_plan = [[(0, 0, 2), (1, 2 * d, 2)] for d in range(3)]
    for step_index in range(STEPS):
        features = jnp.concatenate(
            [embedding, state_now.reshape(2, cell_count).astype(jnp.bfloat16)], axis=0
        )
        rate_values = forward_layers(params, features)[0].reshape((6,) + block_shape)
        neighbours = exchange_neighbours([state_now, rate_values], forward_plan, 0)
        state_nb = [pairs[0] for pairs in neighbours]
        rate_nb = [pairs[1] for pairs in neighbours]
        history.append((state_now, state_nb, rate_values, rate_nb))
        state_now = diffuse(state_now, state_nb, rate_values, rate_nb)
    misfit = state_now - target_masks.astype(jnp.float32)
    total_cells = float(
        cell_count * lax.axis_size("blk") * lax.axis_size("gy") * lax.axis_size("rep")
    )
    loss_part = jnp.sum(misfit * misfit) / (4.0 * total_cells)
    adjoint = misfit / (2.0 * total_cells)
    grads = ([], [], [])
    inputs = ([], [], [])
    for step_index in reversed(range(STEPS)):
        state_t, state_nb, rate_values, rate_nb = history[step_index]
        adjoint_nb = [
            pairs[0] for pairs in exchange_neighbours([adjoint], [[(0, 0, 2)]] * 3, 1)
        ]
        rate_grad = rate_cotangent(state_t, state_nb, adjoint, adjoint_nb).reshape(
            6, cell_count
        )
        features = jnp.concatenate(
            [embedding, state_t.reshape(2, cell_count).astype(jnp.bfloat16)], axis=0
        )
        forward_values = forward_layers(params, features)
        step_grads, state_grad = backward_layers(params, rate_grad, forward_values)
        for index, (grad, layer_input) in enumerate(
            zip(reversed(step_grads), (features, forward_values[2], forward_values[4]))
        ):
            grads[index].append(grad)
            inputs[index].append(layer_input)
        adjoint = diffuse(adjoint, adjoint_nb, rate_values, rate_nb) + state_grad.reshape(
            (2,) + block_shape
        )
    grad_sums = gradient_sums(grads, inputs)
    start_sensitivity = adjoint * (2.0 * total_cells)
    in_both, mid_both, out_both = grad_sums
    back = jnp.array([RATE_ORDER.index(channel) for channel in range(6)])
    out_both = out_both[back]
    units = in_both.shape[0]
    per_unit = jnp.concatenate([in_both, mid_both, out_both[:, :-1].T], axis=1)
    width = per_unit.shape[1]
    last = jnp.concatenate([out_both[:, -1], loss_part[None]])
    rows = -(-(units + 1) // 8) * 8
    packed = jnp.zeros((rows, 128), jnp.float32)
    packed = packed.at[:units, :width].set(per_unit)
    packed = packed.at[units, :last.shape[0]].set(last)
    share_width = w_in.shape[0]
    mine, last_rows = sum_everywhere(packed, share_width)
    n_in = w_in.shape[1]
    n_mid = w_mid.shape[1]
    grad_w_in = mine[:, :n_in]
    grad_b_in = mine[:, n_in]
    grad_w_mid = mine[:, n_in + 1:n_in + 1 + n_mid]
    grad_b_mid = mine[:, n_in + 1 + n_mid]
    grad_w_out = mine[:, n_in + 2 + n_mid:width].T
    grad_b_out = last_rows[units - (rows - 8), :6]
    loss_total = last_rows[units - (rows - 8), 6]
    return (
        state_now,
        loss_total,
        grad_w_in,
        grad_b_in,
        grad_w_mid,
        grad_b_mid,
        grad_w_out,
        grad_b_out,
        start_sensitivity,
    )


def solution(mesh):
    in_specs = (
        P("blk", "gy", "rep"),
        P(None, "blk", "gy", "rep"),
        P(None, "blk", "gy", "rep"),
        P(),
        P("rep", None),
        P("rep"),
        P("rep", None),
        P("rep"),
        P(None, "rep"),
        P(),
    )
    out_specs = (
        P(None, "blk", "gy", "rep"),
        P(),
        P("rep", None),
        P("rep"),
        P("rep", None),
        P("rep"),
        P(None, "rep"),
        P(),
        P(None, "blk", "gy", "rep"),
    )
    return jax.shard_map(
        per_device, mesh=mesh, in_specs=in_specs, out_specs=out_specs, check_vma=False
    )
```

```python
import functools

import jax
import jax.numpy as jnp
from jax import lax
from jax.experimental import pallas as pl
from jax.experimental.pallas import tpu as pltpu
from jax.sharding import PartitionSpec as P

STEPS = 4


RATE_MAX = 0.15

AXES = (("rep", 3), ("gy", 2), ("blk", 1))
MESH_AXES = ("blk", "gy", "rep")
RATE_ORDER = (0, 3, 1, 4, 2, 5)


def _neighbour_kernel(sizes, plan, n_fields, with_step, *refs):
    fields = refs[:n_fields]
    n_items = sum(len(items) for items in plan)
    outs = refs[n_fields:n_fields + 2 * n_items]
    first_scratch = n_fields + 2 * n_items + (1 if with_step else 0)
    landing = refs[first_scratch:first_scratch + 2 * n_items]
    staged = refs[first_scratch + 2 * n_items:first_scratch + 4 * n_items]
    send_sems, recv_sems = refs[-2], refs[-1]
    here = [lax.axis_index(name) for name in MESH_AXES]

    def neighbour(axis, step):
        coords = list(here)
        position = MESH_AXES.index(axis)
        coords[position] = lax.rem(here[position] + step + sizes[position], sizes[position])
        return tuple(coords)

    targets = [(neighbour(axis, 1), neighbour(axis, -1)) for axis, dim in AXES]
    barrier = pltpu.get_barrier_semaphore()
    for plus, minus in targets:
        for peer in (plus, minus):
            pl.semaphore_signal(barrier, 1, device_id=peer, device_id_type=pl.DeviceIdType.MESH)
    pl.semaphore_wait(barrier, 6)
    copies = []
    item = 0
    for direction, (axis, dim) in enumerate(AXES):
        plus, minus = targets[direction]
        for field, first, count in plan[direction]:
            group = fields[field].at[first:first + count]
            depth = fields[field].shape[1]
            if dim == 1:
                to_plus, to_minus = group.at[:, depth - 1], group.at[:, 0]
            elif dim == 2:
                rows = group.shape[2]
                staged[2 * item][...] = group[:, :, rows - 1, :]
                staged[2 * item + 1][...] = group[:, :, 0, :]
                to_plus, to_minus = staged[2 * item], staged[2 * item + 1]
            else:
                to_plus, to_minus = group, group
            for slot, source, peer in ((0, to_plus, plus), (1, to_minus, minus)):
                index = 2 * item + slot
                copy = pltpu.make_async_remote_copy(
                    src_ref=source,
                    dst_ref=landing[index],
                    send_sem=send_sems.at[index],
                    recv_sem=recv_sems.at[index],
                    device_id=peer,
                    device_id_type=pl.DeviceIdType.MESH,
                )
                copy.start()
                copies.append(copy)
            item += 1
    for copy in copies:
        copy.wait()
    item = 0
    for direction, (axis, dim) in enumerate(AXES):
        for field, first, count in plan[direction]:
            group = fields[field].at[first:first + count]
            from_below, from_above = landing[2 * item], landing[2 * item + 1]
            out_plus, out_minus = outs[2 * item], outs[2 * item + 1]
            if dim == 1:
                depth = group.shape[1]
                out_plus[:, 0:depth - 1] = group[:, 1:depth]
                out_plus[:, depth - 1] = from_above[...]
                out_minus[:, 1:depth] = group[:, 0:depth - 1]
                out_minus[:, 0] = from_below[...]
            else:
                values = group[...]
                size = values.shape[dim]
                index = lax.broadcasted_iota(jnp.int32, values.shape, dim)
                above, below = from_above[...], from_below[...]
                if dim == 2:
                    above = jnp.broadcast_to(above[:, :, None, :], values.shape)
                    below = jnp.broadcast_to(below[:, :, None, :], values.shape)
                out_plus[...] = pltpu.roll(jnp.where(index == 0, above, values), size - 1, dim)
                out_minus[...] = pltpu.roll(
                    jnp.where(index == size - 1, below, values), 1, dim
                )
            item += 1
    if with_step:
        new_state = refs[n_fields + 2 * n_items]
        field = fields[0][...]
        summed = field
        for direction in range(3):
            rate_here = fields[1][2 * direction:2 * direction + 2]
            for side in range(2):
                field_next = outs[2 * (2 * direction) + side][...]
                rate_next = outs[2 * (2 * direction + 1) + side][...]
                summed = summed + 0.5 * (rate_here + rate_next) * (field_next - field)
        new_state[...] = summed


def exchange_neighbours(fields, plan, collective_id, with_step=False):
    sizes = tuple(lax.axis_size(name) for name in MESH_AXES)
    group_shapes = []
    landing_shapes = []
    for direction, (axis, dim) in enumerate(AXES):
        for field, first, count in plan[direction]:
            shape = (count,) + fields[field].shape[1:]
            group_shapes.append(shape)
            if dim == 1:
                layer = shape[:1] + shape[2:]
            elif dim == 2:
                layer = shape[:2] + shape[3:]
            else:
                layer = shape
            landing_shapes += [layer, layer]
    n_items = len(group_shapes)
    vmem = pl.BlockSpec(memory_space=pltpu.VMEM)
    out_shapes = []
    for shape in group_shapes:
        out_shapes += [jax.ShapeDtypeStruct(shape, jnp.float32)] * 2
    if with_step:
        out_shapes.append(jax.ShapeDtypeStruct(fields[0].shape, jnp.float32))
    shifted = pl.pallas_call(
        functools.partial(_neighbour_kernel, sizes, plan, len(fields), with_step),
        out_shape=tuple(out_shapes),
        in_specs=[vmem] * len(fields),
        out_specs=(vmem,) * len(out_shapes),
        scratch_shapes=[pltpu.VMEM(shape, jnp.float32) for shape in landing_shapes]
        + [pltpu.VMEM(shape, jnp.float32) for shape in landing_shapes]
        + [pltpu.SemaphoreType.DMA((2 * n_items,)), pltpu.SemaphoreType.DMA((2 * n_items,))],
        compiler_params=pltpu.CompilerParams(collective_id=collective_id, has_side_effects=True),
    )(*fields)
    result = []
    item = 0
    for direction in range(3):
        pairs = []
        for _ in plan[direction]:
            pairs.append((shifted[2 * item], shifted[2 * item + 1]))
            item += 1
        result.append(pairs)
    if with_step:
        return result, shifted[-1]
    return result


def _allreduce_kernel(stages, partial_ref, mine_ref, last_ref, acc, landing, send_sems, recv_sems):
    here = [lax.axis_index(name) for name in MESH_AXES]

    def member(name, stride, size, digit):
        position = MESH_AXES.index(name)
        own = lax.rem(here[position] // stride, size)
        coords = list(here)
        coords[position] = here[position] + (digit - own) * stride
        return tuple(coords), own

    barrier = pltpu.get_barrier_semaphore()
    partner_count = 0
    for name, stride, size in stages:
        for step in range(1, size):
            position = MESH_AXES.index(name)
            own = lax.rem(here[position] // stride, size)
            digit = lax.rem(own + step, size)
            peer, _ = member(name, stride, size, digit)
            pl.semaphore_signal(barrier, 1, device_id=peer, device_id_type=pl.DeviceIdType.MESH)
            partner_count += 1
    pl.semaphore_wait(barrier, partner_count)
    acc[...] = partial_ref[...]
    for stage, (name, stride, size) in enumerate(stages):
        position = MESH_AXES.index(name)
        own = lax.rem(here[position] // stride, size)
        landing[stage, own] = acc[...]
        sends = []
        receives = []
        for step in range(1, size):
            digit = lax.rem(own + step, size)
            peer, _ = member(name, stride, size, digit)
            copy = pltpu.make_async_remote_copy(
                src_ref=acc,
                dst_ref=landing.at[stage, own],
                send_sem=send_sems.at[stage, step],
                recv_sem=recv_sems.at[stage, own],
                device_id=peer,
                device_id_type=pl.DeviceIdType.MESH,
            )
            copy.start()
            sends.append(copy)
            receives.append(
                pltpu.make_async_remote_copy(
                    src_ref=acc,
                    dst_ref=landing.at[stage, digit],
                    send_sem=send_sems.at[stage, step],
                    recv_sem=recv_sems.at[stage, digit],
                    device_id=peer,
                    device_id_type=pl.DeviceIdType.MESH,
                )
            )
        for copy in sends:
            copy.wait_send()
        for copy in receives:
            copy.wait_recv()
        if size == 4:
            acc[...] = (landing[stage, 0] + landing[stage, 1]) + (
                landing[stage, 2] + landing[stage, 3]
            )
        else:
            acc[...] = landing[stage, 0] + landing[stage, 1]
    share = mine_ref.shape[0]
    start = pl.multiple_of(here[MESH_AXES.index("rep")] * share, 8)
    mine_ref[...] = acc[pl.ds(start, share), :]
    last_ref[...] = acc[acc.shape[0] - last_ref.shape[0]:, :]


def _stages():
    stages = []
    for name in ("rep", "gy", "blk"):
        size = lax.axis_size(name)
        stride = 1
        while stride < size:
            group = 4 if size // stride >= 4 else 2
            stages.append((name, stride, group))
            stride *= group
    return stages


def _power_of_two(count):
    return count & (count - 1) == 0


def sum_everywhere(block, share):
    if not all(_power_of_two(lax.axis_size(name)) for name in MESH_AXES):
        summed = lax.psum(block, MESH_AXES)
        mine = lax.dynamic_slice_in_dim(summed, lax.axis_index("rep") * share, share, 0)
        return mine, summed[-8:]
    stages = _stages()
    vmem = pl.BlockSpec(memory_space=pltpu.VMEM)
    summed = pl.pallas_call(
        functools.partial(_allreduce_kernel, stages),
        out_shape=(
            jax.ShapeDtypeStruct((share, block.shape[1]), block.dtype),
            jax.ShapeDtypeStruct((8, block.shape[1]), block.dtype),
        ),
        in_specs=[vmem],
        out_specs=(vmem, vmem),
        scratch_shapes=[
            pltpu.VMEM(block.shape, block.dtype),
            pltpu.VMEM((len(stages), 4) + block.shape, block.dtype),
            pltpu.SemaphoreType.DMA((len(stages), 4)),
            pltpu.SemaphoreType.DMA((len(stages), 4)),
        ],
        compiler_params=pltpu.CompilerParams(collective_id=2, has_side_effects=True),
    )(block)
    return summed


def diffuse(field, field_nb, rates, rate_nb):
    summed = field
    for direction in range(3):
        rate_here = rates[2 * direction:2 * direction + 2]
        for side, offset in enumerate((1, -1)):
            summed = summed + 0.5 * (rate_here + rate_nb[direction][side]) * (
                field_nb[direction][side] - field
            )
    return summed


def rate_cotangent(state, state_nb, adjoint, adjoint_nb):
    pieces_list = []
    for direction in range(3):
        summed = jnp.zeros_like(state)
        for side, offset in enumerate((1, -1)):
            summed = summed + (state_nb[direction][side] - state) * (
                adjoint_nb[direction][side] - adjoint
            )
        pieces_list.append(-0.5 * summed)
    return jnp.concatenate(pieces_list, axis=0)


def embed_lookup(emb_table, grain_flat):
    table_rows = emb_table.shape[0]
    one_hot = (grain_flat[None, :] == lax.broadcasted_iota(jnp.int32, (table_rows, 1), 0)).astype(
        jnp.bfloat16
    )
    looked = jnp.dot(emb_table.T, one_hot, preferred_element_type=jnp.float32)
    return looked.astype(jnp.bfloat16)


def forward_layers(params, features):
    w_in, b_in, w_mid, b_mid, w_out, b_out = params
    act_one = jnp.tanh(
        jnp.dot(w_in, features, preferred_element_type=jnp.float32)
        + b_in.astype(jnp.float32)[:, None]
    )
    hid_one = act_one.astype(jnp.bfloat16)
    act_two = jnp.tanh(
        jnp.dot(w_mid, hid_one, preferred_element_type=jnp.float32)
        + b_mid.astype(jnp.float32)[:, None]
    )
    hid_two = act_two.astype(jnp.bfloat16)
    logits = (
        jnp.dot(w_out, hid_two, preferred_element_type=jnp.float32)
        + b_out.astype(jnp.float32)[:, None]
    )
    return (RATE_MAX * jax.nn.sigmoid(logits), act_one, hid_one, act_two, hid_two)


def backward_layers(params, rate_grad, forward_values):
    w_in, b_in, w_mid, b_mid, w_out, b_out = params
    rate_values, act_one, hid_one, act_two, hid_two = forward_values
    out_grad = (rate_grad * rate_values * (1.0 - rate_values / RATE_MAX)).astype(jnp.bfloat16)
    two_grad = (
        jnp.dot(w_out.T, out_grad, preferred_element_type=jnp.float32) * (1.0 - act_two * act_two)
    ).astype(jnp.bfloat16)
    one_grad = (
        jnp.dot(w_mid.T, two_grad, preferred_element_type=jnp.float32) * (1.0 - act_one * act_one)
    ).astype(jnp.bfloat16)
    state_grad = jnp.dot(w_in[:, -2:].T, one_grad, preferred_element_type=jnp.float32)
    return (out_grad, two_grad, one_grad), state_grad


def gradient_sums(grads, inputs):
    terms = []
    for grad_list, input_list in zip(grads, inputs):
        grad = jnp.concatenate(grad_list, axis=1)
        ones = jnp.ones((1, grad.shape[1]), jnp.bfloat16)
        layer_input = jnp.concatenate(input_list, axis=1)
        layer_input = jnp.concatenate([layer_input, ones], axis=0)
        terms.append(jnp.dot(grad, layer_input.T, preferred_element_type=jnp.float32))
    return terms


def gather_params(w_in, b_in, w_mid, b_mid, w_out, b_out):
    n_in = w_in.shape[1]
    n_mid = w_mid.shape[1]
    packed = jnp.concatenate(
        [w_in, b_in[:, None], w_mid, b_mid[:, None], w_out.T], axis=1
    ).astype(jnp.bfloat16)
    full = lax.all_gather(packed, "rep", axis=0, tiled=True)
    col = 0
    w_in_b = full[:, col:col + n_in]
    col += n_in
    b_in_b = full[:, col]
    col += 1
    w_mid_b = full[:, col:col + n_mid]
    col += n_mid
    b_mid_b = full[:, col]
    col += 1
    w_out_b = full[:, col:].T
    order = jnp.array(RATE_ORDER)
    return (w_in_b, b_in_b, w_mid_b, b_mid_b, w_out_b[order], b_out.astype(jnp.bfloat16)[order])


def per_device(
    grain_id, init_masks, target_masks, emb_table, w_in, b_in, w_mid, b_mid, w_out, b_out
):
    params = gather_params(w_in, b_in, w_mid, b_mid, w_out, b_out)
    depth_cells, row_cells, col_cells = grain_id.shape
    cell_count = depth_cells * row_cells * col_cells
    block_shape = (depth_cells, row_cells, col_cells)
    embedding = embed_lookup(emb_table, grain_id.reshape(cell_count))
    state_now = init_masks.astype(jnp.float32)
    history = []
    forward_plan = [[(0, 0, 2), (1, 2 * d, 2)] for d in range(3)]
    for step_index in range(STEPS):
        features = jnp.concatenate(
            [embedding, state_now.reshape(2, cell_count).astype(jnp.bfloat16)], axis=0
        )
        rate_values = forward_layers(params, features)[0].reshape((6,) + block_shape)
        neighbours, state_next = exchange_neighbours(
            [state_now, rate_values], forward_plan, 0, with_step=True
        )
        state_nb = [pairs[0] for pairs in neighbours]
        rate_nb = [pairs[1] for pairs in neighbours]
        history.append((state_now, state_nb, rate_values, rate_nb))
        state_now = state_next
    misfit = state_now - target_masks.astype(jnp.float32)
    total_cells = float(
        cell_count * lax.axis_size("blk") * lax.axis_size("gy") * lax.axis_size("rep")
    )
    loss_part = jnp.sum(misfit * misfit) / (4.0 * total_cells)
    adjoint = misfit / (2.0 * total_cells)
    grads = ([], [], [])
    inputs = ([], [], [])
    for step_index in reversed(range(STEPS)):
        state_t, state_nb, rate_values, rate_nb = history[step_index]
        adjoint_nb = [
            pairs[0] for pairs in exchange_neighbours([adjoint], [[(0, 0, 2)]] * 3, 1)
        ]
        rate_grad = rate_cotangent(state_t, state_nb, adjoint, adjoint_nb).reshape(
            6, cell_count
        )
        features = jnp.concatenate(
            [embedding, state_t.reshape(2, cell_count).astype(jnp.bfloat16)], axis=0
        )
        forward_values = forward_layers(params, features)
        step_grads, state_grad = backward_layers(params, rate_grad, forward_values)
        for index, (grad, layer_input) in enumerate(
            zip(reversed(step_grads), (features, forward_values[2], forward_values[4]))
        ):
            grads[index].append(grad)
            inputs[index].append(layer_input)
        adjoint = diffuse(adjoint, adjoint_nb, rate_values, rate_nb) + state_grad.reshape(
            (2,) + block_shape
        )
    grad_sums = gradient_sums(grads, inputs)
    start_sensitivity = adjoint * (2.0 * total_cells)
    in_both, mid_both, out_both = grad_sums
    back = jnp.array([RATE_ORDER.index(channel) for channel in range(6)])
    out_both = out_both[back]
    units = in_both.shape[0]
    per_unit = jnp.concatenate([in_both, mid_both, out_both[:, :-1].T], axis=1)
    width = per_unit.shape[1]
    last = jnp.concatenate([out_both[:, -1], loss_part[None]])
    rows = -(-(units + 1) // 8) * 8
    packed = jnp.zeros((rows, 128), jnp.float32)
    packed = packed.at[:units, :width].set(per_unit)
    packed = packed.at[units, :last.shape[0]].set(last)
    share_width = w_in.shape[0]
    mine, last_rows = sum_everywhere(packed, share_width)
    n_in = w_in.shape[1]
    n_mid = w_mid.shape[1]
    grad_w_in = mine[:, :n_in]
    grad_b_in = mine[:, n_in]
    grad_w_mid = mine[:, n_in + 1:n_in + 1 + n_mid]
    grad_b_mid = mine[:, n_in + 1 + n_mid]
    grad_w_out = mine[:, n_in + 2 + n_mid:width].T
    grad_b_out = last_rows[units - (rows - 8), :6]
    loss_total = last_rows[units - (rows - 8), 6]
    return (
        state_now,
        loss_total,
        grad_w_in,
        grad_b_in,
        grad_w_mid,
        grad_b_mid,
        grad_w_out,
        grad_b_out,
        start_sensitivity,
    )


def solution(mesh):
    in_specs = (
        P("blk", "gy", "rep"),
        P(None, "blk", "gy", "rep"),
        P(None, "blk", "gy", "rep"),
        P(),
        P("rep", None),
        P("rep"),
        P("rep", None),
        P("rep"),
        P(None, "rep"),
        P(),
    )
    out_specs = (
        P(None, "blk", "gy", "rep"),
        P(),
        P("rep", None),
        P("rep"),
        P("rep", None),
        P("rep"),
        P(None, "rep"),
        P(),
        P(None, "blk", "gy", "rep"),
    )
    return jax.shard_map(
        per_device, mesh=mesh, in_specs=in_specs, out_specs=out_specs, check_vma=False
    )
```

```python
import functools

import jax
import jax.numpy as jnp
from jax import lax
from jax.experimental import pallas as pl
from jax.experimental.pallas import tpu as pltpu
from jax.sharding import PartitionSpec as P

STEPS = 4


RATE_MAX = 0.15

AXES = (("rep", 3), ("gy", 2), ("blk", 1))
MESH_AXES = ("blk", "gy", "rep")
RATE_ORDER = (0, 3, 1, 4, 2, 5)


def _neighbour_kernel(sizes, plan, n_fields, *refs):
    fields = refs[:n_fields]
    n_items = sum(len(items) for items in plan)
    outs = refs[n_fields:n_fields + 2 * n_items]
    landing = refs[n_fields + 2 * n_items:n_fields + 4 * n_items]
    staged = refs[n_fields + 4 * n_items:n_fields + 6 * n_items]
    send_sems, recv_sems = refs[-2], refs[-1]
    here = [lax.axis_index(name) for name in MESH_AXES]

    def neighbour(axis, step):
        coords = list(here)
        position = MESH_AXES.index(axis)
        coords[position] = lax.rem(here[position] + step + sizes[position], sizes[position])
        return tuple(coords)

    targets = [(neighbour(axis, 1), neighbour(axis, -1)) for axis, dim in AXES]
    barrier = pltpu.get_barrier_semaphore()
    for plus, minus in targets:
        for peer in (plus, minus):
            pl.semaphore_signal(barrier, 1, device_id=peer, device_id_type=pl.DeviceIdType.MESH)
    pl.semaphore_wait(barrier, 6)
    copies = []
    item = 0
    for direction, (axis, dim) in enumerate(AXES):
        plus, minus = targets[direction]
        for field, first, count in plan[direction]:
            group = fields[field].at[first:first + count]
            depth = fields[field].shape[1]
            if dim == 1:
                to_plus, to_minus = group.at[:, depth - 1], group.at[:, 0]
            elif dim == 2:
                rows = group.shape[2]
                staged[2 * item][...] = group[:, :, rows - 1, :]
                staged[2 * item + 1][...] = group[:, :, 0, :]
                to_plus, to_minus = staged[2 * item], staged[2 * item + 1]
            else:
                to_plus, to_minus = group, group
            for slot, source, peer in ((0, to_plus, plus), (1, to_minus, minus)):
                index = 2 * item + slot
                copy = pltpu.make_async_remote_copy(
                    src_ref=source,
                    dst_ref=landing[index],
                    send_sem=send_sems.at[index],
                    recv_sem=recv_sems.at[index],
                    device_id=peer,
                    device_id_type=pl.DeviceIdType.MESH,
                )
                copy.start()
                copies.append(copy)
            item += 1
    for copy in copies:
        copy.wait()
    item = 0
    for direction, (axis, dim) in enumerate(AXES):
        for field, first, count in plan[direction]:
            group = fields[field].at[first:first + count]
            from_below, from_above = landing[2 * item], landing[2 * item + 1]
            out_plus, out_minus = outs[2 * item], outs[2 * item + 1]
            if dim == 1:
                depth = group.shape[1]
                out_plus[:, 0:depth - 1] = group[:, 1:depth]
                out_plus[:, depth - 1] = from_above[...]
                out_minus[:, 1:depth] = group[:, 0:depth - 1]
                out_minus[:, 0] = from_below[...]
            else:
                values = group[...]
                size = values.shape[dim]
                index = lax.broadcasted_iota(jnp.int32, values.shape, dim)
                above, below = from_above[...], from_below[...]
                if dim == 2:
                    above = jnp.broadcast_to(above[:, :, None, :], values.shape)
                    below = jnp.broadcast_to(below[:, :, None, :], values.shape)
                out_plus[...] = pltpu.roll(jnp.where(index == 0, above, values), size - 1, dim)
                out_minus[...] = pltpu.roll(
                    jnp.where(index == size - 1, below, values), 1, dim
                )
            item += 1


def exchange_neighbours(fields, plan, collective_id):
    sizes = tuple(lax.axis_size(name) for name in MESH_AXES)
    group_shapes = []
    landing_shapes = []
    for direction, (axis, dim) in enumerate(AXES):
        for field, first, count in plan[direction]:
            shape = (count,) + fields[field].shape[1:]
            group_shapes.append(shape)
            if dim == 1:
                layer = shape[:1] + shape[2:]
            elif dim == 2:
                layer = shape[:2] + shape[3:]
            else:
                layer = shape
            landing_shapes += [layer, layer]
    n_items = len(group_shapes)
    vmem = pl.BlockSpec(memory_space=pltpu.VMEM)
    out_shapes = []
    for shape in group_shapes:
        out_shapes += [jax.ShapeDtypeStruct(shape, jnp.float32)] * 2
    shifted = pl.pallas_call(
        functools.partial(_neighbour_kernel, sizes, plan, len(fields)),
        out_shape=tuple(out_shapes),
        in_specs=[vmem] * len(fields),
        out_specs=(vmem,) * len(out_shapes),
        scratch_shapes=[pltpu.VMEM(shape, jnp.float32) for shape in landing_shapes]
        + [pltpu.VMEM(shape, jnp.float32) for shape in landing_shapes]
        + [pltpu.SemaphoreType.DMA((2 * n_items,)), pltpu.SemaphoreType.DMA((2 * n_items,))],
        compiler_params=pltpu.CompilerParams(collective_id=collective_id, has_side_effects=True),
    )(*fields)
    result = []
    item = 0
    for direction in range(3):
        pairs = []
        for _ in plan[direction]:
            pairs.append((shifted[2 * item], shifted[2 * item + 1]))
            item += 1
        result.append(pairs)
    return result


def _allreduce_kernel(stages, partial_ref, mine_ref, last_ref, acc, landing, send_sems, recv_sems):
    here = [lax.axis_index(name) for name in MESH_AXES]

    def member(name, stride, size, digit):
        position = MESH_AXES.index(name)
        own = lax.rem(here[position] // stride, size)
        coords = list(here)
        coords[position] = here[position] + (digit - own) * stride
        return tuple(coords), own

    barrier = pltpu.get_barrier_semaphore()
    partner_count = 0
    for name, stride, size in stages:
        for step in range(1, size):
            position = MESH_AXES.index(name)
            own = lax.rem(here[position] // stride, size)
            digit = lax.rem(own + step, size)
            peer, _ = member(name, stride, size, digit)
            pl.semaphore_signal(barrier, 1, device_id=peer, device_id_type=pl.DeviceIdType.MESH)
            partner_count += 1
    pl.semaphore_wait(barrier, partner_count)
    acc[...] = partial_ref[...]
    for stage, (name, stride, size) in enumerate(stages):
        position = MESH_AXES.index(name)
        own = lax.rem(here[position] // stride, size)
        landing[stage, own] = acc[...]
        sends = []
        receives = []
        for step in range(1, size):
            digit = lax.rem(own + step, size)
            peer, _ = member(name, stride, size, digit)
            copy = pltpu.make_async_remote_copy(
                src_ref=acc,
                dst_ref=landing.at[stage, own],
                send_sem=send_sems.at[stage, step],
                recv_sem=recv_sems.at[stage, own],
                device_id=peer,
                device_id_type=pl.DeviceIdType.MESH,
            )
            copy.start()
            sends.append(copy)
            receives.append(
                pltpu.make_async_remote_copy(
                    src_ref=acc,
                    dst_ref=landing.at[stage, digit],
                    send_sem=send_sems.at[stage, step],
                    recv_sem=recv_sems.at[stage, digit],
                    device_id=peer,
                    device_id_type=pl.DeviceIdType.MESH,
                )
            )
        for copy in sends:
            copy.wait_send()
        for copy in receives:
            copy.wait_recv()
        if size == 4:
            acc[...] = (landing[stage, 0] + landing[stage, 1]) + (
                landing[stage, 2] + landing[stage, 3]
            )
        else:
            acc[...] = landing[stage, 0] + landing[stage, 1]
    share = mine_ref.shape[0]
    start = pl.multiple_of(here[MESH_AXES.index("rep")] * share, 8)
    mine_ref[...] = acc[pl.ds(start, share), :]
    last_ref[...] = acc[0:last_ref.shape[0], :]


def _stages():
    stages = []
    for name in ("rep", "gy", "blk"):
        size = lax.axis_size(name)
        stride = 1
        while stride < size:
            group = 4 if size // stride >= 4 else 2
            stages.append((name, stride, group))
            stride *= group
    return stages


def _power_of_two(count):
    return count & (count - 1) == 0


def sum_everywhere(block, share):
    if not all(_power_of_two(lax.axis_size(name)) for name in MESH_AXES):
        summed = lax.psum(block, MESH_AXES)
        mine = lax.dynamic_slice_in_dim(summed, lax.axis_index("rep") * share, share, 0)
        return mine, summed[:8]
    stages = _stages()
    vmem = pl.BlockSpec(memory_space=pltpu.VMEM)
    summed = pl.pallas_call(
        functools.partial(_allreduce_kernel, stages),
        out_shape=(
            jax.ShapeDtypeStruct((share, block.shape[1]), block.dtype),
            jax.ShapeDtypeStruct((8, block.shape[1]), block.dtype),
        ),
        in_specs=[vmem],
        out_specs=(vmem, vmem),
        scratch_shapes=[
            pltpu.VMEM(block.shape, block.dtype),
            pltpu.VMEM((len(stages), 4) + block.shape, block.dtype),
            pltpu.SemaphoreType.DMA((len(stages), 4)),
            pltpu.SemaphoreType.DMA((len(stages), 4)),
        ],
        compiler_params=pltpu.CompilerParams(collective_id=2, has_side_effects=True),
    )(block)
    return summed


def diffuse(field, field_nb, rates, rate_nb):
    summed = field
    for direction in range(3):
        rate_here = rates[2 * direction:2 * direction + 2]
        for side, offset in enumerate((1, -1)):
            summed = summed + 0.5 * (rate_here + rate_nb[direction][side]) * (
                field_nb[direction][side] - field
            )
    return summed


def rate_cotangent(state, state_nb, adjoint, adjoint_nb):
    pieces_list = []
    for direction in range(3):
        summed = jnp.zeros_like(state)
        for side, offset in enumerate((1, -1)):
            summed = summed + (state_nb[direction][side] - state) * (
                adjoint_nb[direction][side] - adjoint
            )
        pieces_list.append(-0.5 * summed)
    return jnp.concatenate(pieces_list, axis=0)


def embed_lookup(emb_table, grain_flat):
    table_rows = emb_table.shape[0]
    one_hot = (grain_flat[None, :] == lax.broadcasted_iota(jnp.int32, (table_rows, 1), 0)).astype(
        jnp.bfloat16
    )
    looked = jnp.dot(emb_table.T, one_hot, preferred_element_type=jnp.float32)
    return looked.astype(jnp.bfloat16)


def forward_layers(params, features):
    w_in, b_in, w_mid, b_mid, w_out, b_out = params
    act_one = jnp.tanh(
        jnp.dot(w_in, features, preferred_element_type=jnp.float32)
        + b_in.astype(jnp.float32)[:, None]
    )
    hid_one = act_one.astype(jnp.bfloat16)
    act_two = jnp.tanh(
        jnp.dot(w_mid, hid_one, preferred_element_type=jnp.float32)
        + b_mid.astype(jnp.float32)[:, None]
    )
    hid_two = act_two.astype(jnp.bfloat16)
    logits = (
        jnp.dot(w_out, hid_two, preferred_element_type=jnp.float32)
        + b_out.astype(jnp.float32)[:, None]
    )
    return (RATE_MAX * jax.nn.sigmoid(logits), act_one, hid_one, act_two, hid_two)


def backward_layers(params, rate_grad, forward_values):
    w_in, b_in, w_mid, b_mid, w_out, b_out = params
    rate_values, act_one, hid_one, act_two, hid_two = forward_values
    out_grad = (rate_grad * rate_values * (1.0 - rate_values / RATE_MAX)).astype(jnp.bfloat16)
    two_grad = (
        jnp.dot(w_out.T, out_grad, preferred_element_type=jnp.float32) * (1.0 - act_two * act_two)
    ).astype(jnp.bfloat16)
    one_grad = (
        jnp.dot(w_mid.T, two_grad, preferred_element_type=jnp.float32) * (1.0 - act_one * act_one)
    ).astype(jnp.bfloat16)
    state_grad = jnp.dot(w_in[:, -2:].T, one_grad, preferred_element_type=jnp.float32)
    return (out_grad, two_grad, one_grad), state_grad


def gradient_sums(grads, inputs):
    terms = []
    for grad_list, input_list in zip(grads, inputs):
        grad = jnp.concatenate(grad_list, axis=1)
        ones = jnp.ones((1, grad.shape[1]), jnp.bfloat16)
        layer_input = jnp.concatenate(input_list, axis=1)
        layer_input = jnp.concatenate([layer_input, ones], axis=0)
        terms.append(jnp.dot(grad, layer_input.T, preferred_element_type=jnp.float32))
    return terms


def gather_params(w_in, b_in, w_mid, b_mid, w_out, b_out):
    n_in = w_in.shape[1]
    n_mid = w_mid.shape[1]
    packed = jnp.concatenate(
        [w_in, b_in[:, None], w_mid, b_mid[:, None], w_out.T], axis=1
    ).astype(jnp.bfloat16)
    full = lax.all_gather(packed, "rep", axis=0, tiled=True)
    col = 0
    w_in_b = full[:, col:col + n_in]
    col += n_in
    b_in_b = full[:, col]
    col += 1
    w_mid_b = full[:, col:col + n_mid]
    col += n_mid
    b_mid_b = full[:, col]
    col += 1
    w_out_b = full[:, col:].T
    order = jnp.array(RATE_ORDER)
    return (w_in_b, b_in_b, w_mid_b, b_mid_b, w_out_b[order], b_out.astype(jnp.bfloat16)[order])


def per_device(
    grain_id, init_masks, target_masks, emb_table, w_in, b_in, w_mid, b_mid, w_out, b_out
):
    params = gather_params(w_in, b_in, w_mid, b_mid, w_out, b_out)
    depth_cells, row_cells, col_cells = grain_id.shape
    cell_count = depth_cells * row_cells * col_cells
    block_shape = (depth_cells, row_cells, col_cells)
    embedding = embed_lookup(emb_table, grain_id.reshape(cell_count))
    state_now = init_masks.astype(jnp.float32)
    history = []
    forward_plan = [[(0, 0, 2), (1, 2 * d, 2)] for d in range(3)]
    for step_index in range(STEPS):
        features = jnp.concatenate(
            [embedding, state_now.reshape(2, cell_count).astype(jnp.bfloat16)], axis=0
        )
        rate_values = forward_layers(params, features)[0].reshape((6,) + block_shape)
        neighbours = exchange_neighbours([state_now, rate_values], forward_plan, 0)
        state_nb = [pairs[0] for pairs in neighbours]
        rate_nb = [pairs[1] for pairs in neighbours]
        history.append((state_now, state_nb, rate_values, rate_nb))
        state_now = diffuse(state_now, state_nb, rate_values, rate_nb)
    misfit = state_now - target_masks.astype(jnp.float32)
    total_cells = float(
        cell_count * lax.axis_size("blk") * lax.axis_size("gy") * lax.axis_size("rep")
    )
    loss_part = jnp.sum(misfit * misfit) / (4.0 * total_cells)
    adjoint = misfit / (2.0 * total_cells)
    grads = ([], [], [])
    inputs = ([], [], [])
    for step_index in reversed(range(STEPS)):
        state_t, state_nb, rate_values, rate_nb = history[step_index]
        adjoint_nb = [
            pairs[0] for pairs in exchange_neighbours([adjoint], [[(0, 0, 2)]] * 3, 1)
        ]
        rate_grad = rate_cotangent(state_t, state_nb, adjoint, adjoint_nb).reshape(
            6, cell_count
        )
        features = jnp.concatenate(
            [embedding, state_t.reshape(2, cell_count).astype(jnp.bfloat16)], axis=0
        )
        forward_values = forward_layers(params, features)
        step_grads, state_grad = backward_layers(params, rate_grad, forward_values)
        for index, (grad, layer_input) in enumerate(
            zip(reversed(step_grads), (features, forward_values[2], forward_values[4]))
        ):
            grads[index].append(grad)
            inputs[index].append(layer_input)
        adjoint = diffuse(adjoint, adjoint_nb, rate_values, rate_nb) + state_grad.reshape(
            (2,) + block_shape
        )
    grad_sums = gradient_sums(grads, inputs)
    start_sensitivity = adjoint * (2.0 * total_cells)
    in_both, mid_both, out_both = grad_sums
    back = jnp.array([RATE_ORDER.index(channel) for channel in range(6)])
    out_both = out_both[back]
    units = in_both.shape[0]
    per_unit = jnp.concatenate([in_both, mid_both, out_both[:, :-1].T], axis=1)
    width = per_unit.shape[1]
    last = jnp.concatenate([out_both[:, -1], loss_part[None]])
    assert width + last.shape[0] <= 128 and units % 8 == 0
    packed = jnp.zeros((units, 128), jnp.float32)
    packed = packed.at[:, :width].set(per_unit)
    packed = packed.at[0, width:width + last.shape[0]].set(last)
    share_width = w_in.shape[0]
    mine, last_rows = sum_everywhere(packed, share_width)
    n_in = w_in.shape[1]
    n_mid = w_mid.shape[1]
    grad_w_in = mine[:, :n_in]
    grad_b_in = mine[:, n_in]
    grad_w_mid = mine[:, n_in + 1:n_in + 1 + n_mid]
    grad_b_mid = mine[:, n_in + 1 + n_mid]
    grad_w_out = mine[:, n_in + 2 + n_mid:width].T
    grad_b_out = last_rows[0, width:width + 6]
    loss_total = last_rows[0, width + 6]
    return (
        state_now,
        loss_total,
        grad_w_in,
        grad_b_in,
        grad_w_mid,
        grad_b_mid,
        grad_w_out,
        grad_b_out,
        start_sensitivity,
    )


def solution(mesh):
    in_specs = (
        P("blk", "gy", "rep"),
        P(None, "blk", "gy", "rep"),
        P(None, "blk", "gy", "rep"),
        P(),
        P("rep", None),
        P("rep"),
        P("rep", None),
        P("rep"),
        P(None, "rep"),
        P(),
    )
    out_specs = (
        P(None, "blk", "gy", "rep"),
        P(),
        P("rep", None),
        P("rep"),
        P("rep", None),
        P("rep"),
        P(None, "rep"),
        P(),
        P(None, "blk", "gy", "rep"),
    )
    return jax.shard_map(
        per_device, mesh=mesh, in_specs=in_specs, out_specs=out_specs, check_vma=False
    )
```
